128 devices in a mesh: row: 8 (over y_lo, z), col: 16 (over y_hi, x, core).
Axes of the slice: x: 4, y: 4 (y_hi: 2, y_lo: 2; y = y_hi * 2 + y_lo), z: 4, core: 2. Of those that a mesh axis runs over, the one named last changes fastest.
Arguments:
- tokens: bfloat16 [2, 192, 256, 512], P(None, 'row', 'col'), may hold values from -6 to 6
- w_qkv: bfloat16 [512, 1536], replicated, may hold values from -0.25 to 0.25
- w_out: bfloat16 [512, 512], replicated, may hold values from -0.25 to 0.25
- q_saved: bfloat16 [2, 192, 256, 512], P(None, 'row', 'col'), may hold values from -4 to 4
- k_saved: bfloat16 [2, 192, 256, 512], P(None, 'row', 'col'), may hold values from -4 to 4
- v_saved: bfloat16 [2, 192, 256, 512], P(None, 'row', 'col'), may hold values from -4 to 4
- scale_exp: int32 [2, 24, 32, 24], P(None, 'row', 'col'), may hold values from -1 to 1
- grad_out: bfloat16 [2, 192, 256, 512], P(None, 'row', 'col'), may hold values from -6 to 6
- crop_start: int32 [2, 2], replicated, may hold values from 0 to 3
Outputs:
- grad_tokens: bfloat16 [2, 192, 256, 512], P(None, 'row', 'col')
- grad_w_qkv: float32 [512, 1536], P('row', 'col')
- grad_w_out: float32 [512, 512], P('row', 'col')
The draws below stay inside these ranges and needn't reach their ends.
Inputs may be any that keep to these rules, and one draw needn't show every extreme that they name: crop_start[b] holds the first row and the first column of the region of frame b that the loss covers.
All inputs are finite; a program needn't handle non-finite values.
Results may differ from the reference program's by a relative error of at most 0.017.
Values may be sent and summed in bfloat16 or wider, within the bound.
No kernel may reach another device: no remote copies, remote signals or barrier semaphores. Data moves between devices by JAX's collectives and lax.ppermute only.
A program may use at most 128 MiB of HBM per device.

```python
import math
import jax
import jax.numpy as jnp
from jax import lax

WIDTH = 512
HEADS = 8
RADIUS = 4
BLOCK = 8
BATCH = 2
FRAME_ROWS = 192
FRAME_COLS = 256


def draw_q_saved(key, part):
    shape = (BATCH, FRAME_ROWS, FRAME_COLS, WIDTH)
    own_key = jax.random.fold_in(key, 11)
    return jnp.clip(jax.random.normal(own_key, shape, jnp.float32), -4.0, 4.0).astype(jnp.bfloat16)


def draw_k_saved(key, part):
    shape = (BATCH, FRAME_ROWS, FRAME_COLS, WIDTH)
    own_key = jax.random.fold_in(key, 13)
    return jnp.clip(jax.random.normal(own_key, shape, jnp.float32), -4.0, 4.0).astype(jnp.bfloat16)


def touch_ends(array, key, least, top_value):
    shape = array.shape
    place = [jax.random.randint(jax.random.fold_in(key, axis), (), 0, shape[axis]) for axis in range(len(shape))]
    array = array.at[tuple(place)].set(least)
    longest = shape.index(max(shape))
    place[longest] = (place[longest] + 1) % shape[longest]
    return array.at[tuple(place)].set(top_value)


def strengthened(result, key, source, target, shards_of, factor):
    def block_of(dim):
        return (jnp.arange(result.shape[dim]) // (result.shape[dim] // shards_of)).reshape((-1,) + (1,) * (result.ndim - 1 - dim))

    one_side = jax.random.permutation(key, shards_of)[block_of(target)]
    other_side = (block_of(target) + shards_of // 2) % shards_of
    return jnp.where((block_of(source) == one_side) | (block_of(source) == other_side), factor * result, result)


def block_scale(rng, dims, shards, least, largest):
    level, own = 1.0, jax.random.fold_in(rng, 6)
    for axis_at, shards_of in shards:
        heights = jnp.exp(jax.random.uniform(jax.random.fold_in(own, axis_at), (shards_of,), jnp.float32, least / len(shards), largest / len(shards)))
        level = level * jnp.repeat(heights, dims[axis_at] // shards_of).reshape([-1 if axis == axis_at else 1 for axis in range(len(dims))])
    return level


def scatter_about(rng, shape, deviation, most, cuts=(), held_as=jnp.bfloat16):
    result = deviation * jax.random.normal(rng, shape, jnp.float32)
    if cuts:
        result = result * block_scale(rng, shape, cuts, -0.22, 0.18)
    return jnp.clip(result, -most, most).astype(held_as)


def gaussian_with(stream_key, dims, spread, most, shards, heavy, kind=jnp.bfloat16):
    drawn = spread * jax.random.normal(stream_key, dims, jnp.float32)
    if shards:
        drawn = drawn * block_scale(stream_key, dims, shards, -0.22, 0.18)
    return jnp.clip(strengthened(drawn, jax.random.fold_in(stream_key, 3), *heavy), -most, most).astype(kind)


def setup_inputs(seed: int = 0) -> dict:
    key_of = jax.random.split(jax.random.key(seed), 10)
    tokens = gaussian_with(key_of[0], (BATCH, FRAME_ROWS, FRAME_COLS, WIDTH), 1.0, 6.0, ((1, 8), (2, 16)), (1, 3, 8, 2.0))
    w_qkv = scatter_about(key_of[1], (WIDTH, 3 * WIDTH), WIDTH ** -0.5, 0.25)
    w_out = scatter_about(key_of[2], (WIDTH, WIDTH), WIDTH ** -0.5, 0.25)
    q_saved = draw_q_saved(jax.random.fold_in(key_of[9], 71), 0)
    k_saved = draw_k_saved(jax.random.fold_in(key_of[9], 71), 0)
    v_saved = scatter_about(key_of[5], (BATCH, FRAME_ROWS, FRAME_COLS, WIDTH), 1.0, 4.0, ((1, 8), (2, 16)))
    scale_exp = touch_ends(jax.random.randint(key_of[6], (BATCH, FRAME_ROWS // BLOCK, FRAME_COLS // BLOCK, 3 * HEADS), -1, 2), jax.random.fold_in(key_of[6], 1), -1, 1).astype(jnp.int32)
    grad_out = gaussian_with(key_of[7], (BATCH, FRAME_ROWS, FRAME_COLS, WIDTH), 1.0, 6.0, ((1, 8), (2, 16)), (2, 3, 16, 2.0))
    crop_start = touch_ends(jax.random.randint(key_of[8], (BATCH, 2), 0, RADIUS), jax.random.fold_in(key_of[8], 1), 0, RADIUS - 1).astype(jnp.int32)
    return dict(tokens=tokens, w_qkv=w_qkv, w_out=w_out, q_saved=q_saved, k_saved=k_saved, v_saved=v_saved, scale_exp=scale_exp, grad_out=grad_out, crop_start=crop_start)


max_norm = 1000.0
masked_score = -1e+30
tiny_square = 1e-06

def product(form, left, right):
    return jnp.einsum(form, left.astype(jnp.float32), right.astype(jnp.float32))

def dequantize(mantissa, exponent):
    members, height, breadth, features = mantissa.shape
    heads = exponent.shape[3]
    factor = jnp.exp2(exponent.astype(jnp.float32))
    factor = jnp.repeat(jnp.repeat(factor, BLOCK, axis=1), BLOCK, axis=2)
    scaled = mantissa.astype(jnp.float32).reshape(members, height, breadth, heads, features // heads) * factor[..., None]
    return scaled.reshape(members, height, breadth, features).astype(jnp.bfloat16)

def query_tiles(tensor):
    height, breadth, features = tensor.shape
    blocked = tensor.reshape(height // BLOCK, BLOCK, breadth // BLOCK, BLOCK, HEADS, features // HEADS)
    return blocked.transpose(0, 2, 1, 3, 4, 5).reshape(height // BLOCK, breadth // BLOCK, BLOCK * BLOCK, HEADS, features // HEADS)

def query_untile(tile_set, height, breadth):
    tile_rows, tile_cols = (tile_set.shape[0], tile_set.shape[1])
    features = tile_set.shape[3] * tile_set.shape[4]
    blocked = tile_set.reshape(tile_rows, tile_cols, BLOCK, BLOCK, features)
    return blocked.transpose(0, 2, 1, 3, 4).reshape(height, breadth, features)

def key_tiles(padded):
    height, breadth, features = padded.shape
    tile_rows = height // BLOCK - 1
    tile_cols = breadth // BLOCK - 1
    blocked = padded.reshape(tile_rows + 1, BLOCK, tile_cols + 1, BLOCK, features)
    paired = jnp.stack([blocked[:-1], blocked[1:]], axis=1).reshape(tile_rows, 2 * BLOCK, tile_cols + 1, BLOCK, features)
    paired = jnp.stack([paired[:, :, :-1], paired[:, :, 1:]], axis=3).reshape(tile_rows, 2 * BLOCK, tile_cols, 2 * BLOCK, features)
    return paired.transpose(0, 2, 1, 3, 4).reshape(tile_rows, tile_cols, 4 * BLOCK * BLOCK, HEADS, features // HEADS)

def fold_keys(tile_set):
    tile_rows, tile_cols = (tile_set.shape[0], tile_set.shape[1])
    features = tile_set.shape[3] * tile_set.shape[4]
    tile_grid = tile_set.reshape(tile_rows, tile_cols, 2, BLOCK, 2, BLOCK, features).transpose(0, 2, 3, 1, 4, 5, 6)
    zero_row = jnp.zeros((1, BLOCK, tile_cols, 2, BLOCK, features), tile_set.dtype)
    summed = jnp.concatenate([tile_grid[:, 0], zero_row], 0) + jnp.concatenate([zero_row, tile_grid[:, 1]], 0)
    zero_col = jnp.zeros((tile_rows + 1, BLOCK, 1, BLOCK, features), tile_set.dtype)
    summed = jnp.concatenate([summed[:, :, :, 0], zero_col], 2) + jnp.concatenate([zero_col, summed[:, :, :, 1]], 2)
    return summed.reshape((tile_rows + 1) * BLOCK, (tile_cols + 1) * BLOCK, features)

def key_valid(anchor, tile_count, extent):
    position = anchor + BLOCK * jnp.arange(tile_count, dtype=jnp.int32)[:, None] + jnp.arange(2 * BLOCK, dtype=jnp.int32)[None, :]
    return (position >= 0) & (position < extent)

def window_mask():
    reach = jnp.arange(2 * BLOCK, dtype=jnp.int32)[None, :] - jnp.arange(BLOCK, dtype=jnp.int32)[:, None]
    inside = (reach >= 0) & (reach <= 2 * RADIUS)
    return (inside[:, None, :, None] & inside[None, :, None, :]).reshape(BLOCK * BLOCK, 4 * BLOCK * BLOCK)

def attend(queries, grads_attn, keys_pad, values_pad, row_anchor, col_anchor, frame_rows, frame_cols):
    height, breadth, features = queries.shape
    score_scale = 1.0 / math.sqrt(features // HEADS)
    q_tiles = query_tiles(queries)
    g_tiles = query_tiles(grads_attn)
    k_tiles = key_tiles(keys_pad)
    v_tiles = key_tiles(values_pad)
    tile_rows, tile_cols = (q_tiles.shape[0], q_tiles.shape[1])
    row_ok = key_valid(row_anchor, tile_rows, frame_rows)
    col_ok = key_valid(col_anchor, tile_cols, frame_cols)
    keys_ok = (row_ok[:, None, :, None] & col_ok[None, :, None, :]).reshape(tile_rows, tile_cols, 1, 1, 4 * BLOCK * BLOCK)
    allowed = keys_ok & window_mask()[None, None, None]
    scores = product('ijqhd,ijkhd->ijhqk', q_tiles, k_tiles) * score_scale
    scores = jnp.where(allowed, scores, masked_score)
    row_max = lax.optimization_barrier(jnp.max(scores, axis=-1, keepdims=True))
    weights = jnp.exp(scores - row_max)
    softmax = weights / lax.optimization_barrier(jnp.sum(weights, axis=-1, keepdims=True))
    softmax_half = softmax.astype(jnp.bfloat16)
    out_tiles = product('ijhqk,ijkhd->ijqhd', softmax_half, v_tiles).astype(jnp.bfloat16)
    row_delta = product('ijqhd,ijqhd->ijhq', g_tiles, out_tiles)
    grad_probs = product('ijqhd,ijkhd->ijhqk', g_tiles, v_tiles)
    grad_scores = (softmax * (grad_probs - row_delta[..., None]) * score_scale).astype(jnp.bfloat16)
    grad_q_tiles = product('ijhqk,ijkhd->ijqhd', grad_scores, k_tiles)
    grad_k_tiles = product('ijhqk,ijqhd->ijkhd', grad_scores, q_tiles)
    grad_v_tiles = product('ijhqk,ijqhd->ijkhd', softmax_half, g_tiles)
    return (query_untile(out_tiles, height, breadth), query_untile(grad_q_tiles, height, breadth), fold_keys(grad_k_tiles), fold_keys(grad_v_tiles))

def reference(tokens, w_qkv, w_out, q_saved, k_saved, v_saved, scale_exp, grad_out, crop_start):
    members, height, breadth, features = tokens.shape
    queries = dequantize(q_saved, scale_exp[..., :HEADS])
    keys_full = dequantize(k_saved, scale_exp[..., HEADS:2 * HEADS])
    values = dequantize(v_saved, scale_exp[..., 2 * HEADS:])
    row_place = jnp.arange(height, dtype=jnp.int32)
    col_place = jnp.arange(breadth, dtype=jnp.int32)
    inside = (row_place[None, :, None] >= crop_start[:, 0][:, None, None]) & (col_place[None, None, :] >= crop_start[:, 1][:, None, None])
    masked = jnp.where(inside[..., None], grad_out, jnp.zeros_like(grad_out))
    flat_grad = masked.reshape(-1, features)
    grad_attn = jnp.dot(flat_grad, w_out.T, preferred_element_type=jnp.float32).astype(jnp.bfloat16).reshape(masked.shape)
    padding = ((RADIUS, RADIUS), (RADIUS, RADIUS), (0, 0))

    def one_member(member):
        q_member, g_member, k_member, v_member = member
        keys_pad = jnp.pad(k_member, padding)
        values_pad = jnp.pad(v_member, padding)

        def strip_step(running, strip_index):
            row_start = (strip_index * BLOCK).astype(jnp.int32)
            anchor_zero = jnp.zeros((), jnp.int32)
            q_strip = lax.dynamic_slice_in_dim(q_member, row_start, BLOCK, 0)
            g_strip = lax.dynamic_slice_in_dim(g_member, row_start, BLOCK, 0)
            k_strip = lax.dynamic_slice_in_dim(keys_pad, row_start, 2 * BLOCK, 0)
            v_strip = lax.dynamic_slice_in_dim(values_pad, row_start, 2 * BLOCK, 0)
            out_strip, grad_q_strip, grad_k_strip, grad_v_strip = attend(q_strip, g_strip, k_strip, v_strip, row_start - RADIUS, -RADIUS, height, breadth)
            grad_k_sum, grad_v_sum = running
            corner = (row_start, anchor_zero, anchor_zero)
            grad_k_sum = lax.dynamic_update_slice(grad_k_sum, lax.dynamic_slice(grad_k_sum, corner, grad_k_strip.shape) + grad_k_strip, corner)
            grad_v_sum = lax.dynamic_update_slice(grad_v_sum, lax.dynamic_slice(grad_v_sum, corner, grad_v_strip.shape) + grad_v_strip, corner)
            return ((grad_k_sum, grad_v_sum), (out_strip, grad_q_strip))
        initial = (jnp.zeros(keys_pad.shape, jnp.float32), jnp.zeros(values_pad.shape, jnp.float32))
        (grad_k_sum, grad_v_sum), (out_strips, grad_q_strips) = lax.scan(strip_step, initial, jnp.arange(height // BLOCK, dtype=jnp.int32))
        return (out_strips.reshape(height, breadth, features), grad_q_strips.reshape(height, breadth, features), grad_k_sum[RADIUS:RADIUS + height, RADIUS:RADIUS + breadth], grad_v_sum[RADIUS:RADIUS + height, RADIUS:RADIUS + breadth])
    attn_out, grad_query, grad_key, grad_value = lax.map(one_member, (queries, grad_attn, keys_full, values))
    flat_qkv = jnp.concatenate([grad_query, grad_key, grad_value], axis=-1).astype(jnp.bfloat16).reshape(-1, 3 * features)
    grad_tokens = jnp.dot(flat_qkv, w_qkv.T, preferred_element_type=jnp.float32).astype(jnp.bfloat16).reshape(tokens.shape)
    raw_qkv = jnp.dot(tokens.reshape(-1, features).T, flat_qkv, preferred_element_type=jnp.float32)
    raw_out = jnp.dot(attn_out.reshape(-1, features).T, flat_grad, preferred_element_type=jnp.float32)
    squares = jnp.sum(raw_qkv * raw_qkv) + jnp.sum(raw_out * raw_out)
    factor = jnp.minimum(1.0, max_norm / jnp.sqrt(squares + tiny_square))
    return (grad_tokens, factor * raw_qkv, factor * raw_out)
```

```python
import jax
import jax.numpy as jnp
from jax import lax
from jax.experimental import pallas as pl
from jax.experimental.pallas import tpu as pltpu
from jax.sharding import PartitionSpec as P

HEADS = 8
RADIUS = 4
BLOCK = 8
GROUP = 4

max_norm = 1000.0
masked_score = -1e30
tiny_square = 1e-06

f32 = jnp.float32
bf16 = jnp.bfloat16
VMEM = pl.BlockSpec(memory_space=pltpu.VMEM)
COLS = ("pair", "core")
SMEM = pl.BlockSpec(memory_space=pltpu.SMEM)


def call(kernel, outs, ins, scratch=(), smem=(), flops=0, limit=56 << 20):
    moved = sum(a.size * a.dtype.itemsize for a in list(ins) + list(outs))
    return pl.pallas_call(
        kernel,
        out_shape=outs,
        in_specs=[SMEM if n in smem else VMEM for n in range(len(ins))],
        out_specs=jax.tree.map(lambda _: VMEM, outs),
        scratch_shapes=list(scratch),
        compiler_params=pltpu.CompilerParams(vmem_limit_bytes=limit),
        cost_estimate=pl.CostEstimate(
            flops=flops, bytes_accessed=moved, transcendentals=0
        ),
    )(*ins)


def shape(*dims, dtype=bf16):
    return jax.ShapeDtypeStruct(dims, dtype)


def turn(x):
    return pltpu.roll(x, 4, 1)


def sublane(x):
    return lax.broadcasted_iota(jnp.int32, x.shape, 1)


def block_of(ref, fac_ref, part, b, i, j, rows, features):
    tiles = fac_ref.shape[2]
    factor = fac_ref[b, i, j : j + 1, part * features : (part + 1) * features]
    del tiles
    x = ref[b, rows, 8 * j : 8 * j + 8, :].astype(f32)
    return x * factor[None]


def edge_kernel(k_ref, v_ref, fac_ref, up_ref, down_ref, left_ref, right_ref):
    members, height, breadth, features = k_ref.shape
    tiles, last = breadth // 8, height // 8 - 1
    for b in range(members):
        for n, ref in enumerate((k_ref, v_ref)):
            top = [block_of(ref, fac_ref, n + 1, b, 0, j, pl.ds(0, 4), features) for j in range(tiles)]
            up_ref[n, b] = jnp.concatenate(top, 1).astype(bf16)
            low = [
                block_of(ref, fac_ref, n + 1, b, last, j, pl.ds(height - 4, 4), features)
                for j in range(tiles)
            ]
            down_ref[n, b] = jnp.concatenate(low, 1).astype(bf16)
        for i in range(height // 8):
            rows = pl.ds(8 * i, 8)
            k0 = block_of(k_ref, fac_ref, 1, b, i, 0, rows, features)
            v0 = block_of(v_ref, fac_ref, 2, b, i, 0, rows, features)
            k1 = block_of(k_ref, fac_ref, 1, b, i, tiles - 1, rows, features)
            v1 = block_of(v_ref, fac_ref, 2, b, i, tiles - 1, rows, features)
            low = sublane(k0) < 4
            left_ref[b, rows] = jnp.where(low, k0, turn(v0)).astype(bf16)
            right_ref[b, rows] = jnp.where(low, turn(v1), k1).astype(bf16)


def corner_kernel(top_ref, bottom_ref, left_ref, right_ref):
    parts, members, rows, breadth, features = top_ref.shape
    for b in range(members):
        for n, ref in enumerate((top_ref, bottom_ref)):
            k0 = ref[0, b, :, 0:8, :].astype(f32)
            v0 = ref[1, b, :, 0:8, :].astype(f32)
            k1 = ref[0, b, :, breadth - 8 : breadth, :].astype(f32)
            v1 = ref[1, b, :, breadth - 8 : breadth, :].astype(f32)
            low = sublane(k0) < 4
            left_ref[b, 4 * n : 4 * n + 4] = jnp.where(low, k0, turn(v0)).astype(bf16)
            right_ref[b, 4 * n : 4 * n + 4] = jnp.where(low, turn(v1), k1).astype(bf16)


def prepare_kernel(place_ref, q_ref, g_ref, fac_ref, w_ref, qs_ref, gm_ref, do_ref):
    members, height, breadth, features = q_ref.shape
    tiles = breadth // 8
    for b in range(members):
        for i in range(height // 8):
            rows = pl.ds(8 * i, 8)
            parts = [block_of(q_ref, fac_ref, 0, b, i, j, rows, features) for j in range(tiles)]
            qs_ref[b, rows] = (jnp.concatenate(parts, 1) * 0.125).astype(bf16)
            g = g_ref[b, rows].astype(f32)
            r = lax.broadcasted_iota(jnp.int32, g.shape, 0) + (8 * i + place_ref[0])
            c = lax.broadcasted_iota(jnp.int32, g.shape, 1) + place_ref[1]
            keep = (r >= place_ref[2 + 2 * b]) & (c >= place_ref[3 + 2 * b])
            gm = jnp.where(keep, g, 0.0).astype(bf16)
            gm_ref[b, rows] = gm
            do = lax.dot_general(
                gm.reshape(8 * breadth, features), w_ref[...], (((1,), (1,)), ((), ())),
                preferred_element_type=f32,
            )
            do_ref[b, rows] = do.astype(bf16).reshape(8, breadth, features)


def attend_kernel(
    place_ref, qs_ref, do_ref, k_ref, v_ref, fac_ref, gm_ref, tok_ref,
    top_ref, bottom_ref, left_ref, right_ref, cl_ref, cr_ref,
    dq_ref, first_ref, dk_ref, dv_ref, dl_ref, dr_ref,
    kt_ref, vt_ref, dkt_ref, dvt_ref, o_ref,
):
    members, height, breadth, features = qs_ref.shape
    strips, tiles = height // 8, breadth // 8
    heads_lanes = features // HEADS
    wide = GROUP * heads_lanes
    groups = HEADS // GROUP
    frame_rows, frame_cols = place_ref[6], place_ref[7]

    def put(b, rows, kblocks, vblocks, lmsg, rmsg):
        low = sublane(lmsg) < 4
        for ref, blocks, lm, rm in (
            (kt_ref, kblocks, lmsg, rmsg),
            (vt_ref, vblocks, turn(lmsg), turn(rmsg)),
        ):
            for t in range(tiles):
                before = lm if t == 0 else blocks[t - 1]
                after = rm if t == tiles - 1 else blocks[t + 1]
                rim = jnp.where(low, after, before)
                ref[b, t, rows] = jnp.concatenate([blocks[t], rim], 1).astype(bf16)

    for b in range(members):
        for n, ref in enumerate((top_ref, bottom_ref)):
            halo = slice(0, 4) if n == 0 else slice(height + 4, height + 8)
            kb = [ref[0, b, :, 8 * j : 8 * j + 8, :].astype(f32) for j in range(tiles)]
            vb = [ref[1, b, :, 8 * j : 8 * j + 8, :].astype(f32) for j in range(tiles)]
            put(b, halo, kb, vb, cl_ref[b, 4 * n : 4 * n + 4].astype(f32), cr_ref[b, 4 * n : 4 * n + 4].astype(f32))
        for i in range(strips):
            rows = pl.ds(8 * i, 8)
            kb = [block_of(k_ref, fac_ref, 1, b, i, j, rows, features) for j in range(tiles)]
            vb = [block_of(v_ref, fac_ref, 2, b, i, j, rows, features) for j in range(tiles)]
            put(b, slice(8 * i + 4, 8 * i + 12), kb, vb, left_ref[b, rows].astype(f32), right_ref[b, rows].astype(f32))

    for b in range(members):
        for t in range(tiles):
            dkt_ref[b, t, 0:8] = jnp.zeros((8, 16, features), f32)
            dvt_ref[b, t, 0:8] = jnp.zeros((8, 16, features), f32)

    lane = lax.broadcasted_iota(jnp.int32, (1, wide), 1) // heads_lanes
    head_mask = [(lane == h).astype(f32).astype(bf16) for h in range(GROUP)]
    half = lax.broadcasted_iota(jnp.int32, (64, 2 * heads_lanes), 1) < heads_lanes

    def spread(x):
        return jnp.concatenate([x * m for m in head_mask], 0)

    def gather(x):
        return jnp.concatenate(
            [
                jnp.where(half, x[128 * n : 128 * n + 64, 128 * n : 128 * n + 128],
                          x[128 * n + 64 : 128 * n + 128, 128 * n : 128 * n + 128])
                for n in range(GROUP // 2)
            ],
            1,
        )

    def bias_of(i, t):
        qn = lax.broadcasted_iota(jnp.int32, (64, 256), 0)
        kn = lax.broadcasted_iota(jnp.int32, (64, 256), 1)
        qr, qc = qn // 8, qn % 8
        kr, ks = kn // 16, kn % 16
        kc = jnp.where(ks < 8, ks, jnp.where(ks < 12, ks, ks - 16))
        row = place_ref[0] + 8 * i - 4 + kr
        col = place_ref[1] + 8 * t + kc
        ok = (kr >= qr) & (kr <= qr + 8) & (kc >= qc - 4) & (kc <= qc + 4)
        ok &= (row >= 0) & (row < frame_rows) & (col >= 0) & (col < frame_cols)
        return jnp.where(ok, 0.0, masked_score)

    def step(n, _):
        b, i = n // strips, n % strips
        rows = pl.ds(8 * i, 8)
        q8 = qs_ref[b, rows].astype(f32)
        g8 = do_ref[b, rows].astype(f32)
        outs, grads = [], []
        for t in range(tiles):
            bias = bias_of(i, t)
            bias4 = jnp.concatenate([bias] * GROUP, 0)
            q64 = q8[:, 8 * t : 8 * t + 8].reshape(64, features).astype(bf16)
            g64 = g8[:, 8 * t : 8 * t + 8].reshape(64, features).astype(bf16)
            keys = pl.ds(8 * i, 16)
            ot, dqt = [], []
            for g in range(groups):
                lanes = slice(g * wide, (g + 1) * wide)
                qx, gx = spread(q64[:, lanes]), spread(g64[:, lanes])
                k = kt_ref[b, t, keys, :, lanes].reshape(256, wide)
                v = vt_ref[b, t, keys, :, lanes].reshape(256, wide)
                across = (((1,), (1,)), ((), ()))
                s = lax.dot_general(qx, k, across, preferred_element_type=f32) + bias4
                w = jnp.exp(s - jnp.max(s, 1, keepdims=True))
                p = w * (1.0 / jnp.sum(w, 1, keepdims=True))
                ph = p.astype(bf16)
                o = jnp.dot(ph, v, preferred_element_type=f32).astype(bf16).astype(f32)
                delta = jnp.sum(o * gx.astype(f32), 1, keepdims=True)
                dp = lax.dot_general(gx, v, across, preferred_element_type=f32)
                ds = (p * (dp - delta)).astype(bf16)
                dq = jnp.dot(ds, k, preferred_element_type=f32)
                down = (((0,), (0,)), ((), ()))
                dk = lax.dot_general(ds, qx, down, preferred_element_type=f32).reshape(16, 16, wide)
                dv = lax.dot_general(ph, gx, down, preferred_element_type=f32).reshape(16, 16, wide)
                ot.append(gather(o))
                dqt.append(gather(dq) * 0.125)
                for ref, x in ((dkt_ref, dk), (dvt_ref, dv)):
                    ref[b, t, rows, :, lanes] = ref[b, t, rows, :, lanes] + x[0:8]
                    ref[b, t, pl.ds(8 * i + 8, 8), :, lanes] = x[8:16]
            outs.append(jnp.concatenate(ot, 1).reshape(8, 8, features))
            grads.append(jnp.concatenate(dqt, 1).reshape(8, 8, features))
        o_ref[b, rows] = jnp.concatenate(outs, 1).astype(bf16)
        dq_ref[b, rows] = jnp.concatenate(grads, 1).astype(bf16)
        return 0

    lax.fori_loop(0, members * strips, step, 0)

    for b in range(members):
        for r in range(0, height + 8, 8):
            rows = slice(r, r + 8)
            rims = []
            for ref, out in ((dkt_ref, dk_ref), (dvt_ref, dv_ref)):
                rim = [ref[b, t, rows, 8:16] for t in range(tiles)]
                low = sublane(rim[0]) < 4
                own = []
                for t in range(tiles):
                    x = ref[b, t, rows, 0:8]
                    if t > 0:
                        x = x + jnp.where(low, rim[t - 1], 0.0)
                    if t < tiles - 1:
                        x = x + jnp.where(low, 0.0, rim[t + 1])
                    own.append(x)
                out[b, rows] = jnp.concatenate(own, 1)
                rims.append((rim[0], rim[tiles - 1]))
            (kl, kr), (vl, vr) = rims
            dl_ref[b, rows] = jnp.where(low, turn(vl), kl).astype(bf16)
            dr_ref[b, rows] = jnp.where(low, kr, turn(vr)).astype(bf16)

    cells = members * height * breadth
    down = (((0,), (0,)), ((), ()))
    first_ref[:, 0:features] = lax.dot_general(
        tok_ref[...].reshape(cells, features), dq_ref[...].reshape(cells, features), down,
        preferred_element_type=f32,
    ).astype(first_ref.dtype)
    first_ref[:, features:] = lax.dot_general(
        o_ref[...].reshape(cells, features), gm_ref[...].reshape(cells, features), down,
        preferred_element_type=f32,
    ).astype(first_ref.dtype)


def rim_kernel(dk_ref, dv_ref, fl_ref, fr_ref, dkc_ref, dvc_ref, up_ref, down_ref):
    members, tall, breadth, features = dk_ref.shape
    height = tall - 8
    last = breadth - 8
    for b in range(members):
        for r in range(0, tall, 4):
            rows = slice(r, r + 4)
            fl = fl_ref[b, rows].astype(f32)
            fr = fr_ref[b, rows].astype(f32)
            low = sublane(fl) < 4
            adds = (
                (jnp.where(low, fl, 0.0), jnp.where(low, 0.0, fr)),
                (jnp.where(low, turn(fl), 0.0), jnp.where(low, 0.0, turn(fr))),
            )
            for n, (ref, out) in enumerate(((dk_ref, dkc_ref), (dv_ref, dvc_ref))):
                x = ref[b, rows]
                parts = [x[:, 8 * j : 8 * j + 8] for j in range(breadth // 8)]
                parts[0] = parts[0] + adds[n][0]
                parts[-1] = parts[-1] + adds[n][1]
                x = jnp.concatenate(parts, 1)
                if r == 0:
                    up_ref[n, b] = x.astype(bf16)
                elif r == tall - 4:
                    down_ref[n, b] = x.astype(bf16)
                else:
                    out[b, r - 4 : r] = x
    del last, height


def finish_kernel(
    core_ref, dk_ref, dv_ref, ft_ref, fb_ref, dq_ref, tok_ref, w_ref, first_ref,
    gt_ref, keep_ref, send_ref, kv_ref, all_ref,
):
    members, height, breadth, features = dk_ref.shape
    for n, ref in enumerate((dk_ref, dv_ref)):
        lanes = slice(n * features, (n + 1) * features)
        for b in range(members):
            for r in range(0, height, 4):
                x = ref[b, r : r + 4]
                if r == 0:
                    x = x + ft_ref[n, b].astype(f32)
                if r == height - 4:
                    x = x + fb_ref[n, b].astype(f32)
                kv_ref[b, r : r + 4, :, lanes] = x.astype(bf16)
    cells = members * height * breadth
    down = (((0,), (0,)), ((), ()))
    across = (((1,), (1,)), ((), ()))
    kv = kv_ref[...].reshape(cells, 2 * features)
    all_ref[:, 0:features] = first_ref[:, 0:features]
    all_ref[:, features : 3 * features] = lax.dot_general(
        tok_ref[...].reshape(cells, features), kv, down, preferred_element_type=f32
    )
    gt = lax.dot_general(
        dq_ref[...].reshape(cells, features), w_ref[:, 0:features], across, preferred_element_type=f32
    ) + lax.dot_general(kv, w_ref[:, features:], across, preferred_element_type=f32)
    gt_ref[...] = gt.astype(bf16).reshape(members, height, breadth, features)

    rows, pairs, deep, wide = keep_ref.shape
    count = 2 * pairs
    main, rest = 3 * features // count, features // count
    lane = lax.broadcasted_iota(jnp.int32, (features, wide), 1)

    def window(ref, start, end):
        base, off = start // wide * wide, start % wide
        x = ref[:, base : base + wide]
        if off:
            x = pltpu.roll(x, wide - off, 1)
        if end > base + wide:
            y = pltpu.roll(ref[:, base + wide : base + 2 * wide], wide - off, 1)
            x = jnp.where(lane < wide - off, x, y)
        return x

    def block(c):
        x = window(all_ref, main * c, main * (c + 1))
        base, off = rest * c // wide * wide, rest * c % wide
        y = first_ref[:, features + base : features + base + wide]
        if off != main:
            y = pltpu.roll(y, (main - off) % wide, 1)
        return jnp.where(lane < main, x, y).astype(bf16).reshape(rows, deep, wide)

    mine = core_ref[0] == 0
    for p in range(pairs):
        even, odd = block(2 * p), block(2 * p + 1)
        keep_ref[:, p] = jnp.where(mine, even, odd)
        send_ref[:, p] = jnp.where(mine, odd, even)


def total_kernel(x_ref, sum_ref, square_ref):
    x = jnp.sum(x_ref[...].astype(f32), 0)
    sum_ref[...] = x
    square = jnp.sum(x * x, 0, keepdims=True)
    square_ref[...] = jnp.broadcast_to(square, square_ref.shape)


def clip_kernel(x_ref, square_ref, qkv_ref, out_ref):
    total = jnp.sum(jnp.sum(square_ref[...], 0, keepdims=True), 1, keepdims=True)
    clip = jnp.minimum(1.0, max_norm / jnp.sqrt(total + tiny_square))
    x = x_ref[...] * clip
    main = qkv_ref.shape[1]
    qkv_ref[...] = x[:, 0:main]
    out_ref[...] = pltpu.roll(x, x.shape[1] - main, 1)[:, 0 : out_ref.shape[1]]


def shift(x, axis, by):
    size = lax.axis_size(axis)
    return lax.ppermute(x, axis, [(i, i + by) for i in range(size) if 0 <= i + by < size])


def body(tokens, w_qkv, w_out, q_saved, k_saved, v_saved, scale_exp, grad_out, crop_start):
    members, height, breadth, features = tokens.shape
    row_index, col_index = lax.axis_index("row"), lax.axis_index(COLS)
    frame_rows = height * lax.axis_size("row")
    frame_cols = breadth * lax.axis_size(COLS)
    place = jnp.concatenate(
        [
            jnp.stack([row_index * height, col_index * breadth]).astype(jnp.int32),
            crop_start.reshape(-1),
            jnp.array([frame_rows, frame_cols], jnp.int32),
        ]
    )
    factor = jnp.repeat(jnp.exp2(scale_exp.astype(f32)), features // HEADS, axis=3)

    up, down, left, right = call(
        edge_kernel,
        (
            shape(2, members, 4, breadth, features),
            shape(2, members, 4, breadth, features),
            shape(members, height, 8, features),
            shape(members, height, 8, features),
        ),
        (k_saved, v_saved, factor),
    )
    top, bottom = shift(down, "row", 1), shift(up, "row", -1)
    from_left, from_right = shift(right, COLS, 1), shift(left, COLS, -1)
    qs, gm, do = call(
        prepare_kernel,
        (shape(*tokens.shape),) * 3,
        (place, q_saved, grad_out, factor, w_out),
        smem=(0,),
    )
    cleft, cright = call(
        corner_kernel,
        (shape(members, 8, 8, features),) * 2,
        (top, bottom),
    )
    corner_left, corner_right = shift(cright, COLS, 1), shift(cleft, COLS, -1)
    tall = height + 8
    tile_shape = (members, breadth // 8, tall, 16, features)
    dq, first, dk, dv, dl, dr = call(
        attend_kernel,
        (
            shape(*tokens.shape),
            shape(features, 2 * features, dtype=f32),
            shape(members, tall, breadth, features, dtype=f32),
            shape(members, tall, breadth, features, dtype=f32),
            shape(members, tall, 8, features),
            shape(members, tall, 8, features),
        ),
        (place, qs, do, k_saved, v_saved, factor, gm, tokens,
         top, bottom, from_left, from_right, corner_left, corner_right),
        scratch=(
            pltpu.VMEM(tile_shape, bf16),
            pltpu.VMEM(tile_shape, bf16),
            pltpu.VMEM(tile_shape, f32),
            pltpu.VMEM(tile_shape, f32),
            pltpu.VMEM(tokens.shape, bf16),
        ),
        smem=(0,),
    )
    back_left, back_right = shift(dr, COLS, 1), shift(dl, COLS, -1)
    dkc, dvc, gup, gdown = call(
        rim_kernel,
        (
            shape(members, height, breadth, features, dtype=f32),
            shape(members, height, breadth, features, dtype=f32),
            shape(2, members, 4, breadth, features),
            shape(2, members, 4, breadth, features),
        ),
        (dk, dv, back_left, back_right),
    )
    back_top, back_bottom = shift(gdown, "row", 1), shift(gup, "row", -1)
    rows, pairs = lax.axis_size("row"), lax.axis_size("pair")
    core = lax.axis_index("core")
    deep = features // rows
    wide = 4 * features // (2 * pairs)
    grad_tokens, keep, send = call(
        finish_kernel,
        (shape(*tokens.shape), shape(rows, pairs, deep, wide), shape(rows, pairs, deep, wide)),
        (core.astype(jnp.int32).reshape(1), dkc, dvc, back_top, back_bottom, dq, tokens, w_qkv, first),
        scratch=(
            pltpu.VMEM((members, height, breadth, 2 * features), bf16),
            pltpu.VMEM((features, 3 * features), f32),
        ),
        smem=(0,),
    )
    other = lax.ppermute(send, "core", [(0, 1), (1, 0)])
    both = (keep.astype(f32) + other.astype(f32)).astype(bf16).reshape(rows * pairs, deep, wide)
    parts = lax.all_to_all(both, ("row", "pair"), 0, 0, tiled=True)
    total, square = call(
        total_kernel,
        (shape(deep, wide, dtype=f32), shape(2 * rows * pairs, wide, dtype=f32)),
        (parts,),
    )
    squares = lax.all_to_all(square, ("row", "pair", "core"), 0, 0, tiled=True)
    main = 3 * features // (2 * pairs)
    grad_qkv, grad_out_w = call(
        clip_kernel,
        (shape(deep, main, dtype=f32), shape(deep, wide - main, dtype=f32)),
        (total, squares),
    )
    return grad_tokens, grad_qkv, grad_out_w


def solution(mesh):
    rows, cols = mesh.devices.shape
    split = jax.sharding.Mesh(mesh.devices.reshape(rows, cols // 2, 2), ("row",) + COLS)
    cells = P(None, "row", COLS, None)
    return jax.shard_map(
        body,
        mesh=split,
        in_specs=(cells, P(), P(), cells, cells, cells, cells, cells, P()),
        out_specs=(cells, P("row", COLS), P("row", COLS)),
        check_vma=False,
    )
```

```python
import jax
import jax.numpy as jnp
from jax import lax
from jax.experimental import pallas as pl
from jax.experimental.pallas import tpu as pltpu
from jax.sharding import PartitionSpec as P

HEADS = 8
RADIUS = 4
BLOCK = 8
GROUP = 4

max_norm = 1000.0
masked_score = -1e30
tiny_square = 1e-06

f32 = jnp.float32
bf16 = jnp.bfloat16
VMEM = pl.BlockSpec(memory_space=pltpu.VMEM)
COLS = ("pair", "core")
ANY = pl.BlockSpec(memory_space=pl.ANY)
SMEM = pl.BlockSpec(memory_space=pltpu.SMEM)


def call(kernel, outs, ins, scratch=(), smem=(), far=(), flops=0, limit=16 << 20):
    moved = sum(a.size * a.dtype.itemsize for a in list(ins) + jax.tree.leaves(outs))
    return pl.pallas_call(
        kernel,
        out_shape=outs,
        in_specs=[SMEM if n in smem else ANY if n in far else VMEM for n in range(len(ins))],
        out_specs=jax.tree.map(lambda _: VMEM, outs),
        scratch_shapes=list(scratch),
        compiler_params=pltpu.CompilerParams(vmem_limit_bytes=limit),
        cost_estimate=pl.CostEstimate(
            flops=flops, bytes_accessed=moved, transcendentals=0
        ),
    )(*ins)


def shape(*dims, dtype=bf16):
    return jax.ShapeDtypeStruct(dims, dtype)


def turn(x):
    return pltpu.roll(x, 4, 1)


def lower(x):
    return lax.broadcasted_iota(jnp.int32, x.shape, 1) < 4


def fetch(copies, sem):
    started = [pltpu.make_async_copy(src, dst, sem.at[n]) for n, (src, dst) in enumerate(copies)]
    for c in started:
        c.start()
    for c in started:
        c.wait()


def block_of(ref, fac_ref, part, b, i, j, rows, features):
    factor = fac_ref[b, i, j : j + 1, part * features : (part + 1) * features]
    return ref[b, rows, 8 * j : 8 * j + 8, :].astype(f32) * factor[None]


def edge_kernel(scale_ref, k_ref, v_ref, tok_ref, fac_ref, left_ref, right_ref):
    members, height, breadth, features = k_ref.shape
    last = breadth // 8 - 1
    count = scale_ref.shape[3]
    per = 3 * features // count
    hot = (
        lax.broadcasted_iota(jnp.int32, (count, 3 * features), 0)
        == lax.broadcasted_iota(jnp.int32, (count, 3 * features), 1) // per
    ).astype(f32).astype(bf16)
    for b in range(members):
        for i in range(height // 8):
            factor = jnp.exp2(scale_ref[b, i].astype(f32)).astype(bf16)
            fac_ref[b, i] = jnp.dot(factor, hot, preferred_element_type=f32)
    half = height // 2
    for b in range(members):
        for i in range(height // 8):
            rows = slice(8 * i, 8 * i + 8)
            k0 = block_of(k_ref, fac_ref, 1, b, i, 0, rows, features)
            v0 = block_of(v_ref, fac_ref, 2, b, i, 0, rows, features)
            k1 = block_of(k_ref, fac_ref, 1, b, i, last, rows, features)
            v1 = block_of(v_ref, fac_ref, 2, b, i, last, rows, features)
            low = lower(k0)
            left_ref[b, rows] = jnp.where(low, k0, turn(v0)).astype(bf16)
            right_ref[b, rows] = jnp.where(low, turn(v1), k1).astype(bf16)
        for r in range(0, half, 4):
            here, there = slice(r, r + 4), slice(half + r, half + r + 4)
            out = slice(height + r, height + r + 4)
            x0 = tok_ref[b, here, 0:8].astype(f32)
            y0 = tok_ref[b, there, 0:8].astype(f32)
            x1 = tok_ref[b, here, breadth - 8 :].astype(f32)
            y1 = tok_ref[b, there, breadth - 8 :].astype(f32)
            low = lower(x0)
            left_ref[b, out] = jnp.where(low, x0, turn(y0)).astype(bf16)
            right_ref[b, out] = jnp.where(low, turn(y1), x1).astype(bf16)


def rims_of(left, right):
    low = lower(left)
    return jnp.where(low, right, left), turn(jnp.where(low, left, right))


def token_rims(left, right):
    low = lower(left)
    return jnp.where(low, right, left), turn(jnp.where(low, left, right))


def strip_kernel(k_ref, v_ref, tok_ref, fac_ref, fl_ref, fr_ref, up_ref, down_ref, k_buf, v_buf, t_buf, sem):
    members, height, breadth, features = k_ref.shape
    tiles, half = breadth // 8, height // 2
    copies = []
    for ref, buf in ((k_ref, k_buf), (v_ref, v_buf), (tok_ref, t_buf)):
        copies.append((ref.at[:, 0:4], buf.at[0]))
        copies.append((ref.at[:, height - 4 : height], buf.at[1]))
    fetch(copies, sem)
    for n, out in enumerate((up_ref, down_ref)):
        row = 0 if n == 0 else height - 4
        i = row // 8
        for b in range(members):
            rim_k, rim_v = rims_of(
                fl_ref[b, row : row + 4].astype(f32), fr_ref[b, row : row + 4].astype(f32)
            )
            packed = height + (row if n == 0 else row - half)
            rim_t = token_rims(
                fl_ref[b, packed : packed + 4].astype(f32), fr_ref[b, packed : packed + 4].astype(f32)
            )[n]
            for m, (buf, rim) in enumerate(((k_buf, rim_k), (v_buf, rim_v))):
                parts = [
                    buf[n, b, :, 8 * j : 8 * j + 8].astype(f32)
                    * fac_ref[b, i, j : j + 1, (m + 1) * features : (m + 2) * features][None]
                    for j in range(tiles)
                ]
                out[m, b] = jnp.concatenate(parts + [rim], 1).astype(bf16)
            out[2, b] = jnp.concatenate([t_buf[n, b].astype(f32), rim_t], 1).astype(bf16)


def prepare_kernel(crop_ref, q_ref, g_ref, fac_ref, w_ref, qs_ref, gm_ref, do_ref):
    members, height, breadth, features = q_ref.shape
    tiles = breadth // 8
    row0 = lax.axis_index("row") * height
    col0 = (lax.axis_index("pair") * 2 + lax.axis_index("core")) * breadth
    for b in range(members):
        for i in range(height // 8):
            rows = slice(8 * i, 8 * i + 8)
            parts = [block_of(q_ref, fac_ref, 0, b, i, j, rows, features) for j in range(tiles)]
            qs_ref[b, rows] = (jnp.concatenate(parts, 1) * 0.125).astype(bf16)
            g = g_ref[b, rows].astype(f32)
            r = lax.broadcasted_iota(jnp.int32, g.shape, 0) + (8 * i + row0)
            c = lax.broadcasted_iota(jnp.int32, g.shape, 1) + col0
            keep = (r >= crop_ref[b, 0]) & (c >= crop_ref[b, 1])
            gm = jnp.where(keep, g, 0.0).astype(bf16)
            gm_ref[b, rows] = gm
            do = lax.dot_general(
                gm.reshape(8 * breadth, features), w_ref[...], (((1,), (1,)), ((), ())),
                preferred_element_type=f32,
            )
            do_ref[b, rows] = do.astype(bf16).reshape(8, breadth, features)


def main_kernel(
    qs_ref, do_ref, k_ref, v_ref, fac_ref, gm_ref, tok_ref,
    fl_ref, fr_ref, top_ref, bottom_ref,
    keep_ref, send_ref, dq_ref, kv_ref,
    kt_ref, vt_ref, dkt_ref, dvt_ref, o_ref, tp_ref, all_ref,
):
    members, height, breadth, features = qs_ref.shape
    tall = height + 8
    strips, tiles = height // 8, breadth // 8
    heads_lanes = features // HEADS
    wide = GROUP * heads_lanes
    groups = HEADS // GROUP
    row0 = lax.axis_index("row") * height
    col0 = (lax.axis_index("pair") * 2 + lax.axis_index("core")) * breadth
    frame_rows = height * lax.axis_size("row")
    frame_cols = breadth * lax.axis_size("pair") * 2

    def put(ref, b, rows, blocks, rim):
        low = lower(rim)
        for t in range(tiles):
            before = rim if t == 0 else blocks[t - 1]
            after = rim if t == tiles - 1 else blocks[t + 1]
            ref[b, t, rows] = jnp.concatenate([blocks[t], jnp.where(low, after, before)], 1).astype(bf16)

    for b in range(members):
        for n, ref in enumerate((top_ref, bottom_ref)):
            halo = slice(0, 4) if n == 0 else slice(height + 4, height + 8)
            for m, out in enumerate((kt_ref, vt_ref)):
                parts = [ref[m, b, :, 8 * j : 8 * j + 8].astype(f32) for j in range(tiles + 1)]
                put(out, b, halo, parts[:tiles], parts[tiles])
            tp_ref[b, halo] = ref[2, b]
        for i in range(strips):
            rows = slice(8 * i, 8 * i + 8)
            rim_k, rim_v = rims_of(fl_ref[b, rows].astype(f32), fr_ref[b, rows].astype(f32))
            for m, (ref, out, rim) in enumerate(((k_ref, kt_ref, rim_k), (v_ref, vt_ref, rim_v))):
                blocks = [block_of(ref, fac_ref, m + 1, b, i, j, rows, features) for j in range(tiles)]
                put(out, b, slice(8 * i + 4, 8 * i + 12), blocks, rim)
        half = height // 2
        for r in range(0, half, 4):
            packed = slice(height + r, height + r + 4)
            pair = token_rims(fl_ref[b, packed].astype(f32), fr_ref[b, packed].astype(f32))
            for rim, row in zip(pair, (r, half + r)):
                own = tok_ref[b, row : row + 4].astype(f32)
                tp_ref[b, row + 4 : row + 8] = jnp.concatenate([own, rim], 1).astype(bf16)
        for t in range(tiles):
            dkt_ref[b, t, 0:8] = jnp.zeros((8, 16, features), f32)
            dvt_ref[b, t, 0:8] = jnp.zeros((8, 16, features), f32)
        dq_ref[b, 0:4] = jnp.zeros((4, breadth, features), bf16)
        dq_ref[b, tall - 4 : tall] = jnp.zeros((4, breadth, features), bf16)

    lane = lax.broadcasted_iota(jnp.int32, (1, wide), 1) // heads_lanes
    head_mask = [(lane == h).astype(f32).astype(bf16) for h in range(GROUP)]
    first = lax.broadcasted_iota(jnp.int32, (64, 2 * heads_lanes), 1) < heads_lanes

    def spread(x):
        return jnp.concatenate([x * m for m in head_mask], 0)

    def gather(x):
        parts = []
        for n in range(GROUP // 2):
            lanes = slice(128 * n, 128 * n + 128)
            parts.append(jnp.where(first, x[128 * n : 128 * n + 64, lanes], x[128 * n + 64 : 128 * n + 128, lanes]))
        return jnp.concatenate(parts, 1)

    def bias_of(i, t):
        qn = lax.broadcasted_iota(jnp.int32, (64, 256), 0)
        kn = lax.broadcasted_iota(jnp.int32, (64, 256), 1)
        qr, qc = qn // 8, qn % 8
        kr, ks = kn // 16, kn % 16
        kc = jnp.where(ks < 12, ks, ks - 16)
        row = row0 + 8 * i - 4 + kr
        col = col0 + 8 * t + kc
        ok = (kr >= qr) & (kr <= qr + 8) & (kc >= qc - 4) & (kc <= qc + 4)
        ok &= (row >= 0) & (row < frame_rows) & (col >= 0) & (col < frame_cols)
        return jnp.where(ok, 0.0, masked_score)

    across = (((1,), (1,)), ((), ()))
    down = (((0,), (0,)), ((), ()))

    def step(n, _):
        b, i = n // strips, n % strips
        rows = pl.ds(8 * i, 8)
        q8 = qs_ref[b, rows].astype(f32)
        g8 = do_ref[b, rows].astype(f32)
        outs, grads = [], []
        for t in range(tiles):
            bias4 = jnp.concatenate([bias_of(i, t)] * GROUP, 0)
            q64 = q8[:, 8 * t : 8 * t + 8].reshape(64, features).astype(bf16)
            g64 = g8[:, 8 * t : 8 * t + 8].reshape(64, features).astype(bf16)
            keys = pl.ds(8 * i, 16)
            ot, dqt = [], []
            for g in range(groups):
                lanes = slice(g * wide, (g + 1) * wide)
                qx, gx = spread(q64[:, lanes]), spread(g64[:, lanes])
                k = kt_ref[b, t, keys, :, lanes].reshape(256, wide)
                v = vt_ref[b, t, keys, :, lanes].reshape(256, wide)
                s = lax.dot_general(qx, k, across, preferred_element_type=f32) + bias4
                w = jnp.exp(s - jnp.max(s, 1, keepdims=True))
                p = w * (1.0 / jnp.sum(w, 1, keepdims=True))
                ph = p.astype(bf16)
                o = jnp.dot(ph, v, preferred_element_type=f32).astype(bf16).astype(f32)
                delta = jnp.sum(o * gx.astype(f32), 1, keepdims=True)
                dp = lax.dot_general(gx, v, across, preferred_element_type=f32)
                ds = (p * (dp - delta)).astype(bf16)
                dq = jnp.dot(ds, k, preferred_element_type=f32)
                dk = lax.dot_general(ds, qx, down, preferred_element_type=f32).reshape(16, 16, wide)
                dv = lax.dot_general(ph, gx, down, preferred_element_type=f32).reshape(16, 16, wide)
                ot.append(gather(o))
                dqt.append(gather(dq) * 0.125)
                for ref, x in ((dkt_ref, dk), (dvt_ref, dv)):
                    ref[b, t, rows, :, lanes] = ref[b, t, rows, :, lanes] + x[0:8]
                    ref[b, t, pl.ds(8 * i + 8, 8), :, lanes] = x[8:16]
            outs.append(jnp.concatenate(ot, 1).reshape(8, 8, features))
            grads.append(jnp.concatenate(dqt, 1).reshape(8, 8, features))
        o_ref[b, rows] = jnp.concatenate(outs, 1).astype(bf16)
        dq_ref[b, pl.ds(8 * i + 4, 8)] = jnp.concatenate(grads, 1).astype(bf16)
        return 0

    lax.fori_loop(0, members * strips, step, 0)

    for b in range(members):
        for r in range(0, tall, 8):
            rows = slice(r, r + 8)
            for m, ref in enumerate((dkt_ref, dvt_ref)):
                rim = [ref[b, t, rows, 8:16] for t in range(tiles)]
                low = lower(rim[0])
                own = []
                for t in range(tiles):
                    x = ref[b, t, rows, 0:8]
                    if t > 0:
                        x = x + jnp.where(low, rim[t - 1], 0.0)
                    if t < tiles - 1:
                        x = x + jnp.where(low, 0.0, rim[t + 1])
                    own.append(x)
                own.append(jnp.where(low, rim[tiles - 1], rim[0]))
                kv_ref[b, rows, :, m * features : (m + 1) * features] = jnp.concatenate(own, 1).astype(bf16)

    cells = members * height * breadth
    padded = members * tall * (breadth + 8)
    for b in range(members):
        x = lax.dot_general(
            tok_ref[b].reshape(cells // members, features),
            dq_ref[b, 4 : tall - 4].reshape(cells // members, features), down,
            preferred_element_type=f32,
        )
        y = lax.dot_general(
            o_ref[b].reshape(cells // members, features), gm_ref[b].reshape(cells // members, features), down,
            preferred_element_type=f32,
        )
        if b:
            x, y = x + all_ref[:, 0:features], y + all_ref[:, 3 * features :]
        all_ref[:, 0:features] = x
        all_ref[:, 3 * features :] = y
    kv = kv_ref[...].reshape(padded, 2 * features)
    all_ref[:, features : 3 * features] = lax.dot_general(
        tp_ref[...].reshape(padded, features), kv, down, preferred_element_type=f32
    )

    deep_rows, pairs, deep, broad = keep_ref.shape
    count = 2 * pairs
    main, rest = 3 * features // count, features // count
    lanes = lax.broadcasted_iota(jnp.int32, (features, broad), 1)

    def window(start, end):
        base, off = start // broad * broad, start % broad
        x = all_ref[:, base : base + broad]
        if off:
            x = pltpu.roll(x, broad - off, 1)
        if end > base + broad:
            y = pltpu.roll(all_ref[:, base + broad : base + 2 * broad], broad - off, 1)
            x = jnp.where(lanes < broad - off, x, y)
        return x

    def block(c):
        x = window(main * c, main * (c + 1))
        base, off = 3 * features + rest * c // broad * broad, rest * c % broad
        y = all_ref[:, base : base + broad]
        if off != main:
            y = pltpu.roll(y, (main - off) % broad, 1)
        return jnp.where(lanes < main, x, y).astype(bf16).reshape(deep_rows, deep, broad)

    mine = lax.axis_index("core") == 0
    for p in range(pairs):
        even, odd = block(2 * p), block(2 * p + 1)
        keep_ref[:, p] = jnp.where(mine, even, odd)
        send_ref[:, p] = jnp.where(mine, odd, even)


def token_kernel(kv_ref, dq_ref, w_ref, gt_ref, left_ref, right_ref):
    members, tall, breadth, features = dq_ref.shape
    across = (((1,), (1,)), ((), ()))
    middle = tall // 2
    for b in range(members):
        y = lax.dot_general(
            kv_ref[b].reshape(tall * (breadth + 8), 2 * features), w_ref[:, features:], across,
            preferred_element_type=f32,
        ).reshape(tall, breadth + 8, features)
        z = lax.dot_general(
            dq_ref[b].reshape(tall * breadth, features), w_ref[:, 0:features], across,
            preferred_element_type=f32,
        ).reshape(tall, breadth, features)
        gt_ref[b] = (y[:, 0:breadth] + z).astype(bf16)
        here, there = y[0:middle, breadth:], turn(y[middle:, breadth:])
        low = lower(here)
        right_ref[b] = jnp.where(low, here, there).astype(bf16)
        left_ref[b] = jnp.where(low, there, here).astype(bf16)


def back_rims(fl, fr):
    low = lower(fl)
    here = (jnp.where(low, fl, 0.0), jnp.where(low, 0.0, fr))
    there = (jnp.where(low, turn(fl), 0.0), jnp.where(low, 0.0, turn(fr)))
    return here, there


def plus_rims(x, rims):
    last = x.shape[1] - 8
    return jnp.concatenate([x[:, 0:8] + rims[0], x[:, 8:last], x[:, last:] + rims[1]], 1) if last > 8 else (
        jnp.concatenate([x[:, 0:8] + rims[0], x[:, 8:] + rims[1]], 1)
    )


def total_kernel(x_ref, sum_ref, square_ref):
    x = jnp.sum(x_ref[...].astype(f32), 0)
    sum_ref[...] = x
    square = jnp.sum(x * x, 0, keepdims=True)
    square_ref[...] = jnp.broadcast_to(square, square_ref.shape)


def halo_kernel(gt_ref, fl_ref, fr_ref, up_ref, down_ref):
    members, tall = gt_ref.shape[:2]
    half = tall // 2
    for b in range(members):
        here, _ = back_rims(fl_ref[b, 0:4].astype(f32), fr_ref[b, 0:4].astype(f32))
        _, there = back_rims(fl_ref[b, half - 4 : half].astype(f32), fr_ref[b, half - 4 : half].astype(f32))
        up_ref[b] = plus_rims(gt_ref[b, 0:4].astype(f32), here).astype(bf16)
        down_ref[b] = plus_rims(gt_ref[b, tall - 4 : tall].astype(f32), there).astype(bf16)


def join_kernel(gt_ref, fl_ref, fr_ref, ft_ref, fb_ref, tok_ref):
    members, height = tok_ref.shape[:2]
    half = (height + 8) // 2
    for b in range(members):
        for r in range(0, half, 4):
            pair = back_rims(fl_ref[b, r : r + 4].astype(f32), fr_ref[b, r : r + 4].astype(f32))
            for rims, row in zip(pair, (r, half + r)):
                if row == 0 or row == height + 4:
                    continue
                y = plus_rims(gt_ref[b, row : row + 4].astype(f32), rims)
                if row == 4:
                    y = y + ft_ref[b].astype(f32)
                if row == height:
                    y = y + fb_ref[b].astype(f32)
                tok_ref[b, row - 4 : row] = y.astype(bf16)


def clip_kernel(x_ref, square_ref, qkv_ref, out_ref):
    total = jnp.sum(jnp.sum(square_ref[...], 0, keepdims=True), 1, keepdims=True)
    clip = jnp.minimum(1.0, max_norm / jnp.sqrt(total + tiny_square))
    x = x_ref[...] * clip
    main = qkv_ref.shape[1]
    qkv_ref[...] = x[:, 0:main]
    out_ref[...] = x.T[main:]


def shift(x, axes, by):
    size = lax.axis_size(axes)
    return lax.ppermute(x, axes, [(i, i + by) for i in range(size) if 0 <= i + by < size])


def body(tokens, w_qkv, w_out, q_saved, k_saved, v_saved, scale_exp, grad_out, crop_start):
    members, height, breadth, features = tokens.shape
    tall = height + 8
    packed = height + height // 2
    factor, left, right = call(
        edge_kernel,
        (
            shape(*scale_exp.shape[:3], 3 * features, dtype=f32),
            shape(members, packed, 8, features),
            shape(members, packed, 8, features),
        ),
        (scale_exp, k_saved, v_saved, tokens),
    )
    from_left, from_right = shift(right, COLS, 1), shift(left, COLS, -1)
    strip = shape(3, members, 4, breadth + 8, features)
    edge_rows = pltpu.VMEM((2, members, 4, breadth, features), bf16)
    up, down = call(
        strip_kernel,
        (strip, strip),
        (k_saved, v_saved, tokens, factor, from_left, from_right),
        scratch=(edge_rows,) * 3 + (pltpu.SemaphoreType.DMA((6,)),),
        far=(0, 1, 2),
    )
    top, bottom = shift(down, "row", 1), shift(up, "row", -1)
    cells = members * height * breadth
    qs, gm, do = call(
        prepare_kernel,
        (shape(*tokens.shape),) * 3,
        (crop_start, q_saved, grad_out, factor, w_out),
        smem=(0,),
        flops=2 * cells * features * features,
    )
    rows, pairs = lax.axis_size("row"), lax.axis_size("pair")
    deep, wide = features // rows, 4 * features // (2 * pairs)
    tile_shape = (members, breadth // 8, tall, 16, features)
    keep, send, dq, kv = call(
        main_kernel,
        (
            shape(rows, pairs, deep, wide),
            shape(rows, pairs, deep, wide),
            shape(members, tall, breadth, features),
            shape(members, tall, breadth + 8, 2 * features),
        ),
        (qs, do, k_saved, v_saved, factor, gm, tokens, from_left, from_right, top, bottom),
        scratch=(
            pltpu.VMEM(tile_shape, bf16),
            pltpu.VMEM(tile_shape, bf16),
            pltpu.VMEM(tile_shape, f32),
            pltpu.VMEM(tile_shape, f32),
            pltpu.VMEM(tokens.shape, bf16),
            pltpu.VMEM((members, tall, breadth + 8, features), bf16),
            pltpu.VMEM((features, 4 * features), f32),
        ),
        flops=12 * cells * features * features,
        limit=44 << 20,
    )
    other = lax.ppermute(send, "core", [(0, 1), (1, 0)])
    both = (keep.astype(f32) + other.astype(f32)).astype(bf16).reshape(rows * pairs, deep, wide)
    parts = lax.all_to_all(both, ("row", "pair"), 0, 0, tiled=True)
    gt, left, right = call(
        token_kernel,
        (
            shape(members, tall, breadth, features),
            shape(members, tall // 2, 8, features),
            shape(members, tall // 2, 8, features),
        ),
        (kv, dq, w_qkv),
        flops=6 * cells * features * features,
        limit=24 << 20,
    )
    back_left, back_right = shift(right, COLS, 1), shift(left, COLS, -1)
    halo = shape(members, 4, breadth, features)
    up, down = call(halo_kernel, (halo, halo), (gt, back_left, back_right))
    back_top, back_bottom = shift(down, "row", 1), shift(up, "row", -1)
    grad_tokens = call(
        join_kernel, shape(*tokens.shape), (gt, back_left, back_right, back_top, back_bottom)
    )
    total, square = call(
        total_kernel,
        (shape(deep, wide, dtype=f32), shape(2 * rows * pairs, wide, dtype=f32)),
        (parts,),
    )
    squares = lax.all_to_all(square, ("row", "pair", "core"), 0, 0, tiled=True)
    main = 3 * features // (2 * pairs)
    grad_qkv, grad_w_out = call(
        clip_kernel,
        (shape(deep, main, dtype=f32), shape(wide - main, deep, dtype=f32)),
        (total, squares),
    )
    return grad_tokens, grad_qkv, grad_w_out.T


def solution(mesh):
    rows, cols = mesh.devices.shape
    split = jax.sharding.Mesh(mesh.devices.reshape(rows, cols // 2, 2), ("row",) + COLS)
    cells = P(None, "row", COLS, None)
    return jax.shard_map(
        body,
        mesh=split,
        in_specs=(cells, P(), P(), cells, cells, cells, cells, cells, P()),
        out_specs=(cells, P("row", COLS), P("row", COLS)),
        check_vma=False,
    )
```

```python
import jax
import jax.numpy as jnp
from jax import lax
from jax.experimental import pallas as pl
from jax.experimental.pallas import tpu as pltpu
from jax.sharding import PartitionSpec as P

HEADS = 8
RADIUS = 4
BLOCK = 8
GROUP = 4

max_norm = 1000.0
masked_score = -1e30
tiny_square = 1e-06

f32 = jnp.float32
bf16 = jnp.bfloat16
VMEM = pl.BlockSpec(memory_space=pltpu.VMEM)
COLS = ("pair", "core")
ANY = pl.BlockSpec(memory_space=pltpu.HBM)
SMEM = pl.BlockSpec(memory_space=pltpu.SMEM)


def call(kernel, outs, ins, scratch=(), smem=(), far=(), far_outs=(), flops=0, limit=16 << 20):
    moved = sum(a.size * a.dtype.itemsize for a in list(ins) + jax.tree.leaves(outs))
    return pl.pallas_call(
        kernel,
        out_shape=outs,
        in_specs=[SMEM if n in smem else ANY if n in far else VMEM for n in range(len(ins))],
        out_specs=tuple(ANY if n in far_outs else VMEM for n in range(len(outs))) if isinstance(outs, tuple) else VMEM,
        scratch_shapes=list(scratch),
        compiler_params=pltpu.CompilerParams(vmem_limit_bytes=limit),
        cost_estimate=pl.CostEstimate(
            flops=flops, bytes_accessed=moved, transcendentals=0
        ),
    )(*ins)


def shape(*dims, dtype=bf16):
    return jax.ShapeDtypeStruct(dims, dtype)


def turn(x):
    return pltpu.roll(x, 4, 1)


def lower(x):
    return lax.broadcasted_iota(jnp.int32, x.shape, 1) < 4


def block_of(ref, fac_ref, part, b, i, j, rows, features):
    factor = fac_ref[b, i, j : j + 1, part * features : (part + 1) * features]
    return ref[b, rows, 8 * j : 8 * j + 8, :].astype(f32) * factor[None]


def edge_kernel(
    scale_ref, k_ref, v_ref, tok_ref, fac_ref, left_ref, right_ref, up_ref, down_ref, k_buf, v_buf, t_buf, sem
):
    members, height, breadth, features = k_ref.shape
    tiles = breadth // 8
    copies = [
        pltpu.make_async_copy(src, dst, sem.at[n])
        for n, (src, dst) in enumerate(((k_ref, k_buf), (v_ref, v_buf), (tok_ref, t_buf)))
    ]
    for c in copies:
        c.start()
    count = scale_ref.shape[3]
    per = 3 * features // count
    hot = (
        lax.broadcasted_iota(jnp.int32, (count, 3 * features), 0)
        == lax.broadcasted_iota(jnp.int32, (count, 3 * features), 1) // per
    ).astype(f32).astype(bf16)
    for b in range(members):
        for i in range(height // 8):
            factor = jnp.exp2(scale_ref[b, i].astype(f32)).astype(bf16)
            fac_ref[b, i] = jnp.dot(factor, hot, preferred_element_type=f32)
    for c in copies:
        c.wait()
    half = height // 2
    for b in range(members):
        for i in range(height // 8):
            rows = slice(8 * i, 8 * i + 8)
            k = [block_of(k_buf, fac_ref, 1, b, i, j, rows, features) for j in range(tiles)]
            v = [block_of(v_buf, fac_ref, 2, b, i, j, rows, features) for j in range(tiles)]
            low = lower(k[0])
            left_ref[b, rows] = jnp.where(low, k[0], turn(v[0])).astype(bf16)
            right_ref[b, rows] = jnp.where(low, turn(v[-1]), k[-1]).astype(bf16)
            for m, parts in enumerate((k, v)):
                x = jnp.concatenate(parts, 1).astype(bf16)
                if i == 0:
                    up_ref[m, b] = x[0:4]
                if i == height // 8 - 1:
                    down_ref[m, b] = x[4:8]
        up_ref[2, b] = t_buf[b, 0:4]
        down_ref[2, b] = t_buf[b, height - 4 : height]
        for r in range(0, half, 4):
            here, there = slice(r, r + 4), slice(half + r, half + r + 4)
            out = slice(height + r, height + r + 4)
            pack_columns(t_buf.at[b, here], t_buf.at[b, there], left_ref.at[b, out], right_ref.at[b, out])


def pack_columns(one_ref, two_ref, left_ref, right_ref):
    last = one_ref.shape[1] - 8
    x0, y0 = one_ref[:, 0:8].astype(f32), two_ref[:, 0:8].astype(f32)
    x1, y1 = one_ref[:, last:].astype(f32), two_ref[:, last:].astype(f32)
    low = lower(x0)
    left_ref[...] = jnp.where(low, x0, turn(y0)).astype(bf16)
    right_ref[...] = jnp.where(low, turn(y1), x1).astype(bf16)


def corner_kernel(top_ref, bottom_ref, left_ref, right_ref):
    for b in range(top_ref.shape[1]):
        for n, (one, two) in enumerate(
            (
                (top_ref.at[0, b], top_ref.at[1, b]),
                (bottom_ref.at[0, b], bottom_ref.at[1, b]),
                (top_ref.at[2, b], bottom_ref.at[2, b]),
            )
        ):
            out = slice(4 * n, 4 * n + 4)
            pack_columns(one, two, left_ref.at[b, out], right_ref.at[b, out])


def rims_of(left_ref, right_ref, b, rows):
    left, right = left_ref[b, rows].astype(f32), right_ref[b, rows].astype(f32)
    low = lower(left)
    return jnp.where(low, right, left), turn(jnp.where(low, left, right))


def prepare_kernel(crop_ref, q_ref, g_ref, fac_ref, w_ref, qs_ref, gm_ref, do_ref):
    members, height, breadth, features = q_ref.shape
    tiles = breadth // 8
    row0 = lax.axis_index("row") * height
    col0 = (lax.axis_index("pair") * 2 + lax.axis_index("core")) * breadth
    for b in range(members):
        for i in range(height // 8):
            rows = slice(8 * i, 8 * i + 8)
            parts = [block_of(q_ref, fac_ref, 0, b, i, j, rows, features) for j in range(tiles)]
            qs_ref[b, rows] = (jnp.concatenate(parts, 1) * 0.125).astype(bf16)
            g = g_ref[b, rows].astype(f32)
            r = lax.broadcasted_iota(jnp.int32, g.shape, 0) + (8 * i + row0)
            c = lax.broadcasted_iota(jnp.int32, g.shape, 1) + col0
            keep = (r >= crop_ref[b, 0]) & (c >= crop_ref[b, 1])
            gm = jnp.where(keep, g, 0.0).astype(bf16)
            gm_ref[b, rows] = gm
            do = lax.dot_general(
                gm.reshape(8 * breadth, features), w_ref[...], (((1,), (1,)), ((), ())),
                preferred_element_type=f32,
            )
            do_ref[b, rows] = do.astype(bf16).reshape(8, breadth, features)


def key_tile(blocks, rim, t):
    low = lower(rim)
    before = rim if t == 0 else blocks[t - 1]
    after = rim if t == len(blocks) - 1 else blocks[t + 1]
    return jnp.concatenate([blocks[t], jnp.where(low, after, before)], 1).astype(bf16)


def place_of(height, breadth):
    row0 = lax.axis_index("row") * height
    col0 = (lax.axis_index("pair") * 2 + lax.axis_index("core")) * breadth
    return row0, col0, height * lax.axis_size("row"), breadth * lax.axis_size("pair") * 2


def attend(q, g, keys_of, i, place, emit):
    features = q.shape[2]
    head_lanes = features // HEADS
    wide = GROUP * head_lanes
    row0, col0, frame_rows, frame_cols = place
    lane = lax.broadcasted_iota(jnp.int32, (1, wide), 1) // head_lanes
    head_mask = [(lane == h).astype(f32).astype(bf16) for h in range(GROUP)]
    first = lax.broadcasted_iota(jnp.int32, (64, 2 * head_lanes), 1) < head_lanes
    across = (((1,), (1,)), ((), ()))
    down = (((0,), (0,)), ((), ()))

    def spread(x):
        return jnp.concatenate([x * m for m in head_mask], 0)

    def gather(x):
        parts = []
        for n in range(GROUP // 2):
            lanes = slice(128 * n, 128 * n + 128)
            parts.append(jnp.where(first, x[128 * n : 128 * n + 64, lanes], x[128 * n + 64 : 128 * n + 128, lanes]))
        return jnp.concatenate(parts, 1)

    outs, grads = [], []
    for t in range(q.shape[1] // 8):
        qn = lax.broadcasted_iota(jnp.int32, (64, 256), 0)
        kn = lax.broadcasted_iota(jnp.int32, (64, 256), 1)
        qr, qc = qn // 8, qn % 8
        kr, ks = kn // 16, kn % 16
        kc = jnp.where(ks < 12, ks, ks - 16)
        row = row0 + 8 * i - 4 + kr
        col = col0 + 8 * t + kc
        ok = (kr >= qr) & (kr <= qr + 8) & (kc >= qc - 4) & (kc <= qc + 4)
        ok &= (row >= 0) & (row < frame_rows) & (col >= 0) & (col < frame_cols)
        bias = jnp.concatenate([jnp.where(ok, 0.0, masked_score)] * GROUP, 0)
        q64 = q[:, 8 * t : 8 * t + 8].reshape(64, features).astype(bf16)
        g64 = g[:, 8 * t : 8 * t + 8].reshape(64, features).astype(bf16)
        ot, dqt = [], []
        for lanes in [slice(n * wide, (n + 1) * wide) for n in range(HEADS // GROUP)]:
            qx, gx = spread(q64[:, lanes]), spread(g64[:, lanes])
            k, v = keys_of(t, lanes)
            s = lax.dot_general(qx, k, across, preferred_element_type=f32) + bias
            w = jnp.exp(s - jnp.max(s, 1, keepdims=True))
            p = w * (1.0 / jnp.sum(w, 1, keepdims=True))
            ph = p.astype(bf16)
            o = jnp.dot(ph, v, preferred_element_type=f32).astype(bf16).astype(f32)
            delta = jnp.sum(o * gx.astype(f32), 1, keepdims=True)
            dp = lax.dot_general(gx, v, across, preferred_element_type=f32)
            ds = (p * (dp - delta)).astype(bf16)
            dq = jnp.dot(ds, k, preferred_element_type=f32)
            dk = lax.dot_general(ds, qx, down, preferred_element_type=f32).reshape(16, 16, wide)
            dv = lax.dot_general(ph, gx, down, preferred_element_type=f32).reshape(16, 16, wide)
            ot.append(gather(o))
            dqt.append(gather(dq) * 0.125)
            emit(t, lanes, dk, dv)
        outs.append(jnp.concatenate(ot, 1).reshape(8, 8, features))
        grads.append(jnp.concatenate(dqt, 1).reshape(8, 8, features))
    return jnp.concatenate(outs, 1), jnp.concatenate(grads, 1)


def middle_kernel(
    qs_ref, do_ref, k_ref, v_ref, fac_ref, fl_ref, fr_ref, kt_ref, vt_ref, dk_ref, dv_ref, o_ref, dq_ref
):
    members, height, breadth, features = qs_ref.shape
    strips, tiles = height // 8, breadth // 8
    place = place_of(height, breadth)
    for b in range(members):
        for i in range(strips):
            rows = slice(8 * i, 8 * i + 8)
            rims = rims_of(fl_ref, fr_ref, b, rows)
            for m, (ref, out) in enumerate(((k_ref, kt_ref), (v_ref, vt_ref))):
                blocks = [block_of(ref, fac_ref, m + 1, b, i, j, rows, features) for j in range(tiles)]
                for t in range(tiles):
                    out[b, t, rows] = key_tile(blocks, rims[m], t)

    def step(b, _):
        def keys_of(t, lanes):
            return tuple(ref[b, t, 4:20, :, lanes].reshape(256, -1) for ref in (kt_ref, vt_ref))

        def emit(t, lanes, dk, dv):
            dk_ref[b, t, :, :, lanes] = dk
            dv_ref[b, t, :, :, lanes] = dv

        o, dq = attend(qs_ref[b, 8:16].astype(f32), do_ref[b, 8:16].astype(f32), keys_of, 1, place, emit)
        o_ref[b] = o.astype(bf16)
        dq_ref[b] = dq.astype(bf16)
        return 0

    lax.fori_loop(0, members, step, 0)


def main_kernel(
    qs_ref, do_ref, kt_ref, vt_ref, dkm_ref, dvm_ref, om_ref, dqm_ref, gm_ref, tok_ref,
    fl_ref, fr_ref, top_ref, bottom_ref, cl_ref, cr_ref,
    keep_ref, send_ref, dq_out, kv_out,
    kh_ref, vh_ref, dkt_ref, dvt_ref, o_ref, tp_ref, all_ref, dq_ref, kv_ref, sem,
):
    members, height, breadth, features = qs_ref.shape
    tall = height + 8
    tiles = breadth // 8
    place = place_of(height, breadth)
    for b in range(members):
        token_rims = rims_of(cl_ref, cr_ref, b, slice(8, 12))
        for n, ref in enumerate((top_ref, bottom_ref)):
            rims = rims_of(cl_ref, cr_ref, b, slice(4 * n, 4 * n + 4))
            for m, out in enumerate((kh_ref, vh_ref)):
                blocks = [ref[m, b, :, 8 * j : 8 * j + 8].astype(f32) for j in range(tiles)]
                for t in range(tiles):
                    out[n, b, t] = key_tile(blocks, rims[m], t)
            halo = slice(0, 4) if n == 0 else slice(tall - 4, tall)
            tp_ref[b, halo] = jnp.concatenate([ref[2, b].astype(f32), token_rims[n]], 1).astype(bf16)
            dq_ref[b, halo] = jnp.zeros((4, breadth, features), bf16)
        half = height // 2
        for r in range(0, half, 4):
            pair = rims_of(fl_ref, fr_ref, b, slice(height + r, height + r + 4))
            for rim, row in zip(pair, (r, half + r)):
                own = tok_ref[b, row : row + 4].astype(f32)
                tp_ref[b, row + 4 : row + 8] = jnp.concatenate([own, rim], 1).astype(bf16)
        o_ref[b, 8:16] = om_ref[b]
        dq_ref[b, 12:20] = dqm_ref[b]

    def step(b, _):
        for n, i in enumerate((0, height // 8 - 1)):
            def keys_of(t, lanes):
                parts = []
                for ref, halo in ((kt_ref, kh_ref), (vt_ref, vh_ref)):
                    rim = halo[n, b, t, :, :, lanes]
                    own = ref[b, t, slice(0, 12) if n == 0 else slice(height - 12, height), :, lanes]
                    both = [rim, own] if n == 0 else [own, rim]
                    parts.append(jnp.concatenate(both, 0).reshape(256, -1))
                return tuple(parts)

            def emit(t, lanes, dk, dv):
                for ref, mid, x in ((dkt_ref, dkm_ref, dk), (dvt_ref, dvm_ref, dv)):
                    if n == 0:
                        ref[b, t, 0:8, :, lanes] = x[0:8]
                        ref[b, t, 8:16, :, lanes] = x[8:16] + mid[b, t, 0:8, :, lanes]
                    else:
                        ref[b, t, 16:24, :, lanes] = x[0:8] + mid[b, t, 8:16, :, lanes]
                        ref[b, t, 24:32, :, lanes] = x[8:16]

            rows = slice(8 * i, 8 * i + 8)
            o, dq = attend(qs_ref[b, rows].astype(f32), do_ref[b, rows].astype(f32), keys_of, i, place, emit)
            o_ref[b, rows] = o.astype(bf16)
            dq_ref[b, 8 * i + 4 : 8 * i + 12] = dq.astype(bf16)
        return 0

    lax.fori_loop(0, members, step, 0)

    for b in range(members):
        for r in range(0, tall, 8):
            rows = slice(r, r + 8)
            for m, ref in enumerate((dkt_ref, dvt_ref)):
                rim = [ref[b, t, rows, 8:16] for t in range(tiles)]
                low = lower(rim[0])
                own = []
                for t in range(tiles):
                    x = ref[b, t, rows, 0:8]
                    if t > 0:
                        x = x + jnp.where(low, rim[t - 1], 0.0)
                    if t < tiles - 1:
                        x = x + jnp.where(low, 0.0, rim[t + 1])
                    own.append(x)
                own.append(jnp.where(low, rim[tiles - 1], rim[0]))
                kv_ref[b, rows, :, m * features : (m + 1) * features] = jnp.concatenate(own, 1).astype(bf16)

    copies = [
        pltpu.make_async_copy(src, dst, sem.at[n])
        for n, (src, dst) in enumerate(((dq_ref, dq_out), (kv_ref, kv_out)))
    ]
    for c in copies:
        c.start()
    down = (((0,), (0,)), ((), ()))
    cells = members * height * breadth
    padded = members * tall * (breadth + 8)
    for b in range(members):
        x = lax.dot_general(
            tok_ref[b].reshape(cells // members, features),
            dq_ref[b, 4 : tall - 4].reshape(cells // members, features), down,
            preferred_element_type=f32,
        )
        y = lax.dot_general(
            o_ref[b].reshape(cells // members, features), gm_ref[b].reshape(cells // members, features), down,
            preferred_element_type=f32,
        )
        if b:
            x, y = x + all_ref[:, 0:features], y + all_ref[:, 3 * features :]
        all_ref[:, 0:features] = x
        all_ref[:, 3 * features :] = y
    kv = kv_ref[...].reshape(padded, 2 * features)
    all_ref[:, features : 3 * features] = lax.dot_general(
        tp_ref[...].reshape(padded, features), kv, down, preferred_element_type=f32
    )

    deep_rows, pairs, deep, broad = keep_ref.shape
    count = 2 * pairs
    main, rest = 3 * features // count, features // count
    lanes = lax.broadcasted_iota(jnp.int32, (features, broad), 1)

    def window(start, end):
        base, off = start // broad * broad, start % broad
        x = all_ref[:, base : base + broad]
        if off:
            x = pltpu.roll(x, broad - off, 1)
        if end > base + broad:
            y = pltpu.roll(all_ref[:, base + broad : base + 2 * broad], broad - off, 1)
            x = jnp.where(lanes < broad - off, x, y)
        return x

    def block(c):
        x = window(main * c, main * (c + 1))
        base, off = 3 * features + rest * c // broad * broad, rest * c % broad
        y = all_ref[:, base : base + broad]
        if off != main:
            y = pltpu.roll(y, (main - off) % broad, 1)
        return jnp.where(lanes < main, x, y).astype(bf16).reshape(deep_rows, deep, broad)

    mine = lax.axis_index("core") == 0
    for p in range(pairs):
        even, odd = block(2 * p), block(2 * p + 1)
        keep_ref[:, p] = jnp.where(mine, even, odd)
        send_ref[:, p] = jnp.where(mine, odd, even)
    for c in copies:
        c.wait()


def token_kernel(kv_ref, dq_ref, w_ref, gt_ref, left_ref, right_ref):
    members, tall, breadth, features = dq_ref.shape
    across = (((1,), (1,)), ((), ()))
    middle = tall // 2
    for b in range(members):
        y = lax.dot_general(
            kv_ref[b].reshape(tall * (breadth + 8), 2 * features), w_ref[:, features:], across,
            preferred_element_type=f32,
        ).reshape(tall, breadth + 8, features)
        z = lax.dot_general(
            dq_ref[b].reshape(tall * breadth, features), w_ref[:, 0:features], across,
            preferred_element_type=f32,
        ).reshape(tall, breadth, features)
        gt_ref[b] = (y[:, 0:breadth] + z).astype(bf16)
        here, there = y[0:middle, breadth:], turn(y[middle:, breadth:])
        low = lower(here)
        right_ref[b] = jnp.where(low, here, there).astype(bf16)
        left_ref[b] = jnp.where(low, there, here).astype(bf16)


def back_rims(fl, fr):
    low = lower(fl)
    here = (jnp.where(low, fl, 0.0), jnp.where(low, 0.0, fr))
    there = (jnp.where(low, turn(fl), 0.0), jnp.where(low, 0.0, turn(fr)))
    return here, there


def plus_rims(x, rims):
    last = x.shape[1] - 8
    return jnp.concatenate([x[:, 0:8] + rims[0], x[:, 8:last], x[:, last:] + rims[1]], 1) if last > 8 else (
        jnp.concatenate([x[:, 0:8] + rims[0], x[:, 8:] + rims[1]], 1)
    )


def add_kernel(x_ref, y_ref, sum_ref):
    sum_ref[...] = (x_ref[...].astype(f32) + y_ref[...].astype(f32)).astype(bf16)


def total_kernel(x_ref, sum_ref, square_ref):
    x = jnp.sum(x_ref[...].astype(f32), 0)
    sum_ref[...] = x
    square = jnp.sum(x * x, 0, keepdims=True)
    square_ref[...] = jnp.broadcast_to(square, square_ref.shape)


def halo_kernel(gt_ref, fl_ref, fr_ref, up_ref, down_ref):
    members, tall = gt_ref.shape[:2]
    half = tall // 2
    for b in range(members):
        here, _ = back_rims(fl_ref[b, 0:4].astype(f32), fr_ref[b, 0:4].astype(f32))
        _, there = back_rims(fl_ref[b, half - 4 : half].astype(f32), fr_ref[b, half - 4 : half].astype(f32))
        up_ref[b] = plus_rims(gt_ref[b, 0:4].astype(f32), here).astype(bf16)
        down_ref[b] = plus_rims(gt_ref[b, tall - 4 : tall].astype(f32), there).astype(bf16)


def join_kernel(gt_ref, fl_ref, fr_ref, ft_ref, fb_ref, tok_ref):
    members, height = tok_ref.shape[:2]
    half = (height + 8) // 2
    for b in range(members):
        for r in range(0, half, 4):
            pair = back_rims(fl_ref[b, r : r + 4].astype(f32), fr_ref[b, r : r + 4].astype(f32))
            for rims, row in zip(pair, (r, half + r)):
                if row == 0 or row == height + 4:
                    continue
                y = plus_rims(gt_ref[b, row : row + 4].astype(f32), rims)
                if row == 4:
                    y = y + ft_ref[b].astype(f32)
                if row == height:
                    y = y + fb_ref[b].astype(f32)
                tok_ref[b, row - 4 : row] = y.astype(bf16)


def clip_kernel(x_ref, square_ref, qkv_ref, out_ref):
    total = jnp.sum(jnp.sum(square_ref[...], 0, keepdims=True), 1, keepdims=True)
    clip = jnp.minimum(1.0, max_norm / jnp.sqrt(total + tiny_square))
    x = x_ref[...] * clip
    main = qkv_ref.shape[1]
    qkv_ref[...] = x[:, 0:main]
    out_ref[...] = x.T[main:]


def shift(x, axes, by):
    size = lax.axis_size(axes)
    return lax.ppermute(x, axes, [(i, i + by) for i in range(size) if 0 <= i + by < size])


def body(tokens, w_qkv, w_out, q_saved, k_saved, v_saved, scale_exp, grad_out, crop_start):
    members, height, breadth, features = tokens.shape
    tall = height + 8
    packed = height + height // 2
    packed_columns = shape(members, packed, 8, features)
    strip = shape(3, members, 4, breadth, features)
    factor, left, right, up, down = call(
        edge_kernel,
        (
            shape(*scale_exp.shape[:3], 3 * features, dtype=f32),
            packed_columns, packed_columns, strip, strip,
        ),
        (scale_exp, k_saved, v_saved, tokens),
        scratch=(pltpu.VMEM(tokens.shape, bf16),) * 3 + (pltpu.SemaphoreType.DMA((3,)),),
        far=(1, 2, 3),
        limit=58 << 20,
    )
    top, bottom = shift(down, "row", 1), shift(up, "row", -1)
    from_left, from_right = shift(right, COLS, 1), shift(left, COLS, -1)
    cells = members * height * breadth
    qs, gm, do = call(
        prepare_kernel,
        (shape(*tokens.shape),) * 3,
        (crop_start, q_saved, grad_out, factor, w_out),
        smem=(0,),
        flops=2 * cells * features * features,
    )
    corner = shape(members, 12, 8, features)
    top, bottom, do = lax.optimization_barrier((top, bottom, do))
    left, right = call(corner_kernel, (corner, corner), (top, bottom))
    corner_left, corner_right = shift(right, COLS, 1), shift(left, COLS, -1)
    tiles = breadth // 8
    own_tiles = shape(members, tiles, height, 16, features)
    middle_tiles = shape(members, tiles, 16, 16, features, dtype=f32)
    middle_rows = shape(members, 8, breadth, features)
    kt, vt, dk, dv, out, dq = call(
        middle_kernel,
        (own_tiles, own_tiles, middle_tiles, middle_tiles, middle_rows, middle_rows),
        (qs, do, k_saved, v_saved, factor, from_left, from_right),
        flops=4 * cells * features * features,
        limit=20 << 20,
    )
    rows, pairs = lax.axis_size("row"), lax.axis_size("pair")
    deep, wide = features // rows, 4 * features // (2 * pairs)
    halo_tiles = pltpu.VMEM((2, members, tiles, 4, 16, features), bf16)
    all_tiles = pltpu.VMEM((members, tiles, tall, 16, features), f32)
    keep, send, dq, kv = call(
        main_kernel,
        (
            shape(rows, pairs, deep, wide),
            shape(rows, pairs, deep, wide),
            shape(members, tall, breadth, features),
            shape(members, tall, breadth + 8, 2 * features),
        ),
        (
            qs, do, kt, vt, dk, dv, out, dq, gm, tokens,
            from_left, from_right, top, bottom, corner_left, corner_right,
        ),
        scratch=(
            halo_tiles, halo_tiles, all_tiles, all_tiles,
            pltpu.VMEM(tokens.shape, bf16),
            pltpu.VMEM((members, tall, breadth + 8, features), bf16),
            pltpu.VMEM((features, 4 * features), f32),
            pltpu.VMEM((members, tall, breadth, features), bf16),
            pltpu.VMEM((members, tall, breadth + 8, 2 * features), bf16),
            pltpu.SemaphoreType.DMA((2,)),
        ),
        far_outs=(2, 3),
        flops=12 * cells * features * features,
        limit=37 << 20,
    )
    other = lax.ppermute(send, "core", [(0, 1), (1, 0)])
    both = call(add_kernel, shape(rows, pairs, deep, wide), (keep, other)).reshape(rows * pairs, deep, wide)
    parts = lax.all_to_all(both, ("row", "pair"), 0, 0, tiled=True)
    gt, left, right = call(
        token_kernel,
        (
            shape(members, tall, breadth, features),
            shape(members, tall // 2, 8, features),
            shape(members, tall // 2, 8, features),
        ),
        (kv, dq, w_qkv),
        flops=6 * cells * features * features,
        limit=20 << 20,
    )
    back_left, back_right = shift(right, COLS, 1), shift(left, COLS, -1)
    halo = shape(members, 4, breadth, features)
    up, down = call(halo_kernel, (halo, halo), (gt, back_left, back_right))
    back_top, back_bottom = shift(down, "row", 1), shift(up, "row", -1)
    grad_tokens = call(
        join_kernel, shape(*tokens.shape), (gt, back_left, back_right, back_top, back_bottom)
    )
    total, square = call(
        total_kernel,
        (shape(deep, wide, dtype=f32), shape(2 * rows * pairs, wide, dtype=f32)),
        (parts,),
    )
    squares = lax.all_to_all(square, ("row", "pair", "core"), 0, 0, tiled=True)
    main = 3 * features // (2 * pairs)
    grad_qkv, grad_w_out = call(
        clip_kernel,
        (shape(deep, main, dtype=f32), shape(wide - main, deep, dtype=f32)),
        (total, squares),
    )
    return grad_tokens, grad_qkv, grad_w_out.T


def solution(mesh):
    rows, cols = mesh.devices.shape
    split = jax.sharding.Mesh(mesh.devices.reshape(rows, cols // 2, 2), ("row",) + COLS)
    cells = P(None, "row", COLS, None)
    return jax.shard_map(
        body,
        mesh=split,
        in_specs=(cells, P(), P(), cells, cells, cells, cells, cells, P()),
        out_specs=(cells, P("row", COLS), P("row", COLS)),
        check_vma=False,
    )
```

```python
import jax
import jax.numpy as jnp
from jax import lax
from jax.experimental import pallas as pl
from jax.experimental.pallas import tpu as pltpu
from jax.sharding import PartitionSpec as P

HEADS = 8
RADIUS = 4
BLOCK = 8
GROUP = 4

max_norm = 1000.0
masked_score = -1e30
tiny_square = 1e-06

f32 = jnp.float32
bf16 = jnp.bfloat16
VMEM = pl.BlockSpec(memory_space=pltpu.VMEM)
COLS = ("pair", "core")
ANY = pl.BlockSpec(memory_space=pltpu.HBM)
SMEM = pl.BlockSpec(memory_space=pltpu.SMEM)


def call(kernel, outs, ins, scratch=(), smem=(), far=(), far_outs=(), flops=0, limit=16 << 20):
    moved = sum(a.size * a.dtype.itemsize for a in list(ins) + jax.tree.leaves(outs))
    return pl.pallas_call(
        kernel,
        out_shape=outs,
        in_specs=[SMEM if n in smem else ANY if n in far else VMEM for n in range(len(ins))],
        out_specs=tuple(ANY if n in far_outs else VMEM for n in range(len(outs))) if isinstance(outs, tuple) else VMEM,
        scratch_shapes=list(scratch),
        compiler_params=pltpu.CompilerParams(vmem_limit_bytes=limit),
        cost_estimate=pl.CostEstimate(
            flops=flops, bytes_accessed=moved, transcendentals=0
        ),
    )(*ins)


def shape(*dims, dtype=bf16):
    return jax.ShapeDtypeStruct(dims, dtype)


def turn(x):
    return pltpu.roll(x, 4, 1)


def lower(x):
    return lax.broadcasted_iota(jnp.int32, x.shape, 1) < 4


def block_of(ref, fac_ref, part, b, i, j, rows, features):
    factor = fac_ref[b, i, j : j + 1, part * features : (part + 1) * features]
    return ref[b, rows, 8 * j : 8 * j + 8, :].astype(f32) * factor[None]


def edge_kernel(
    scale_ref, k_ref, v_ref, tok_ref, fac_ref, up_ref, down_ref, left_ref, right_ref, k_buf, v_buf, t_buf, sem
):
    members, height, breadth, features = k_ref.shape
    tiles = breadth // 8
    copies = [
        pltpu.make_async_copy(src, dst, sem.at[n])
        for n, (src, dst) in enumerate(((k_ref, k_buf), (v_ref, v_buf), (tok_ref, t_buf)))
    ]
    for c in copies:
        c.start()
    count = scale_ref.shape[3]
    per = 3 * features // count
    hot = (
        lax.broadcasted_iota(jnp.int32, (count, 3 * features), 0)
        == lax.broadcasted_iota(jnp.int32, (count, 3 * features), 1) // per
    ).astype(f32).astype(bf16)
    for b in range(members):
        for i in range(height // 8):
            factor = jnp.exp2(scale_ref[b, i].astype(f32)).astype(bf16)
            fac_ref[b, i] = jnp.dot(factor, hot, preferred_element_type=f32)
    for c in copies:
        c.wait()
    half = height // 2
    for b in range(members):
        for i in range(height // 8):
            rows = slice(8 * i, 8 * i + 8)
            k = [block_of(k_buf, fac_ref, 1, b, i, j, rows, features) for j in range(tiles)]
            v = [block_of(v_buf, fac_ref, 2, b, i, j, rows, features) for j in range(tiles)]
            low = lower(k[0])
            left_ref[b, rows] = jnp.where(low, k[0], turn(v[0])).astype(bf16)
            right_ref[b, rows] = jnp.where(low, turn(v[-1]), k[-1]).astype(bf16)
            for m, parts in enumerate((k, v)):
                x = jnp.concatenate(parts, 1).astype(bf16)
                if i == 0:
                    up_ref[m, b] = x[0:4]
                if i == height // 8 - 1:
                    down_ref[m, b] = x[4:8]
        up_ref[2, b] = t_buf[b, 0:4]
        down_ref[2, b] = t_buf[b, height - 4 : height]
        for r in range(0, half, 4):
            here, there = slice(r, r + 4), slice(half + r, half + r + 4)
            out = slice(height + r, height + r + 4)
            pack_columns(t_buf.at[b, here], t_buf.at[b, there], left_ref.at[b, out], right_ref.at[b, out])


def pack_columns(one_ref, two_ref, left_ref, right_ref):
    last = one_ref.shape[1] - 8
    x0, y0 = one_ref[:, 0:8].astype(f32), two_ref[:, 0:8].astype(f32)
    x1, y1 = one_ref[:, last:].astype(f32), two_ref[:, last:].astype(f32)
    low = lower(x0)
    left_ref[...] = jnp.where(low, x0, turn(y0)).astype(bf16)
    right_ref[...] = jnp.where(low, turn(y1), x1).astype(bf16)


def corner_kernel(fl_ref, fr_ref, up_ref, down_ref):
    members, packed = fl_ref.shape[:2]
    height = packed * 2 // 3
    half = height // 2
    for b in range(members):
        for n, (out, row) in enumerate(((up_ref, 0), (down_ref, height - 4))):
            k, v = rims_of(fl_ref, fr_ref, b, slice(row, row + 4))
            first = height + (row if n == 0 else row - half)
            t = rims_of(fl_ref, fr_ref, b, slice(first, first + 4))[n]
            out[b] = jnp.concatenate([k, v, t], 0).astype(bf16)


def rims_of(left_ref, right_ref, b, rows):
    left, right = left_ref[b, rows].astype(f32), right_ref[b, rows].astype(f32)
    low = lower(left)
    return jnp.where(low, right, left), turn(jnp.where(low, left, right))


def prepare_kernel(crop_ref, q_ref, g_ref, fac_ref, w_ref, qs_ref, gm_ref, do_ref):
    members, height, breadth, features = q_ref.shape
    tiles = breadth // 8
    row0 = lax.axis_index("row") * height
    col0 = (lax.axis_index("pair") * 2 + lax.axis_index("core")) * breadth
    for b in range(members):
        for i in range(height // 8):
            rows = slice(8 * i, 8 * i + 8)
            parts = [block_of(q_ref, fac_ref, 0, b, i, j, rows, features) for j in range(tiles)]
            qs_ref[b, rows] = (jnp.concatenate(parts, 1) * 0.125).astype(bf16)
            g = g_ref[b, rows].astype(f32)
            r = lax.broadcasted_iota(jnp.int32, g.shape, 0) + (8 * i + row0)
            c = lax.broadcasted_iota(jnp.int32, g.shape, 1) + col0
            keep = (r >= crop_ref[b, 0]) & (c >= crop_ref[b, 1])
            gm = jnp.where(keep, g, 0.0).astype(bf16)
            gm_ref[b, rows] = gm
            do = lax.dot_general(
                gm.reshape(8 * breadth, features), w_ref[...], (((1,), (1,)), ((), ())),
                preferred_element_type=f32,
            )
            do_ref[b, rows] = do.astype(bf16).reshape(8, breadth, features)


def key_tile(blocks, rim, t):
    low = lower(rim)
    before = rim if t == 0 else blocks[t - 1]
    after = rim if t == len(blocks) - 1 else blocks[t + 1]
    return jnp.concatenate([blocks[t], jnp.where(low, after, before)], 1).astype(bf16)


def place_of(height, breadth):
    row0 = lax.axis_index("row") * height
    col0 = (lax.axis_index("pair") * 2 + lax.axis_index("core")) * breadth
    return row0, col0, height * lax.axis_size("row"), breadth * lax.axis_size("pair") * 2


def mask_biases(bias_ref, strips, tiles, place):
    row0, col0, frame_rows, frame_cols = place
    wide = bias_ref.shape[2]

    def key_cell(n):
        kn = lax.broadcasted_iota(jnp.int32, (256, n), 0)
        ks = kn % 16
        return kn // 16, jnp.where(ks < 12, ks, ks - 16)

    kr, kc = key_cell(wide)
    qn = lax.broadcasted_iota(jnp.int32, (256, wide), 1) % 64
    qr, qc = qn // 8, qn % 8
    seen = (kr >= qr) & (kr <= qr + 8) & (kc >= qc - 4) & (kc <= qc + 4)
    window = jnp.where(seen, 0.0, masked_score)
    kr, kc = key_cell(128)
    for n, i in enumerate(strips):
        for t in range(tiles):
            row, col = kr + (row0 + 8 * i - 4), kc + (col0 + 8 * t)
            inside = (row >= 0) & (row < frame_rows) & (col >= 0) & (col < frame_cols)
            edge = jnp.where(inside, 0.0, masked_score)
            bias_ref[n * tiles + t] = window + jnp.concatenate([edge] * (wide // 128), 1)


def attend(q, g, keys_of, bias_of, emit):
    features = q.shape[2]
    tiles = q.shape[1] // 8
    head_lanes = features // HEADS
    wide = GROUP * head_lanes
    lane = lax.broadcasted_iota(jnp.int32, (1, wide), 1) // head_lanes
    head_mask = [(lane == h).astype(f32).astype(bf16) for h in range(GROUP)]
    first = lax.broadcasted_iota(jnp.int32, (64, 2 * head_lanes), 1) < head_lanes

    def spread(x):
        return jnp.concatenate([x * m for m in head_mask], 0)

    def gather(x):
        parts = []
        for n in range(GROUP // 2):
            lanes = slice(128 * n, 128 * n + 128)
            parts.append(jnp.where(first, x[128 * n : 128 * n + 64, lanes], x[128 * n + 64 : 128 * n + 128, lanes]))
        return jnp.concatenate(parts, 1)

    def dot(x, y, left, right):
        return lax.dot_general(x, y, (((left,), (right,)), ((), ())), preferred_element_type=f32)

    groups = []
    for t in range(tiles):
        q64 = q[:, 8 * t : 8 * t + 8].reshape(64, features).astype(bf16)
        g64 = g[:, 8 * t : 8 * t + 8].reshape(64, features).astype(bf16)
        for n in range(HEADS // GROUP):
            lanes = slice(n * wide, (n + 1) * wide)
            k, v = keys_of(t, lanes)
            groups.append((t, lanes, spread(q64[:, lanes]), spread(g64[:, lanes]), k, v))
    scores = [dot(k, qx, 1, 1) + bias_of(t) for t, _, qx, _, k, _ in groups]
    grad_probs = [dot(v, gx, 1, 1) for _, _, _, gx, _, v in groups]
    halves = []
    for s, dp in zip(scores, grad_probs):
        w = jnp.exp(s - jnp.max(s, 0, keepdims=True))
        scale = 1.0 / jnp.sum(w, 0, keepdims=True)
        delta = jnp.sum(w * dp, 0, keepdims=True) * scale
        p = w * scale
        halves.append((p.astype(bf16), (p * (dp - delta)).astype(bf16)))
    outs, grads = [[] for _ in range(tiles)], [[] for _ in range(tiles)]
    for (t, lanes, qx, gx, k, v), (ph, ds) in zip(groups, halves):
        outs[t].append(gather(dot(ph, v, 0, 0)))
        grads[t].append(gather(dot(ds, k, 0, 0)) * 0.125)
        dk = dot(ds, qx, 1, 0).reshape(16, 16, wide)
        dv = dot(ph, gx, 1, 0).reshape(16, 16, wide)
        emit(t, lanes, dk, dv)
    join = lambda x: jnp.concatenate([jnp.concatenate(y, 1).reshape(8, 8, features) for y in x], 1)
    return join(outs), join(grads)


def middle_kernel(
    qs_ref, do_ref, k_ref, v_ref, fac_ref, fl_ref, fr_ref, kt_ref, vt_ref, dk_ref, dv_ref, o_ref, dq_ref, bias_ref
):
    members, height, breadth, features = qs_ref.shape
    strips, tiles = height // 8, breadth // 8
    mask_biases(bias_ref, (1,), tiles, place_of(height, breadth))
    for b in range(members):
        for i in range(strips):
            rows = slice(8 * i, 8 * i + 8)
            rims = rims_of(fl_ref, fr_ref, b, rows)
            for m, (ref, out) in enumerate(((k_ref, kt_ref), (v_ref, vt_ref))):
                blocks = [block_of(ref, fac_ref, m + 1, b, i, j, rows, features) for j in range(tiles)]
                for t in range(tiles):
                    out[b, t, rows] = key_tile(blocks, rims[m], t)

    def step(b, _):
        def keys_of(t, lanes):
            return tuple(ref[b, t, 4:20, :, lanes].reshape(256, -1) for ref in (kt_ref, vt_ref))

        def emit(t, lanes, dk, dv):
            dk_ref[b, t, :, :, lanes] = dk
            dv_ref[b, t, :, :, lanes] = dv

        o, dq = attend(qs_ref[b, 8:16].astype(f32), do_ref[b, 8:16].astype(f32), keys_of, lambda t: bias_ref[t], emit)
        o_ref[b] = o.astype(bf16)
        dq_ref[b] = dq.astype(bf16)
        return 0

    lax.fori_loop(0, members, step, 0)


def main_kernel(
    qs_ref, do_ref, kt_ref, vt_ref, dkm_ref, dvm_ref, om_ref, dqm_ref, gm_ref, tok_ref,
    fl_ref, fr_ref, top_ref, bottom_ref, ct_ref, cb_ref,
    keep_ref, send_ref, dq_out, kv_out,
    kh_ref, vh_ref, dkt_ref, dvt_ref, o_ref, tp_ref, all_ref, dq_ref, kv_ref, bias_ref, sem,
):
    members, height, breadth, features = qs_ref.shape
    tall = height + 8
    tiles = breadth // 8
    mask_biases(bias_ref, (0, height // 8 - 1), tiles, place_of(height, breadth))
    for b in range(members):
        for n, (ref, corner) in enumerate(((top_ref, ct_ref), (bottom_ref, cb_ref))):
            rims = [corner[b, 4 * m : 4 * m + 4].astype(f32) for m in range(3)]
            for m, out in enumerate((kh_ref, vh_ref)):
                blocks = [ref[m, b, :, 8 * j : 8 * j + 8].astype(f32) for j in range(tiles)]
                for t in range(tiles):
                    out[n, b, t] = key_tile(blocks, rims[m], t)
            halo = slice(0, 4) if n == 0 else slice(tall - 4, tall)
            tp_ref[b, halo] = jnp.concatenate([ref[2, b].astype(f32), rims[2]], 1).astype(bf16)
            dq_ref[b, halo] = jnp.zeros((4, breadth, features), bf16)
        half = height // 2
        for r in range(0, half, 4):
            pair = rims_of(fl_ref, fr_ref, b, slice(height + r, height + r + 4))
            for rim, row in zip(pair, (r, half + r)):
                own = tok_ref[b, row : row + 4].astype(f32)
                tp_ref[b, row + 4 : row + 8] = jnp.concatenate([own, rim], 1).astype(bf16)
        o_ref[b, 8:16] = om_ref[b]
        dq_ref[b, 12:20] = dqm_ref[b]

    def step(b, _):
        for n, i in enumerate((0, height // 8 - 1)):
            def keys_of(t, lanes):
                parts = []
                for ref, halo in ((kt_ref, kh_ref), (vt_ref, vh_ref)):
                    rim = halo[n, b, t, :, :, lanes]
                    own = ref[b, t, slice(0, 12) if n == 0 else slice(height - 12, height), :, lanes]
                    both = [rim, own] if n == 0 else [own, rim]
                    parts.append(jnp.concatenate(both, 0).reshape(256, -1))
                return tuple(parts)

            def emit(t, lanes, dk, dv):
                for ref, mid, x in ((dkt_ref, dkm_ref, dk), (dvt_ref, dvm_ref, dv)):
                    if n == 0:
                        ref[b, t, 0:8, :, lanes] = x[0:8]
                        ref[b, t, 8:16, :, lanes] = x[8:16] + mid[b, t, 0:8, :, lanes]
                    else:
                        ref[b, t, 16:24, :, lanes] = x[0:8] + mid[b, t, 8:16, :, lanes]
                        ref[b, t, 24:32, :, lanes] = x[8:16]

            rows = slice(8 * i, 8 * i + 8)
            o, dq = attend(qs_ref[b, rows].astype(f32), do_ref[b, rows].astype(f32), keys_of, lambda t: bias_ref[n * tiles + t], emit)
            o_ref[b, rows] = o.astype(bf16)
            dq_ref[b, 8 * i + 4 : 8 * i + 12] = dq.astype(bf16)
        return 0

    lax.fori_loop(0, members, step, 0)

    for b in range(members):
        for r in range(0, tall, 8):
            rows = slice(r, r + 8)
            for m, ref in enumerate((dkt_ref, dvt_ref)):
                rim = [ref[b, t, rows, 8:16] for t in range(tiles)]
                low = lower(rim[0])
                own = []
                for t in range(tiles):
                    x = ref[b, t, rows, 0:8]
                    if t > 0:
                        x = x + jnp.where(low, rim[t - 1], 0.0)
                    if t < tiles - 1:
                        x = x + jnp.where(low, 0.0, rim[t + 1])
                    own.append(x)
                own.append(jnp.where(low, rim[tiles - 1], rim[0]))
                kv_ref[b, rows, :, m * features : (m + 1) * features] = jnp.concatenate(own, 1).astype(bf16)

    copies = [
        pltpu.make_async_copy(src, dst, sem.at[n])
        for n, (src, dst) in enumerate(((dq_ref, dq_out), (kv_ref, kv_out)))
    ]
    for c in copies:
        c.start()
    down = (((0,), (0,)), ((), ()))
    cells = members * height * breadth
    padded = members * tall * (breadth + 8)
    for b in range(members):
        x = lax.dot_general(
            tok_ref[b].reshape(cells // members, features),
            dq_ref[b, 4 : tall - 4].reshape(cells // members, features), down,
            preferred_element_type=f32,
        )
        y = lax.dot_general(
            o_ref[b].reshape(cells // members, features), gm_ref[b].reshape(cells // members, features), down,
            preferred_element_type=f32,
        )
        if b:
            x, y = x + all_ref[:, 0:features], y + all_ref[:, 3 * features :]
        all_ref[:, 0:features] = x
        all_ref[:, 3 * features :] = y
    kv = kv_ref[...].reshape(padded, 2 * features)
    all_ref[:, features : 3 * features] = lax.dot_general(
        tp_ref[...].reshape(padded, features), kv, down, preferred_element_type=f32
    )

    deep_rows, pairs, deep, broad = keep_ref.shape
    count = 2 * pairs
    main, rest = 3 * features // count, features // count
    lanes = lax.broadcasted_iota(jnp.int32, (features, broad), 1)

    def window(start, end):
        base, off = start // broad * broad, start % broad
        x = all_ref[:, base : base + broad]
        if off:
            x = pltpu.roll(x, broad - off, 1)
        if end > base + broad:
            y = pltpu.roll(all_ref[:, base + broad : base + 2 * broad], broad - off, 1)
            x = jnp.where(lanes < broad - off, x, y)
        return x

    def block(c):
        x = window(main * c, main * (c + 1))
        base, off = 3 * features + rest * c // broad * broad, rest * c % broad
        y = all_ref[:, base : base + broad]
        if off != main:
            y = pltpu.roll(y, (main - off) % broad, 1)
        return jnp.where(lanes < main, x, y).astype(bf16).reshape(deep_rows, deep, broad)

    mine = lax.axis_index("core") == 0
    for p in range(pairs):
        even, odd = block(2 * p), block(2 * p + 1)
        keep_ref[:, p] = jnp.where(mine, even, odd)
        send_ref[:, p] = jnp.where(mine, odd, even)
    for c in copies:
        c.wait()


def token_kernel(kv_ref, dq_ref, w_ref, gt_ref, left_ref, right_ref):
    members, tall, breadth, features = dq_ref.shape
    across = (((1,), (1,)), ((), ()))
    middle = tall // 2
    for b in range(members):
        y = lax.dot_general(
            kv_ref[b].reshape(tall * (breadth + 8), 2 * features), w_ref[:, features:], across,
            preferred_element_type=f32,
        ).reshape(tall, breadth + 8, features)
        z = lax.dot_general(
            dq_ref[b].reshape(tall * breadth, features), w_ref[:, 0:features], across,
            preferred_element_type=f32,
        ).reshape(tall, breadth, features)
        gt_ref[b] = (y[:, 0:breadth] + z).astype(bf16)
        here, there = y[0:middle, breadth:], turn(y[middle:, breadth:])
        low = lower(here)
        right_ref[b] = jnp.where(low, here, there).astype(bf16)
        left_ref[b] = jnp.where(low, there, here).astype(bf16)


def back_rims(fl, fr):
    low = lower(fl)
    here = (jnp.where(low, fl, 0.0), jnp.where(low, 0.0, fr))
    there = (jnp.where(low, turn(fl), 0.0), jnp.where(low, 0.0, turn(fr)))
    return here, there


def plus_rims(x, rims):
    last = x.shape[1] - 8
    return jnp.concatenate([x[:, 0:8] + rims[0], x[:, 8:last], x[:, last:] + rims[1]], 1) if last > 8 else (
        jnp.concatenate([x[:, 0:8] + rims[0], x[:, 8:] + rims[1]], 1)
    )


def add_kernel(x_ref, y_ref, sum_ref):
    sum_ref[...] = (x_ref[...].astype(f32) + y_ref[...].astype(f32)).astype(bf16)


def total_kernel(x_ref, sum_ref, square_ref):
    x = jnp.sum(x_ref[...].astype(f32), 0)
    sum_ref[...] = x
    square = jnp.sum(x * x, 0, keepdims=True)
    square_ref[...] = jnp.broadcast_to(square, square_ref.shape)


def halo_kernel(gt_ref, fl_ref, fr_ref, up_ref, down_ref):
    members, tall = gt_ref.shape[:2]
    half = tall // 2
    for b in range(members):
        here, _ = back_rims(fl_ref[b, 0:4].astype(f32), fr_ref[b, 0:4].astype(f32))
        _, there = back_rims(fl_ref[b, half - 4 : half].astype(f32), fr_ref[b, half - 4 : half].astype(f32))
        up_ref[b] = plus_rims(gt_ref[b, 0:4].astype(f32), here).astype(bf16)
        down_ref[b] = plus_rims(gt_ref[b, tall - 4 : tall].astype(f32), there).astype(bf16)


def join_kernel(gt_ref, fl_ref, fr_ref, ft_ref, fb_ref, tok_ref):
    members, height = tok_ref.shape[:2]
    half = (height + 8) // 2
    for b in range(members):
        for r in range(0, half, 4):
            pair = back_rims(fl_ref[b, r : r + 4].astype(f32), fr_ref[b, r : r + 4].astype(f32))
            for rims, row in zip(pair, (r, half + r)):
                if row == 0 or row == height + 4:
                    continue
                y = plus_rims(gt_ref[b, row : row + 4].astype(f32), rims)
                if row == 4:
                    y = y + ft_ref[b].astype(f32)
                if row == height:
                    y = y + fb_ref[b].astype(f32)
                tok_ref[b, row - 4 : row] = y.astype(bf16)


def clip_kernel(x_ref, square_ref, qkv_ref, out_ref):
    total = jnp.sum(jnp.sum(square_ref[...], 0, keepdims=True), 1, keepdims=True)
    clip = jnp.minimum(1.0, max_norm / jnp.sqrt(total + tiny_square))
    x = x_ref[...] * clip
    main = qkv_ref.shape[1]
    qkv_ref[...] = x[:, 0:main]
    out_ref[...] = x.T[main:]


def shift(x, axes, by):
    size = lax.axis_size(axes)
    return lax.ppermute(x, axes, [(i, i + by) for i in range(size) if 0 <= i + by < size])


def body(tokens, w_qkv, w_out, q_saved, k_saved, v_saved, scale_exp, grad_out, crop_start):
    members, height, breadth, features = tokens.shape
    tall = height + 8
    packed = height + height // 2
    packed_columns = shape(members, packed, 8, features)
    strip = shape(3, members, 4, breadth, features)
    factor, up, down, left, right = call(
        edge_kernel,
        (
            shape(*scale_exp.shape[:3], 3 * features, dtype=f32),
            strip, strip, packed_columns, packed_columns,
        ),
        (scale_exp, k_saved, v_saved, tokens),
        scratch=(pltpu.VMEM(tokens.shape, bf16),) * 3 + (pltpu.SemaphoreType.DMA((3,)),),
        far=(1, 2, 3),
        limit=58 << 20,
    )
    top, bottom = shift(down, "row", 1), shift(up, "row", -1)
    cells = members * height * breadth
    qs, gm, do = call(
        prepare_kernel,
        (shape(*tokens.shape),) * 3,
        (crop_start, q_saved, grad_out, factor, w_out),
        smem=(0,),
        flops=2 * cells * features * features,
    )
    from_left, from_right = shift(right, COLS, 1), shift(left, COLS, -1)
    corner = shape(members, 12, 8, features)
    up, down = call(corner_kernel, (corner, corner), (from_left, from_right))
    corner_top, corner_bottom = shift(down, "row", 1), shift(up, "row", -1)
    tiles = breadth // 8
    own_tiles = shape(members, tiles, height, 16, features)
    middle_tiles = shape(members, tiles, 16, 16, features, dtype=f32)
    middle_rows = shape(members, 8, breadth, features)
    kt, vt, dk, dv, out, dq = call(
        middle_kernel,
        (own_tiles, own_tiles, middle_tiles, middle_tiles, middle_rows, middle_rows),
        (qs, do, k_saved, v_saved, factor, from_left, from_right),
        scratch=(pltpu.VMEM((tiles, 256, features // 2), f32),),
        flops=4 * cells * features * features,
        limit=20 << 20,
    )
    rows, pairs = lax.axis_size("row"), lax.axis_size("pair")
    deep, wide = features // rows, 4 * features // (2 * pairs)
    halo_tiles = pltpu.VMEM((2, members, tiles, 4, 16, features), bf16)
    all_tiles = pltpu.VMEM((members, tiles, tall, 16, features), f32)
    keep, send, dq, kv = call(
        main_kernel,
        (
            shape(rows, pairs, deep, wide),
            shape(rows, pairs, deep, wide),
            shape(members, tall, breadth, features),
            shape(members, tall, breadth + 8, 2 * features),
        ),
        (
            qs, do, kt, vt, dk, dv, out, dq, gm, tokens,
            from_left, from_right, top, bottom, corner_top, corner_bottom,
        ),
        scratch=(
            halo_tiles, halo_tiles, all_tiles, all_tiles,
            pltpu.VMEM(tokens.shape, bf16),
            pltpu.VMEM((members, tall, breadth + 8, features), bf16),
            pltpu.VMEM((features, 4 * features), f32),
            pltpu.VMEM((members, tall, breadth, features), bf16),
            pltpu.VMEM((members, tall, breadth + 8, 2 * features), bf16),
            pltpu.VMEM((2 * tiles, 256, features // 2), f32),
            pltpu.SemaphoreType.DMA((2,)),
        ),
        far_outs=(2, 3),
        flops=12 * cells * features * features,
        limit=37 << 20,
    )
    other = lax.ppermute(send, "core", [(0, 1), (1, 0)])
    both = call(add_kernel, shape(rows, pairs, deep, wide), (keep, other)).reshape(rows * pairs, deep, wide)
    parts = lax.all_to_all(both, ("row", "pair"), 0, 0, tiled=True)
    gt, left, right = call(
        token_kernel,
        (
            shape(members, tall, breadth, features),
            shape(members, tall // 2, 8, features),
            shape(members, tall // 2, 8, features),
        ),
        (kv, dq, w_qkv),
        flops=6 * cells * features * features,
        limit=20 << 20,
    )
    back_left, back_right = shift(right, COLS, 1), shift(left, COLS, -1)
    halo = shape(members, 4, breadth, features)
    up, down = call(halo_kernel, (halo, halo), (gt, back_left, back_right))
    back_top, back_bottom = shift(down, "row", 1), shift(up, "row", -1)
    grad_tokens = call(
        join_kernel, shape(*tokens.shape), (gt, back_left, back_right, back_top, back_bottom)
    )
    total, square = call(
        total_kernel,
        (shape(deep, wide, dtype=f32), shape(2 * rows * pairs, wide, dtype=f32)),
        (parts,),
    )
    squares = lax.all_to_all(square, ("row", "pair", "core"), 0, 0, tiled=True)
    main = 3 * features // (2 * pairs)
    grad_qkv, grad_w_out = call(
        clip_kernel,
        (shape(deep, main, dtype=f32), shape(wide - main, deep, dtype=f32)),
        (total, squares),
    )
    return grad_tokens, grad_qkv, grad_w_out.T


def solution(mesh):
    rows, cols = mesh.devices.shape
    split = jax.sharding.Mesh(mesh.devices.reshape(rows, cols // 2, 2), ("row",) + COLS)
    cells = P(None, "row", COLS, None)
    return jax.shard_map(
        body,
        mesh=split,
        in_specs=(cells, P(), P(), cells, cells, cells, cells, cells, P()),
        out_specs=(cells, P("row", COLS), P("row", COLS)),
        check_vma=False,
    )
```

```python
import jax
import jax.numpy as jnp
from jax import lax
from jax.experimental import pallas as pl
from jax.experimental.pallas import tpu as pltpu
from jax.sharding import PartitionSpec as P

HEADS = 8
RADIUS = 4
BLOCK = 8
GROUP = 4

max_norm = 1000.0
masked_score = -1e30
tiny_square = 1e-06

f32 = jnp.float32
bf16 = jnp.bfloat16
VMEM = pl.BlockSpec(memory_space=pltpu.VMEM)
COLS = ("pair", "core")
ANY = pl.BlockSpec(memory_space=pltpu.HBM)
SMEM = pl.BlockSpec(memory_space=pltpu.SMEM)


def call(kernel, outs, ins, scratch=(), smem=(), far=(), far_outs=(), flops=0, limit=16 << 20):
    moved = sum(a.size * a.dtype.itemsize for a in list(ins) + jax.tree.leaves(outs))
    return pl.pallas_call(
        kernel,
        out_shape=outs,
        in_specs=[SMEM if n in smem else ANY if n in far else VMEM for n in range(len(ins))],
        out_specs=tuple(ANY if n in far_outs else VMEM for n in range(len(outs))) if isinstance(outs, tuple) else VMEM,
        scratch_shapes=list(scratch),
        compiler_params=pltpu.CompilerParams(vmem_limit_bytes=limit),
        cost_estimate=pl.CostEstimate(
            flops=flops, bytes_accessed=moved, transcendentals=0
        ),
    )(*ins)


def shape(*dims, dtype=bf16):
    return jax.ShapeDtypeStruct(dims, dtype)


def turn(x):
    return pltpu.roll(x, 4, 1)


def lower(x):
    return lax.broadcasted_iota(jnp.int32, x.shape, 1) < 4


def block_of(ref, fac_ref, part, b, i, j, rows, features):
    factor = fac_ref[b, i, j : j + 1, part * features : (part + 1) * features]
    return ref[b, rows, 8 * j : 8 * j + 8, :].astype(f32) * factor[None]


def even_column():
    return lax.axis_index("core") == 0


def even_row():
    return lax.rem(lax.axis_index("row"), 2) == 0


def swap(even, x, y):
    return jnp.where(even, x, y), jnp.where(even, y, x)


def edge_kernel(
    scale_ref, k_ref, v_ref, tok_ref, fac_ref, re_ref, ro_ref, ce_ref, co_ref, s_buf, k_buf, v_buf, t_buf, sem
):
    members, height, breadth, features = k_ref.shape
    tiles = breadth // 8
    first = pltpu.make_async_copy(scale_ref, s_buf, sem.at[0])
    first.start()
    copies = []
    for b in range(members):
        copies.append([
            pltpu.make_async_copy(src.at[b], dst.at[b], sem.at[1 + 3 * b + n])
            for n, (src, dst) in enumerate(((k_ref, k_buf), (v_ref, v_buf), (tok_ref, t_buf)))
        ])
        for c in copies[b]:
            c.start()
    count = scale_ref.shape[3]
    per = 3 * features // count
    hot = (
        lax.broadcasted_iota(jnp.int32, (count, 3 * features), 0)
        == lax.broadcasted_iota(jnp.int32, (count, 3 * features), 1) // per
    ).astype(f32).astype(bf16)
    first.wait()
    for b in range(members):
        for i in range(height // 8):
            factor = jnp.exp2(s_buf[b, i].astype(f32)).astype(bf16)
            fac_ref[b, i] = jnp.dot(factor, hot, preferred_element_type=f32)
    half, last = height // 2, height // 8 - 1
    even_c, even_r = even_column(), even_row()
    for b in range(members):
        for c in copies[b]:
            c.wait()
        ends = {}
        for i in range(last + 1):
            rows = slice(8 * i, 8 * i + 8)
            k = [block_of(k_buf, fac_ref, 1, b, i, j, rows, features) for j in range(tiles)]
            v = [block_of(v_buf, fac_ref, 2, b, i, j, rows, features) for j in range(tiles)]
            low = lower(k[0])
            left, right = jnp.where(low, k[0], turn(v[0])), jnp.where(low, turn(v[-1]), k[-1])
            x, y = swap(even_c, right, left)
            ce_ref[b, rows], co_ref[b, rows] = x.astype(bf16), y.astype(bf16)
            for m, parts in enumerate((k, v)):
                if i == 0:
                    ends[m, 0] = jnp.concatenate(parts, 1)[0:4]
                if i == last:
                    ends[m, 1] = jnp.concatenate(parts, 1)[4:8]
        ends[2, 0], ends[2, 1] = t_buf[b, 0:4].astype(f32), t_buf[b, height - 4 : height].astype(f32)
        for m in range(3):
            x, y = swap(even_r, ends[m, 1], ends[m, 0])
            re_ref[m, b], ro_ref[m, b] = x.astype(bf16), y.astype(bf16)
        for r in range(0, half, 4):
            here, there = slice(r, r + 4), slice(half + r, half + r + 4)
            out = slice(height + r, height + r + 4)
            left, right = pack_columns(t_buf[b, here], t_buf[b, there])
            x, y = swap(even_c, right, left)
            ce_ref[b, out], co_ref[b, out] = x.astype(bf16), y.astype(bf16)


def pack_columns(one, two):
    last = one.shape[1] - 8
    x0, y0 = one[:, 0:8].astype(f32), two[:, 0:8].astype(f32)
    x1, y1 = one[:, last:].astype(f32), two[:, last:].astype(f32)
    low = lower(x0)
    return jnp.where(low, x0, turn(y0)), jnp.where(low, turn(y1), x1)


def corner_kernel(fe_ref, fo_ref, re_ref, ro_ref):
    members, packed = fe_ref.shape[:2]
    height = packed * 2 // 3
    half = height // 2
    even = even_row()
    for b in range(members):
        ends = []
        for n, row in enumerate((0, height - 4)):
            k, v = rims_of(fe_ref, fo_ref, b, slice(row, row + 4))
            first = height + (row if n == 0 else row - half)
            t = rims_of(fe_ref, fo_ref, b, slice(first, first + 4))[n]
            ends.append(jnp.concatenate([k, v, t], 0))
        x, y = swap(even, ends[1], ends[0])
        re_ref[b], ro_ref[b] = x.astype(bf16), y.astype(bf16)


def columns_of(fe_ref, fo_ref, b, rows):
    right, left = swap(even_column(), fe_ref[b, rows].astype(f32), fo_ref[b, rows].astype(f32))
    return left, right


def rims_of(fe_ref, fo_ref, b, rows):
    left, right = columns_of(fe_ref, fo_ref, b, rows)
    low = lower(left)
    return jnp.where(low, right, left), turn(jnp.where(low, left, right))


def prepare_kernel(crop_ref, q_ref, g_ref, fac_ref, w_ref, qs_ref, gm_ref, do_ref):
    members, height, breadth, features = q_ref.shape
    tiles = breadth // 8
    row0 = lax.axis_index("row") * height
    col0 = (lax.axis_index("pair") * 2 + lax.axis_index("core")) * breadth
    for b in range(members):
        for i in range(height // 8):
            rows = slice(8 * i, 8 * i + 8)
            parts = [block_of(q_ref, fac_ref, 0, b, i, j, rows, features) for j in range(tiles)]
            qs_ref[b, rows] = (jnp.concatenate(parts, 1) * 0.125).astype(bf16)
            g = g_ref[b, rows].astype(f32)
            r = lax.broadcasted_iota(jnp.int32, g.shape, 0) + (8 * i + row0)
            c = lax.broadcasted_iota(jnp.int32, g.shape, 1) + col0
            keep = (r >= crop_ref[b, 0]) & (c >= crop_ref[b, 1])
            gm = jnp.where(keep, g, 0.0).astype(bf16)
            gm_ref[b, rows] = gm
            do = lax.dot_general(
                gm.reshape(8 * breadth, features), w_ref[...], (((1,), (1,)), ((), ())),
                preferred_element_type=f32,
            )
            do_ref[b, rows] = do.astype(bf16).reshape(8, breadth, features)


def key_tile(blocks, rim, t):
    low = lower(rim)
    before = rim if t == 0 else blocks[t - 1]
    after = rim if t == len(blocks) - 1 else blocks[t + 1]
    return jnp.concatenate([blocks[t], jnp.where(low, after, before)], 1).astype(bf16)


def place_of(height, breadth):
    row0 = lax.axis_index("row") * height
    col0 = (lax.axis_index("pair") * 2 + lax.axis_index("core")) * breadth
    return row0, col0, height * lax.axis_size("row"), breadth * lax.axis_size("pair") * 2


def mask_biases(bias_ref, strips, tiles, place):
    row0, col0, frame_rows, frame_cols = place
    wide = bias_ref.shape[2]

    def key_cell(n):
        kn = lax.broadcasted_iota(jnp.int32, (256, n), 0)
        ks = kn % 16
        return kn // 16, jnp.where(ks < 12, ks, ks - 16)

    kr, kc = key_cell(wide)
    qn = lax.broadcasted_iota(jnp.int32, (256, wide), 1) % 64
    qr, qc = qn // 8, qn % 8
    seen = (kr >= qr) & (kr <= qr + 8) & (kc >= qc - 4) & (kc <= qc + 4)
    window = jnp.where(seen, 0.0, masked_score)
    kr, kc = key_cell(128)
    for n, i in enumerate(strips):
        for t in range(tiles):
            row, col = kr + (row0 + 8 * i - 4), kc + (col0 + 8 * t)
            inside = (row >= 0) & (row < frame_rows) & (col >= 0) & (col < frame_cols)
            edge = jnp.where(inside, 0.0, masked_score)
            bias_ref[n * tiles + t] = window + jnp.concatenate([edge] * (wide // 128), 1)


def attend(q, g, keys_of, bias_of, emit):
    features = q.shape[2]
    tiles = q.shape[1] // 8
    head_lanes = features // HEADS
    wide = GROUP * head_lanes
    lane = lax.broadcasted_iota(jnp.int32, (1, wide), 1) // head_lanes
    head_mask = [(lane == h).astype(f32).astype(bf16) for h in range(GROUP)]
    first = lax.broadcasted_iota(jnp.int32, (64, 2 * head_lanes), 1) < head_lanes

    def spread(x):
        return jnp.concatenate([x * m for m in head_mask], 0)

    def gather(x):
        parts = []
        for n in range(GROUP // 2):
            lanes = slice(128 * n, 128 * n + 128)
            parts.append(jnp.where(first, x[128 * n : 128 * n + 64, lanes], x[128 * n + 64 : 128 * n + 128, lanes]))
        return jnp.concatenate(parts, 1)

    def dot(x, y, left, right):
        return lax.dot_general(x, y, (((left,), (right,)), ((), ())), preferred_element_type=f32)

    groups = []
    for t in range(tiles):
        q64 = q[:, 8 * t : 8 * t + 8].reshape(64, features).astype(bf16)
        g64 = g[:, 8 * t : 8 * t + 8].reshape(64, features).astype(bf16)
        for n in range(HEADS // GROUP):
            lanes = slice(n * wide, (n + 1) * wide)
            k, v = keys_of(t, lanes)
            groups.append((t, lanes, spread(q64[:, lanes]), spread(g64[:, lanes]), k, v))
    scores = [dot(k, qx, 1, 1) + bias_of(t) for t, _, qx, _, k, _ in groups]
    grad_probs = [dot(v, gx, 1, 1) for _, _, _, gx, _, v in groups]
    halves = []
    for s, dp in zip(scores, grad_probs):
        w = jnp.exp(s - jnp.max(s, 0, keepdims=True))
        scale = 1.0 / jnp.sum(w, 0, keepdims=True)
        delta = jnp.sum(w * dp, 0, keepdims=True) * scale
        p = w * scale
        halves.append((p.astype(bf16), (p * (dp - delta)).astype(bf16)))
    outs, grads = [[] for _ in range(tiles)], [[] for _ in range(tiles)]
    for (t, lanes, qx, gx, k, v), (ph, ds) in zip(groups, halves):
        outs[t].append(gather(dot(ph, v, 0, 0)))
        grads[t].append(gather(dot(ds, k, 0, 0)) * 0.125)
        dk = dot(ds, qx, 1, 0).reshape(16, 16, wide)
        dv = dot(ph, gx, 1, 0).reshape(16, 16, wide)
        emit(t, lanes, dk, dv)
    join = lambda x: jnp.concatenate([jnp.concatenate(y, 1).reshape(8, 8, features) for y in x], 1)
    return join(outs), join(grads)


def middle_kernel(
    qs_ref, do_ref, k_ref, v_ref, fac_ref, fl_ref, fr_ref, kt_ref, vt_ref, dk_ref, dv_ref, o_ref, dq_ref, bias_ref
):
    members, height, breadth, features = qs_ref.shape
    strips, tiles = height // 8, breadth // 8
    mask_biases(bias_ref, (1,), tiles, place_of(height, breadth))
    for b in range(members):
        for i in range(strips):
            rows = slice(8 * i, 8 * i + 8)
            rims = rims_of(fl_ref, fr_ref, b, rows)
            for m, (ref, out) in enumerate(((k_ref, kt_ref), (v_ref, vt_ref))):
                blocks = [block_of(ref, fac_ref, m + 1, b, i, j, rows, features) for j in range(tiles)]
                for t in range(tiles):
                    out[b, t, rows] = key_tile(blocks, rims[m], t)

    def step(b, _):
        def keys_of(t, lanes):
            return tuple(ref[b, t, 4:20, :, lanes].reshape(256, -1) for ref in (kt_ref, vt_ref))

        def emit(t, lanes, dk, dv):
            dk_ref[b, t, :, :, lanes] = dk
            dv_ref[b, t, :, :, lanes] = dv

        o, dq = attend(qs_ref[b, 8:16].astype(f32), do_ref[b, 8:16].astype(f32), keys_of, lambda t: bias_ref[t], emit)
        o_ref[b] = o.astype(bf16)
        dq_ref[b] = dq.astype(bf16)
        return 0

    lax.fori_loop(0, members, step, 0)


def main_kernel(
    qs_ref, do_ref, kt_ref, vt_ref, dkm_ref, dvm_ref, om_ref, dqm_ref, gm_ref, tok_ref,
    fl_ref, fr_ref, he_ref, ho_ref, ke_ref, ko_ref,
    keep_ref, send_ref, dq_out, kv_out,
    kh_ref, vh_ref, dkt_ref, dvt_ref, o_ref, tp_ref, all_ref, dq_ref, kv_ref, bias_ref, sem,
):
    members, height, breadth, features = qs_ref.shape
    tall = height + 8
    tiles = breadth // 8
    mask_biases(bias_ref, (0, height // 8 - 1), tiles, place_of(height, breadth))
    even = even_row()
    for b in range(members):
        corners = swap(even, ke_ref[b].astype(f32), ko_ref[b].astype(f32))[::-1]
        strips = [swap(even, he_ref[m, b].astype(f32), ho_ref[m, b].astype(f32))[::-1] for m in range(3)]
        for n, corner in enumerate(corners):
            rims = [corner[4 * m : 4 * m + 4] for m in range(3)]
            for m, out in enumerate((kh_ref, vh_ref)):
                blocks = [strips[m][n][:, 8 * j : 8 * j + 8] for j in range(tiles)]
                for t in range(tiles):
                    out[n, b, t] = key_tile(blocks, rims[m], t)
            halo = slice(0, 4) if n == 0 else slice(tall - 4, tall)
            tp_ref[b, halo] = jnp.concatenate([strips[2][n], rims[2]], 1).astype(bf16)
            dq_ref[b, halo] = jnp.zeros((4, breadth, features), bf16)
        half = height // 2
        for r in range(0, half, 4):
            pair = rims_of(fl_ref, fr_ref, b, slice(height + r, height + r + 4))
            for rim, row in zip(pair, (r, half + r)):
                own = tok_ref[b, row : row + 4].astype(f32)
                tp_ref[b, row + 4 : row + 8] = jnp.concatenate([own, rim], 1).astype(bf16)
        o_ref[b, 8:16] = om_ref[b]
        dq_ref[b, 12:20] = dqm_ref[b]

    def step(b, _):
        for n, i in enumerate((0, height // 8 - 1)):
            def keys_of(t, lanes):
                parts = []
                for ref, halo in ((kt_ref, kh_ref), (vt_ref, vh_ref)):
                    rim = halo[n, b, t, :, :, lanes]
                    own = ref[b, t, slice(0, 12) if n == 0 else slice(height - 12, height), :, lanes]
                    both = [rim, own] if n == 0 else [own, rim]
                    parts.append(jnp.concatenate(both, 0).reshape(256, -1))
                return tuple(parts)

            def emit(t, lanes, dk, dv):
                for ref, mid, x in ((dkt_ref, dkm_ref, dk), (dvt_ref, dvm_ref, dv)):
                    if n == 0:
                        ref[b, t, 0:8, :, lanes] = x[0:8]
                        ref[b, t, 8:16, :, lanes] = x[8:16] + mid[b, t, 0:8, :, lanes]
                    else:
                        ref[b, t, 16:24, :, lanes] = x[0:8] + mid[b, t, 8:16, :, lanes]
                        ref[b, t, 24:32, :, lanes] = x[8:16]

            rows = slice(8 * i, 8 * i + 8)
            o, dq = attend(qs_ref[b, rows].astype(f32), do_ref[b, rows].astype(f32), keys_of, lambda t: bias_ref[n * tiles + t], emit)
            o_ref[b, rows] = o.astype(bf16)
            dq_ref[b, 8 * i + 4 : 8 * i + 12] = dq.astype(bf16)
        return 0

    lax.fori_loop(0, members, step, 0)

    for b in range(members):
        for r in range(0, tall, 8):
            rows = slice(r, r + 8)
            for m, ref in enumerate((dkt_ref, dvt_ref)):
                rim = [ref[b, t, rows, 8:16] for t in range(tiles)]
                low = lower(rim[0])
                own = []
                for t in range(tiles):
                    x = ref[b, t, rows, 0:8]
                    if t > 0:
                        x = x + jnp.where(low, rim[t - 1], 0.0)
                    if t < tiles - 1:
                        x = x + jnp.where(low, 0.0, rim[t + 1])
                    own.append(x)
                own.append(jnp.where(low, rim[tiles - 1], rim[0]))
                kv_ref[b, rows, :, m * features : (m + 1) * features] = jnp.concatenate(own, 1).astype(bf16)

    copies = [
        pltpu.make_async_copy(src, dst, sem.at[n])
        for n, (src, dst) in enumerate(((dq_ref, dq_out), (kv_ref, kv_out)))
    ]
    for c in copies:
        c.start()
    down = (((0,), (0,)), ((), ()))
    cells = members * height * breadth
    padded = members * tall * (breadth + 8)
    for b in range(members):
        x = lax.dot_general(
            tok_ref[b].reshape(cells // members, features),
            dq_ref[b, 4 : tall - 4].reshape(cells // members, features), down,
            preferred_element_type=f32,
        )
        y = lax.dot_general(
            o_ref[b].reshape(cells // members, features), gm_ref[b].reshape(cells // members, features), down,
            preferred_element_type=f32,
        )
        if b:
            x, y = x + all_ref[:, 0:features], y + all_ref[:, 3 * features :]
        all_ref[:, 0:features] = x
        all_ref[:, 3 * features :] = y
    kv = kv_ref[...].reshape(padded, 2 * features)
    all_ref[:, features : 3 * features] = lax.dot_general(
        tp_ref[...].reshape(padded, features), kv, down, preferred_element_type=f32
    )

    deep_rows, pairs, deep, broad = keep_ref.shape
    count = 2 * pairs
    main, rest = 3 * features // count, features // count
    lanes = lax.broadcasted_iota(jnp.int32, (features, broad), 1)

    def window(start, end):
        base, off = start // broad * broad, start % broad
        x = all_ref[:, base : base + broad]
        if off:
            x = pltpu.roll(x, broad - off, 1)
        if end > base + broad:
            y = pltpu.roll(all_ref[:, base + broad : base + 2 * broad], broad - off, 1)
            x = jnp.where(lanes < broad - off, x, y)
        return x

    def block(c):
        x = window(main * c, main * (c + 1))
        base, off = 3 * features + rest * c // broad * broad, rest * c % broad
        y = all_ref[:, base : base + broad]
        if off != main:
            y = pltpu.roll(y, (main - off) % broad, 1)
        return jnp.where(lanes < main, x, y).astype(bf16).reshape(deep_rows, deep, broad)

    mine = lax.axis_index("core") == 0
    for p in range(pairs):
        even, odd = block(2 * p), block(2 * p + 1)
        keep_ref[:, p] = jnp.where(mine, even, odd)
        send_ref[:, p] = jnp.where(mine, odd, even)
    for c in copies:
        c.wait()


def token_kernel(kv_ref, dq_ref, w_ref, gt_ref, ce_ref, co_ref):
    members, tall, breadth, features = dq_ref.shape
    across = (((1,), (1,)), ((), ()))
    middle = tall // 2
    for b in range(members):
        y = lax.dot_general(
            kv_ref[b].reshape(tall * (breadth + 8), 2 * features), w_ref[:, features:], across,
            preferred_element_type=f32,
        ).reshape(tall, breadth + 8, features)
        z = lax.dot_general(
            dq_ref[b].reshape(tall * breadth, features), w_ref[:, 0:features], across,
            preferred_element_type=f32,
        ).reshape(tall, breadth, features)
        gt_ref[b] = (y[:, 0:breadth] + z).astype(bf16)
        here, there = y[0:middle, breadth:], turn(y[middle:, breadth:])
        low = lower(here)
        x, y = swap(even_column(), jnp.where(low, here, there), jnp.where(low, there, here))
        ce_ref[b], co_ref[b] = x.astype(bf16), y.astype(bf16)


def back_rims(fl, fr):
    low = lower(fl)
    here = (jnp.where(low, fl, 0.0), jnp.where(low, 0.0, fr))
    there = (jnp.where(low, turn(fl), 0.0), jnp.where(low, 0.0, turn(fr)))
    return here, there


def plus_rims(x, rims):
    last = x.shape[1] - 8
    return jnp.concatenate([x[:, 0:8] + rims[0], x[:, 8:last], x[:, last:] + rims[1]], 1) if last > 8 else (
        jnp.concatenate([x[:, 0:8] + rims[0], x[:, 8:] + rims[1]], 1)
    )


def add_kernel(x_ref, y_ref, sum_ref):
    sum_ref[...] = (x_ref[...].astype(f32) + y_ref[...].astype(f32)).astype(bf16)


def total_kernel(x_ref, sum_ref, square_ref):
    x = jnp.sum(x_ref[...].astype(f32), 0)
    sum_ref[...] = x
    square = jnp.sum(x * x, 0, keepdims=True)
    square_ref[...] = jnp.broadcast_to(square, square_ref.shape)


def halo_kernel(gt_ref, fe_ref, fo_ref, re_ref, ro_ref):
    members, tall = gt_ref.shape[:2]
    half = tall // 2
    for b in range(members):
        here, _ = back_rims(*columns_of(fe_ref, fo_ref, b, slice(0, 4)))
        _, there = back_rims(*columns_of(fe_ref, fo_ref, b, slice(half - 4, half)))
        up = plus_rims(gt_ref[b, 0:4].astype(f32), here)
        down = plus_rims(gt_ref[b, tall - 4 : tall].astype(f32), there)
        x, y = swap(even_row(), down, up)
        re_ref[b], ro_ref[b] = x.astype(bf16), y.astype(bf16)


def join_kernel(gt_ref, fe_ref, fo_ref, he_ref, ho_ref, tok_ref):
    members, height = tok_ref.shape[:2]
    half = (height + 8) // 2
    for b in range(members):
        bottom, top = swap(even_row(), he_ref[b].astype(f32), ho_ref[b].astype(f32))
        for r in range(0, half, 4):
            pair = back_rims(*columns_of(fe_ref, fo_ref, b, slice(r, r + 4)))
            for rims, row in zip(pair, (r, half + r)):
                if row == 0 or row == height + 4:
                    continue
                y = plus_rims(gt_ref[b, row : row + 4].astype(f32), rims)
                if row == 4:
                    y = y + top
                if row == height:
                    y = y + bottom
                tok_ref[b, row - 4 : row] = y.astype(bf16)


def clip_kernel(x_ref, square_ref, qkv_ref, out_ref):
    total = jnp.sum(jnp.sum(square_ref[...], 0, keepdims=True), 1, keepdims=True)
    clip = jnp.minimum(1.0, max_norm / jnp.sqrt(total + tiny_square))
    x = x_ref[...] * clip
    main = qkv_ref.shape[1]
    qkv_ref[...] = x[:, 0:main]
    out_ref[...] = x.T[main:]


def exchange(even, odd, axes):
    size = lax.axis_size(axes)
    out = []
    for x, first in ((even, 0), (odd, 1)):
        pairs = [(i, i + 1) for i in range(first, size - 1, 2)]
        out.append(lax.ppermute(x, axes, pairs + [(j, i) for i, j in pairs]))
    return out


def body(tokens, w_qkv, w_out, q_saved, k_saved, v_saved, scale_exp, grad_out, crop_start):
    members, height, breadth, features = tokens.shape
    tall = height + 8
    packed = height + height // 2
    packed_columns = shape(members, packed, 8, features)
    strip = shape(3, members, 4, breadth, features)
    factor, *sides = call(
        edge_kernel,
        (
            shape(*scale_exp.shape[:3], 3 * features, dtype=f32),
            strip, strip, packed_columns, packed_columns,
        ),
        (scale_exp, k_saved, v_saved, tokens),
        scratch=(pltpu.VMEM(scale_exp.shape, jnp.int32),)
        + (pltpu.VMEM(tokens.shape, bf16),) * 3
        + (pltpu.SemaphoreType.DMA((1 + 3 * members,)),),
        far=(0, 1, 2, 3),
        limit=58 << 20,
    )
    halo_rows = exchange(*sides[0:2], "row")
    cells = members * height * breadth
    qs, gm, do = call(
        prepare_kernel,
        (shape(*tokens.shape),) * 3,
        (crop_start, q_saved, grad_out, factor, w_out),
        smem=(0,),
        flops=2 * cells * features * features,
    )
    halo_columns = exchange(*sides[2:4], COLS)
    corner = shape(members, 12, 8, features)
    corners = exchange(*call(corner_kernel, (corner, corner), halo_columns), "row")
    tiles = breadth // 8
    own_tiles = shape(members, tiles, height, 16, features)
    middle_tiles = shape(members, tiles, 16, 16, features, dtype=f32)
    middle_rows = shape(members, 8, breadth, features)
    kt, vt, dk, dv, out, dq = call(
        middle_kernel,
        (own_tiles, own_tiles, middle_tiles, middle_tiles, middle_rows, middle_rows),
        (qs, do, k_saved, v_saved, factor, *halo_columns),
        scratch=(pltpu.VMEM((tiles, 256, features // 2), f32),),
        flops=4 * cells * features * features,
        limit=20 << 20,
    )
    rows, pairs = lax.axis_size("row"), lax.axis_size("pair")
    deep, wide = features // rows, 4 * features // (2 * pairs)
    halo_tiles = pltpu.VMEM((2, members, tiles, 4, 16, features), bf16)
    all_tiles = pltpu.VMEM((members, tiles, tall, 16, features), f32)
    keep, send, dq, kv = call(
        main_kernel,
        (
            shape(rows, pairs, deep, wide),
            shape(rows, pairs, deep, wide),
            shape(members, tall, breadth, features),
            shape(members, tall, breadth + 8, 2 * features),
        ),
        (
            qs, do, kt, vt, dk, dv, out, dq, gm, tokens,
            *halo_columns, *halo_rows, *corners,
        ),
        scratch=(
            halo_tiles, halo_tiles, all_tiles, all_tiles,
            pltpu.VMEM(tokens.shape, bf16),
            pltpu.VMEM((members, tall, breadth + 8, features), bf16),
            pltpu.VMEM((features, 4 * features), f32),
            pltpu.VMEM((members, tall, breadth, features), bf16),
            pltpu.VMEM((members, tall, breadth + 8, 2 * features), bf16),
            pltpu.VMEM((2 * tiles, 256, features // 2), f32),
            pltpu.SemaphoreType.DMA((2,)),
        ),
        far_outs=(2, 3),
        flops=12 * cells * features * features,
        limit=37 << 20,
    )
    other = lax.ppermute(send, "core", [(0, 1), (1, 0)])
    both = call(add_kernel, shape(rows, pairs, deep, wide), (keep, other)).reshape(rows * pairs, deep, wide)
    parts = lax.all_to_all(both, ("row", "pair"), 0, 0, tiled=True)
    gt, *sides = call(
        token_kernel,
        (
            shape(members, tall, breadth, features),
            shape(members, tall // 2, 8, features),
            shape(members, tall // 2, 8, features),
        ),
        (kv, dq, w_qkv),
        flops=6 * cells * features * features,
        limit=20 << 20,
    )
    back_columns = exchange(*sides, COLS)
    halo = shape(members, 4, breadth, features)
    back_rows = exchange(*call(halo_kernel, (halo, halo), (gt, *back_columns)), "row")
    grad_tokens = call(
        join_kernel, shape(*tokens.shape), (gt, *back_columns, *back_rows)
    )
    total, square = call(
        total_kernel,
        (shape(deep, wide, dtype=f32), shape(2 * rows * pairs, wide, dtype=f32)),
        (parts,),
    )
    squares = lax.all_to_all(square, ("row", "pair", "core"), 0, 0, tiled=True)
    main = 3 * features // (2 * pairs)
    grad_qkv, grad_w_out = call(
        clip_kernel,
        (shape(deep, main, dtype=f32), shape(wide - main, deep, dtype=f32)),
        (total, squares),
    )
    return grad_tokens, grad_qkv, grad_w_out.T


def solution(mesh):
    rows, cols = mesh.devices.shape
    split = jax.sharding.Mesh(mesh.devices.reshape(rows, cols // 2, 2), ("row",) + COLS)
    cells = P(None, "row", COLS, None)
    return jax.shard_map(
        body,
        mesh=split,
        in_specs=(cells, P(), P(), cells, cells, cells, cells, cells, P()),
        out_specs=(cells, P("row", COLS), P("row", COLS)),
        check_vma=False,
    )
```

```python
import jax
import jax.numpy as jnp
from jax import lax
from jax.experimental import pallas as pl
from jax.experimental.pallas import tpu as pltpu
from jax.sharding import PartitionSpec as P

HEADS = 8
RADIUS = 4
BLOCK = 8
GROUP = 4

max_norm = 1000.0
masked_score = -1e30
tiny_square = 1e-06

f32 = jnp.float32
bf16 = jnp.bfloat16
VMEM = pl.BlockSpec(memory_space=pltpu.VMEM)
COLS = ("pair", "core")
ANY = pl.BlockSpec(memory_space=pltpu.HBM)
SMEM = pl.BlockSpec(memory_space=pltpu.SMEM)


def call(kernel, outs, ins, scratch=(), smem=(), far=(), far_outs=(), flops=0, limit=16 << 20):
    moved = sum(a.size * a.dtype.itemsize for a in list(ins) + jax.tree.leaves(outs))
    return pl.pallas_call(
        kernel,
        out_shape=outs,
        in_specs=[SMEM if n in smem else ANY if n in far else VMEM for n in range(len(ins))],
        out_specs=tuple(ANY if n in far_outs else VMEM for n in range(len(outs))) if isinstance(outs, tuple) else VMEM,
        scratch_shapes=list(scratch),
        compiler_params=pltpu.CompilerParams(vmem_limit_bytes=limit),
        cost_estimate=pl.CostEstimate(
            flops=flops, bytes_accessed=moved, transcendentals=0
        ),
    )(*ins)


def shape(*dims, dtype=bf16):
    return jax.ShapeDtypeStruct(dims, dtype)


def turn(x):
    return pltpu.roll(x, 4, 1)


def lower(x):
    return lax.broadcasted_iota(jnp.int32, x.shape, 1) < 4


def block_of(ref, fac_ref, part, b, i, j, rows, features):
    factor = fac_ref[b, i, j : j + 1, part * features : (part + 1) * features]
    return ref[b, rows, 8 * j : 8 * j + 8, :].astype(f32) * factor[None]


def even_column():
    return lax.axis_index("core") == 0


def even_row():
    return lax.rem(lax.axis_index("row"), 2) == 0


def swap(even, x, y):
    return jnp.where(even, x, y), jnp.where(even, y, x)


def row_kernel(scale_ref, k_ref, v_ref, tok_ref, fac_ref, re_ref, ro_ref, s_buf, buf, sem):
    members, height, breadth, features = k_ref.shape
    tiles = breadth // 8
    first = pltpu.make_async_copy(scale_ref, s_buf, sem.at[0])
    first.start()
    copies = [
        pltpu.make_async_copy(src.at[:, rows], buf.at[m, n], sem.at[1 + 2 * m + n])
        for m, src in enumerate((k_ref, v_ref, tok_ref))
        for n, rows in enumerate((slice(0, 4), slice(height - 4, height)))
    ]
    for c in copies:
        c.start()
    count = scale_ref.shape[3]
    per = 3 * features // count
    hot = (
        lax.broadcasted_iota(jnp.int32, (count, 3 * features), 0)
        == lax.broadcasted_iota(jnp.int32, (count, 3 * features), 1) // per
    ).astype(f32).astype(bf16)
    first.wait()
    for b in range(members):
        for i in range(height // 8):
            factor = jnp.exp2(s_buf[b, i].astype(f32)).astype(bf16)
            fac_ref[b, i] = jnp.dot(factor, hot, preferred_element_type=f32)
    for c in copies:
        c.wait()
    even = even_row()
    for b in range(members):
        for m in range(3):
            ends = []
            for n, i in enumerate((0, height // 8 - 1)):
                x = buf[m, n, b].astype(f32)
                if m < 2:
                    lanes = slice((m + 1) * features, (m + 2) * features)
                    x = jnp.concatenate(
                        [x[:, 8 * j : 8 * j + 8] * fac_ref[b, i, j : j + 1, lanes][None] for j in range(tiles)], 1
                    )
                ends.append(x)
            x, y = swap(even, ends[1], ends[0])
            re_ref[m, b], ro_ref[m, b] = x.astype(bf16), y.astype(bf16)


def column_kernel(fac_ref, k_ref, v_ref, tok_ref, ce_ref, co_ref, k_buf, v_buf, t_buf, sem):
    members, height, breadth, features = k_ref.shape
    tiles = breadth // 8
    copies = []
    for b in range(members):
        copies.append([
            pltpu.make_async_copy(src.at[b], dst.at[b], sem.at[3 * b + n])
            for n, (src, dst) in enumerate(((k_ref, k_buf), (v_ref, v_buf), (tok_ref, t_buf)))
        ])
        for c in copies[b]:
            c.start()
    half = height // 2
    even = even_column()
    for b in range(members):
        for c in copies[b]:
            c.wait()
        for i in range(height // 8):
            rows = slice(8 * i, 8 * i + 8)
            k = [block_of(k_buf, fac_ref, 1, b, i, j, rows, features) for j in (0, tiles - 1)]
            v = [block_of(v_buf, fac_ref, 2, b, i, j, rows, features) for j in (0, tiles - 1)]
            low = lower(k[0])
            left, right = jnp.where(low, k[0], turn(v[0])), jnp.where(low, turn(v[1]), k[1])
            x, y = swap(even, right, left)
            ce_ref[b, rows], co_ref[b, rows] = x.astype(bf16), y.astype(bf16)
        for r in range(0, half, 4):
            here, there = slice(r, r + 4), slice(half + r, half + r + 4)
            out = slice(height + r, height + r + 4)
            left, right = pack_columns(t_buf[b, here], t_buf[b, there])
            x, y = swap(even, right, left)
            ce_ref[b, out], co_ref[b, out] = x.astype(bf16), y.astype(bf16)


def pack_columns(one, two):
    last = one.shape[1] - 8
    x0, y0 = one[:, 0:8].astype(f32), two[:, 0:8].astype(f32)
    x1, y1 = one[:, last:].astype(f32), two[:, last:].astype(f32)
    low = lower(x0)
    return jnp.where(low, x0, turn(y0)), jnp.where(low, turn(y1), x1)


def corner_kernel(fe_ref, fo_ref, re_ref, ro_ref):
    members, packed = fe_ref.shape[:2]
    height = packed * 2 // 3
    half = height // 2
    even = even_row()
    for b in range(members):
        ends = []
        for n, row in enumerate((0, height - 4)):
            k, v = rims_of(fe_ref, fo_ref, b, slice(row, row + 4))
            first = height + (row if n == 0 else row - half)
            t = rims_of(fe_ref, fo_ref, b, slice(first, first + 4))[n]
            ends.append(jnp.concatenate([k, v, t], 0))
        x, y = swap(even, ends[1], ends[0])
        re_ref[b], ro_ref[b] = x.astype(bf16), y.astype(bf16)


def columns_of(fe_ref, fo_ref, b, rows):
    right, left = swap(even_column(), fe_ref[b, rows].astype(f32), fo_ref[b, rows].astype(f32))
    return left, right


def rims_of(fe_ref, fo_ref, b, rows):
    left, right = columns_of(fe_ref, fo_ref, b, rows)
    low = lower(left)
    return jnp.where(low, right, left), turn(jnp.where(low, left, right))


def prepare_kernel(crop_ref, q_ref, g_ref, fac_ref, w_ref, qs_ref, gm_ref, do_ref):
    members, height, breadth, features = q_ref.shape
    tiles = breadth // 8
    row0 = lax.axis_index("row") * height
    col0 = (lax.axis_index("pair") * 2 + lax.axis_index("core")) * breadth
    for b in range(members):
        for i in range(height // 8):
            rows = slice(8 * i, 8 * i + 8)
            parts = [block_of(q_ref, fac_ref, 0, b, i, j, rows, features) for j in range(tiles)]
            qs_ref[b, rows] = (jnp.concatenate(parts, 1) * 0.125).astype(bf16)
            g = g_ref[b, rows].astype(f32)
            r = lax.broadcasted_iota(jnp.int32, g.shape, 0) + (8 * i + row0)
            c = lax.broadcasted_iota(jnp.int32, g.shape, 1) + col0
            keep = (r >= crop_ref[b, 0]) & (c >= crop_ref[b, 1])
            gm = jnp.where(keep, g, 0.0).astype(bf16)
            gm_ref[b, rows] = gm
            do = lax.dot_general(
                gm.reshape(8 * breadth, features), w_ref[...], (((1,), (1,)), ((), ())),
                preferred_element_type=f32,
            )
            do_ref[b, rows] = do.astype(bf16).reshape(8, breadth, features)


def key_tile(blocks, rim, t):
    low = lower(rim)
    before = rim if t == 0 else blocks[t - 1]
    after = rim if t == len(blocks) - 1 else blocks[t + 1]
    return jnp.concatenate([blocks[t], jnp.where(low, after, before)], 1).astype(bf16)


def place_of(height, breadth):
    row0 = lax.axis_index("row") * height
    col0 = (lax.axis_index("pair") * 2 + lax.axis_index("core")) * breadth
    return row0, col0, height * lax.axis_size("row"), breadth * lax.axis_size("pair") * 2


def mask_biases(bias_ref, strips, tiles, place):
    row0, col0, frame_rows, frame_cols = place
    wide = bias_ref.shape[2]

    def key_cell(n):
        kn = lax.broadcasted_iota(jnp.int32, (256, n), 0)
        ks = kn % 16
        return kn // 16, jnp.where(ks < 12, ks, ks - 16)

    kr, kc = key_cell(wide)
    qn = lax.broadcasted_iota(jnp.int32, (256, wide), 1) % 64
    qr, qc = qn // 8, qn % 8
    seen = (kr >= qr) & (kr <= qr + 8) & (kc >= qc - 4) & (kc <= qc + 4)
    window = jnp.where(seen, 0.0, masked_score)
    kr, kc = key_cell(128)
    for n, i in enumerate(strips):
        for t in range(tiles):
            row, col = kr + (row0 + 8 * i - 4), kc + (col0 + 8 * t)
            inside = (row >= 0) & (row < frame_rows) & (col >= 0) & (col < frame_cols)
            edge = jnp.where(inside, 0.0, masked_score)
            bias_ref[n * tiles + t] = window + jnp.concatenate([edge] * (wide // 128), 1)


def attend(q, g, keys_of, bias_of, emit):
    features = q.shape[2]
    tiles = q.shape[1] // 8
    head_lanes = features // HEADS
    wide = GROUP * head_lanes
    lane = lax.broadcasted_iota(jnp.int32, (1, wide), 1) // head_lanes
    head_mask = [(lane == h).astype(f32).astype(bf16) for h in range(GROUP)]
    first = lax.broadcasted_iota(jnp.int32, (64, 2 * head_lanes), 1) < head_lanes

    def spread(x):
        return jnp.concatenate([x * m for m in head_mask], 0)

    def gather(x):
        parts = []
        for n in range(GROUP // 2):
            lanes = slice(128 * n, 128 * n + 128)
            parts.append(jnp.where(first, x[128 * n : 128 * n + 64, lanes], x[128 * n + 64 : 128 * n + 128, lanes]))
        return jnp.concatenate(parts, 1)

    def dot(x, y, left, right):
        return lax.dot_general(x, y, (((left,), (right,)), ((), ())), preferred_element_type=f32)

    groups = []
    for t in range(tiles):
        q64 = q[:, 8 * t : 8 * t + 8].reshape(64, features).astype(bf16)
        g64 = g[:, 8 * t : 8 * t + 8].reshape(64, features).astype(bf16)
        for n in range(HEADS // GROUP):
            lanes = slice(n * wide, (n + 1) * wide)
            k, v = keys_of(t, lanes)
            groups.append((t, lanes, spread(q64[:, lanes]), spread(g64[:, lanes]), k, v))
    scores = [dot(k, qx, 1, 1) + bias_of(t) for t, _, qx, _, k, _ in groups]
    grad_probs = [dot(v, gx, 1, 1) for _, _, _, gx, _, v in groups]
    halves = []
    for s, dp in zip(scores, grad_probs):
        w = jnp.exp(s - jnp.max(s, 0, keepdims=True))
        scale = 1.0 / jnp.sum(w, 0, keepdims=True)
        delta = jnp.sum(w * dp, 0, keepdims=True) * scale
        p = w * scale
        halves.append((p.astype(bf16), (p * (dp - delta)).astype(bf16)))
    outs, grads = [[] for _ in range(tiles)], [[] for _ in range(tiles)]
    for (t, lanes, qx, gx, k, v), (ph, ds) in zip(groups, halves):
        outs[t].append(gather(dot(ph, v, 0, 0)))
        grads[t].append(gather(dot(ds, k, 0, 0)) * 0.125)
        dk = dot(ds, qx, 1, 0).reshape(16, 16, wide)
        dv = dot(ph, gx, 1, 0).reshape(16, 16, wide)
        emit(t, lanes, dk, dv)
    join = lambda x: jnp.concatenate([jnp.concatenate(y, 1).reshape(8, 8, features) for y in x], 1)
    return join(outs), join(grads)


def middle_kernel(
    qs_ref, do_ref, k_ref, v_ref, fac_ref, fl_ref, fr_ref, kt_ref, vt_ref, dk_ref, dv_ref, o_ref, dq_ref, bias_ref
):
    members, height, breadth, features = qs_ref.shape
    strips, tiles = height // 8, breadth // 8
    mask_biases(bias_ref, (1,), tiles, place_of(height, breadth))
    for b in range(members):
        for i in range(strips):
            rows = slice(8 * i, 8 * i + 8)
            rims = rims_of(fl_ref, fr_ref, b, rows)
            for m, (ref, out) in enumerate(((k_ref, kt_ref), (v_ref, vt_ref))):
                blocks = [block_of(ref, fac_ref, m + 1, b, i, j, rows, features) for j in range(tiles)]
                for t in range(tiles):
                    out[b, t, rows] = key_tile(blocks, rims[m], t)

    def step(b, _):
        def keys_of(t, lanes):
            return tuple(ref[b, t, 4:20, :, lanes].reshape(256, -1) for ref in (kt_ref, vt_ref))

        def emit(t, lanes, dk, dv):
            dk_ref[b, t, :, :, lanes] = dk
            dv_ref[b, t, :, :, lanes] = dv

        o, dq = attend(qs_ref[b, 8:16].astype(f32), do_ref[b, 8:16].astype(f32), keys_of, lambda t: bias_ref[t], emit)
        o_ref[b] = o.astype(bf16)
        dq_ref[b] = dq.astype(bf16)
        return 0

    lax.fori_loop(0, members, step, 0)


def main_kernel(
    qs_ref, do_ref, kt_ref, vt_ref, dkm_ref, dvm_ref, om_ref, dqm_ref, gm_ref, tok_ref,
    fl_ref, fr_ref, he_ref, ho_ref, ke_ref, ko_ref,
    keep_ref, send_ref, dq_out, kv_out,
    kh_ref, vh_ref, dkt_ref, dvt_ref, o_ref, tp_ref, all_ref, dq_ref, kv_ref, bias_ref, sem,
):
    members, height, breadth, features = qs_ref.shape
    tall = height + 8
    tiles = breadth // 8
    mask_biases(bias_ref, (0, height // 8 - 1), tiles, place_of(height, breadth))
    even = even_row()
    for b in range(members):
        corners = swap(even, ke_ref[b].astype(f32), ko_ref[b].astype(f32))[::-1]
        strips = [swap(even, he_ref[m, b].astype(f32), ho_ref[m, b].astype(f32))[::-1] for m in range(3)]
        for n, corner in enumerate(corners):
            rims = [corner[4 * m : 4 * m + 4] for m in range(3)]
            for m, out in enumerate((kh_ref, vh_ref)):
                blocks = [strips[m][n][:, 8 * j : 8 * j + 8] for j in range(tiles)]
                for t in range(tiles):
                    out[n, b, t] = key_tile(blocks, rims[m], t)
            halo = slice(0, 4) if n == 0 else slice(tall - 4, tall)
            tp_ref[b, halo] = jnp.concatenate([strips[2][n], rims[2]], 1).astype(bf16)
            dq_ref[b, halo] = jnp.zeros((4, breadth, features), bf16)
        half = height // 2
        for r in range(0, half, 4):
            pair = rims_of(fl_ref, fr_ref, b, slice(height + r, height + r + 4))
            for rim, row in zip(pair, (r, half + r)):
                own = tok_ref[b, row : row + 4].astype(f32)
                tp_ref[b, row + 4 : row + 8] = jnp.concatenate([own, rim], 1).astype(bf16)
        o_ref[b, 8:16] = om_ref[b]
        dq_ref[b, 12:20] = dqm_ref[b]

    def step(b, _):
        for n, i in enumerate((0, height // 8 - 1)):
            def keys_of(t, lanes):
                parts = []
                for ref, halo in ((kt_ref, kh_ref), (vt_ref, vh_ref)):
                    rim = halo[n, b, t, :, :, lanes]
                    own = ref[b, t, slice(0, 12) if n == 0 else slice(height - 12, height), :, lanes]
                    both = [rim, own] if n == 0 else [own, rim]
                    parts.append(jnp.concatenate(both, 0).reshape(256, -1))
                return tuple(parts)

            def emit(t, lanes, dk, dv):
                for ref, mid, x in ((dkt_ref, dkm_ref, dk), (dvt_ref, dvm_ref, dv)):
                    if n == 0:
                        ref[b, t, 0:8, :, lanes] = x[0:8]
                        ref[b, t, 8:16, :, lanes] = x[8:16] + mid[b, t, 0:8, :, lanes]
                    else:
                        ref[b, t, 16:24, :, lanes] = x[0:8] + mid[b, t, 8:16, :, lanes]
                        ref[b, t, 24:32, :, lanes] = x[8:16]

            rows = slice(8 * i, 8 * i + 8)
            o, dq = attend(qs_ref[b, rows].astype(f32), do_ref[b, rows].astype(f32), keys_of, lambda t: bias_ref[n * tiles + t], emit)
            o_ref[b, rows] = o.astype(bf16)
            dq_ref[b, 8 * i + 4 : 8 * i + 12] = dq.astype(bf16)
        return 0

    lax.fori_loop(0, members, step, 0)

    for b in range(members):
        for r in range(0, tall, 8):
            rows = slice(r, r + 8)
            for m, ref in enumerate((dkt_ref, dvt_ref)):
                rim = [ref[b, t, rows, 8:16] for t in range(tiles)]
                low = lower(rim[0])
                own = []
                for t in range(tiles):
                    x = ref[b, t, rows, 0:8]
                    if t > 0:
                        x = x + jnp.where(low, rim[t - 1], 0.0)
                    if t < tiles - 1:
                        x = x + jnp.where(low, 0.0, rim[t + 1])
                    own.append(x)
                own.append(jnp.where(low, rim[tiles - 1], rim[0]))
                kv_ref[b, rows, :, m * features : (m + 1) * features] = jnp.concatenate(own, 1).astype(bf16)

    copies = [
        pltpu.make_async_copy(src, dst, sem.at[n])
        for n, (src, dst) in enumerate(
            (x.at[b], y.at[b]) for x, y in ((dq_ref, dq_out), (kv_ref, kv_out)) for b in range(members)
        )
    ]
    for c in copies:
        c.start()
    down = (((0,), (0,)), ((), ()))
    cells = members * height * breadth
    padded = members * tall * (breadth + 8)
    for b in range(members):
        x = lax.dot_general(
            tok_ref[b].reshape(cells // members, features),
            dq_ref[b, 4 : tall - 4].reshape(cells // members, features), down,
            preferred_element_type=f32,
        )
        y = lax.dot_general(
            o_ref[b].reshape(cells // members, features), gm_ref[b].reshape(cells // members, features), down,
            preferred_element_type=f32,
        )
        if b:
            x, y = x + all_ref[:, 0:features], y + all_ref[:, 3 * features :]
        all_ref[:, 0:features] = x
        all_ref[:, 3 * features :] = y
    kv = kv_ref[...].reshape(padded, 2 * features)
    all_ref[:, features : 3 * features] = lax.dot_general(
        tp_ref[...].reshape(padded, features), kv, down, preferred_element_type=f32
    )

    deep_rows, pairs, deep, broad = keep_ref.shape
    count = 2 * pairs
    main, rest = 3 * features // count, features // count
    lanes = lax.broadcasted_iota(jnp.int32, (features, broad), 1)

    def window(start, end):
        base, off = start // broad * broad, start % broad
        x = all_ref[:, base : base + broad]
        if off:
            x = pltpu.roll(x, broad - off, 1)
        if end > base + broad:
            y = pltpu.roll(all_ref[:, base + broad : base + 2 * broad], broad - off, 1)
            x = jnp.where(lanes < broad - off, x, y)
        return x

    def block(c):
        x = window(main * c, main * (c + 1))
        base, off = 3 * features + rest * c // broad * broad, rest * c % broad
        y = all_ref[:, base : base + broad]
        if off != main:
            y = pltpu.roll(y, (main - off) % broad, 1)
        return jnp.where(lanes < main, x, y).astype(bf16).reshape(deep_rows, deep, broad)

    mine = lax.axis_index("core") == 0
    for p in range(pairs):
        even, odd = block(2 * p), block(2 * p + 1)
        keep_ref[:, p] = jnp.where(mine, even, odd)
        send_ref[:, p] = jnp.where(mine, odd, even)
    for c in copies:
        c.wait()


def token_kernel(kv_ref, dq_ref, w_ref, gt_ref, ce_ref, co_ref):
    members, tall, breadth, features = dq_ref.shape
    across = (((1,), (1,)), ((), ()))
    middle = tall // 2
    for b in range(members):
        y = lax.dot_general(
            kv_ref[b].reshape(tall * (breadth + 8), 2 * features), w_ref[:, features:], across,
            preferred_element_type=f32,
        ).reshape(tall, breadth + 8, features)
        z = lax.dot_general(
            dq_ref[b].reshape(tall * breadth, features), w_ref[:, 0:features], across,
            preferred_element_type=f32,
        ).reshape(tall, breadth, features)
        gt_ref[b] = (y[:, 0:breadth] + z).astype(bf16)
        here, there = y[0:middle, breadth:], turn(y[middle:, breadth:])
        low = lower(here)
        x, y = swap(even_column(), jnp.where(low, here, there), jnp.where(low, there, here))
        ce_ref[b], co_ref[b] = x.astype(bf16), y.astype(bf16)


def back_rims(fl, fr):
    low = lower(fl)
    here = (jnp.where(low, fl, 0.0), jnp.where(low, 0.0, fr))
    there = (jnp.where(low, turn(fl), 0.0), jnp.where(low, 0.0, turn(fr)))
    return here, there


def plus_rims(x, rims):
    last = x.shape[1] - 8
    return jnp.concatenate([x[:, 0:8] + rims[0], x[:, 8:last], x[:, last:] + rims[1]], 1) if last > 8 else (
        jnp.concatenate([x[:, 0:8] + rims[0], x[:, 8:] + rims[1]], 1)
    )


def add_kernel(x_ref, y_ref, sum_ref):
    sum_ref[...] = (x_ref[...].astype(f32) + y_ref[...].astype(f32)).astype(bf16)


def total_kernel(x_ref, sum_ref, square_ref):
    x = jnp.sum(x_ref[...].astype(f32), 0)
    sum_ref[...] = x
    square = jnp.sum(x * x, 0, keepdims=True)
    square_ref[...] = jnp.broadcast_to(square, square_ref.shape)


def halo_kernel(gt_ref, fe_ref, fo_ref, re_ref, ro_ref):
    members, tall = gt_ref.shape[:2]
    half = tall // 2
    for b in range(members):
        here, _ = back_rims(*columns_of(fe_ref, fo_ref, b, slice(0, 4)))
        _, there = back_rims(*columns_of(fe_ref, fo_ref, b, slice(half - 4, half)))
        up = plus_rims(gt_ref[b, 0:4].astype(f32), here)
        down = plus_rims(gt_ref[b, tall - 4 : tall].astype(f32), there)
        x, y = swap(even_row(), down, up)
        re_ref[b], ro_ref[b] = x.astype(bf16), y.astype(bf16)


def join_kernel(gt_ref, fe_ref, fo_ref, he_ref, ho_ref, tok_ref):
    members, height = tok_ref.shape[:2]
    half = (height + 8) // 2
    for b in range(members):
        bottom, top = swap(even_row(), he_ref[b].astype(f32), ho_ref[b].astype(f32))
        for r in range(0, half, 4):
            pair = back_rims(*columns_of(fe_ref, fo_ref, b, slice(r, r + 4)))
            for rims, row in zip(pair, (r, half + r)):
                if row == 0 or row == height + 4:
                    continue
                y = plus_rims(gt_ref[b, row : row + 4].astype(f32), rims)
                if row == 4:
                    y = y + top
                if row == height:
                    y = y + bottom
                tok_ref[b, row - 4 : row] = y.astype(bf16)


def clip_kernel(x_ref, square_ref, qkv_ref, out_ref):
    total = jnp.sum(jnp.sum(square_ref[...], 0, keepdims=True), 1, keepdims=True)
    clip = jnp.minimum(1.0, max_norm / jnp.sqrt(total + tiny_square))
    x = x_ref[...] * clip
    main = qkv_ref.shape[1]
    qkv_ref[...] = x[:, 0:main]
    out_ref[...] = x.T[main:]


def exchange(even, odd, axes):
    size = lax.axis_size(axes)
    out = []
    for x, first in ((even, 0), (odd, 1)):
        pairs = [(i, i + 1) for i in range(first, size - 1, 2)]
        out.append(lax.ppermute(x, axes, pairs + [(j, i) for i, j in pairs]))
    return out


def body(tokens, w_qkv, w_out, q_saved, k_saved, v_saved, scale_exp, grad_out, crop_start):
    members, height, breadth, features = tokens.shape
    tall = height + 8
    packed = height + height // 2
    packed_columns = shape(members, packed, 8, features)
    strip = shape(3, members, 4, breadth, features)
    factor, *sides = call(
        row_kernel,
        (shape(*scale_exp.shape[:3], 3 * features, dtype=f32), strip, strip),
        (scale_exp, k_saved, v_saved, tokens),
        scratch=(
            pltpu.VMEM(scale_exp.shape, jnp.int32),
            pltpu.VMEM((3, 2, members, 4, breadth, features), bf16),
            pltpu.SemaphoreType.DMA((7,)),
        ),
        far=(0, 1, 2, 3),
        limit=58 << 20,
    )
    halo_rows = exchange(*sides, "row")
    sides = call(
        column_kernel,
        (packed_columns, packed_columns),
        (factor, k_saved, v_saved, tokens),
        scratch=(pltpu.VMEM(tokens.shape, bf16),) * 3 + (pltpu.SemaphoreType.DMA((3 * members,)),),
        far=(1, 2, 3),
        limit=58 << 20,
    )
    cells = members * height * breadth
    qs, gm, do = call(
        prepare_kernel,
        (shape(*tokens.shape),) * 3,
        (crop_start, q_saved, grad_out, factor, w_out),
        smem=(0,),
        flops=200 * cells * features * features,
    )
    *halo_columns, do = lax.optimization_barrier((*exchange(*sides, COLS), do))
    corner = shape(members, 12, 8, features)
    corners = exchange(*call(corner_kernel, (corner, corner), halo_columns), "row")
    tiles = breadth // 8
    own_tiles = shape(members, tiles, height, 16, features)
    middle_tiles = shape(members, tiles, 16, 16, features, dtype=f32)
    middle_rows = shape(members, 8, breadth, features)
    kt, vt, dk, dv, out, dq = call(
        middle_kernel,
        (own_tiles, own_tiles, middle_tiles, middle_tiles, middle_rows, middle_rows),
        (qs, do, k_saved, v_saved, factor, *halo_columns),
        scratch=(pltpu.VMEM((tiles, 256, features // 2), f32),),
        flops=4 * cells * features * features,
        limit=20 << 20,
    )
    rows, pairs = lax.axis_size("row"), lax.axis_size("pair")
    deep, wide = features // rows, 4 * features // (2 * pairs)
    halo_tiles = pltpu.VMEM((2, members, tiles, 4, 16, features), bf16)
    all_tiles = pltpu.VMEM((members, tiles, tall, 16, features), f32)
    keep, send, dq, kv = call(
        main_kernel,
        (
            shape(rows, pairs, deep, wide),
            shape(rows, pairs, deep, wide),
            shape(members, tall, breadth, features),
            shape(members, tall, breadth + 8, 2 * features),
        ),
        (
            qs, do, kt, vt, dk, dv, out, dq, gm, tokens,
            *halo_columns, *halo_rows, *corners,
        ),
        scratch=(
            halo_tiles, halo_tiles, all_tiles, all_tiles,
            pltpu.VMEM(tokens.shape, bf16),
            pltpu.VMEM((members, tall, breadth + 8, features), bf16),
            pltpu.VMEM((features, 4 * features), f32),
            pltpu.VMEM((members, tall, breadth, features), bf16),
            pltpu.VMEM((members, tall, breadth + 8, 2 * features), bf16),
            pltpu.VMEM((2 * tiles, 256, features // 2), f32),
            pltpu.SemaphoreType.DMA((2 * members,)),
        ),
        far_outs=(2, 3),
        flops=12 * cells * features * features,
        limit=37 << 20,
    )
    other = lax.ppermute(send, "core", [(0, 1), (1, 0)])
    both = call(add_kernel, shape(rows, pairs, deep, wide), (keep, other)).reshape(rows * pairs, deep, wide)
    parts = lax.all_to_all(both, ("row", "pair"), 0, 0, tiled=True)
    gt, *sides = call(
        token_kernel,
        (
            shape(members, tall, breadth, features),
            shape(members, tall // 2, 8, features),
            shape(members, tall // 2, 8, features),
        ),
        (kv, dq, w_qkv),
        flops=6 * cells * features * features,
        limit=20 << 20,
    )
    back_columns = exchange(*sides, COLS)
    halo = shape(members, 4, breadth, features)
    back_rows = exchange(*call(halo_kernel, (halo, halo), (gt, *back_columns)), "row")
    grad_tokens = call(
        join_kernel, shape(*tokens.shape), (gt, *back_columns, *back_rows)
    )
    total, square = call(
        total_kernel,
        (shape(deep, wide, dtype=f32), shape(2 * rows * pairs, wide, dtype=f32)),
        (parts,),
    )
    squares = lax.all_to_all(square, ("row", "pair", "core"), 0, 0, tiled=True)
    main = 3 * features // (2 * pairs)
    grad_qkv, grad_w_out = call(
        clip_kernel,
        (shape(deep, main, dtype=f32), shape(wide - main, deep, dtype=f32)),
        (total, squares),
    )
    return grad_tokens, grad_qkv, grad_w_out.T


def solution(mesh):
    rows, cols = mesh.devices.shape
    split = jax.sharding.Mesh(mesh.devices.reshape(rows, cols // 2, 2), ("row",) + COLS)
    cells = P(None, "row", COLS, None)
    return jax.shard_map(
        body,
        mesh=split,
        in_specs=(cells, P(), P(), cells, cells, cells, cells, cells, P()),
        out_specs=(cells, P("row", COLS), P("row", COLS)),
        check_vma=False,
    )
```

```python
import jax
import jax.numpy as jnp
from jax import lax
from jax.experimental import pallas as pl
from jax.experimental.pallas import tpu as pltpu
from jax.sharding import PartitionSpec as P

HEADS = 8
RADIUS = 4
BLOCK = 8
GROUP = 4

max_norm = 1000.0
masked_score = -1e30
tiny_square = 1e-06

f32 = jnp.float32
bf16 = jnp.bfloat16
VMEM = pl.BlockSpec(memory_space=pltpu.VMEM)
COLS = ("pair", "core")
ANY = pl.BlockSpec(memory_space=pltpu.HBM)
SMEM = pl.BlockSpec(memory_space=pltpu.SMEM)


def call(kernel, outs, ins, scratch=(), smem=(), far=(), far_outs=(), flops=0, limit=16 << 20):
    moved = sum(a.size * a.dtype.itemsize for a in list(ins) + jax.tree.leaves(outs))
    return pl.pallas_call(
        kernel,
        out_shape=outs,
        in_specs=[SMEM if n in smem else ANY if n in far else VMEM for n in range(len(ins))],
        out_specs=tuple(ANY if n in far_outs else VMEM for n in range(len(outs))) if isinstance(outs, tuple) else VMEM,
        scratch_shapes=list(scratch),
        compiler_params=pltpu.CompilerParams(vmem_limit_bytes=limit),
        cost_estimate=pl.CostEstimate(
            flops=flops, bytes_accessed=moved, transcendentals=0
        ),
    )(*ins)


def shape(*dims, dtype=bf16):
    return jax.ShapeDtypeStruct(dims, dtype)


def turn(x):
    return pltpu.roll(x, 4, 1)


def lower(x):
    return lax.broadcasted_iota(jnp.int32, x.shape, 1) < 4


def block_of(ref, fac_ref, part, b, i, j, rows, features):
    factor = fac_ref[b, i, j : j + 1, part * features : (part + 1) * features]
    return ref[b, rows, 8 * j : 8 * j + 8, :].astype(f32) * factor[None]


def even_column():
    return lax.axis_index("core") == 0


def even_row():
    return lax.rem(lax.axis_index("row"), 2) == 0


def swap(even, x, y):
    return jnp.where(even, x, y), jnp.where(even, y, x)


def edge_kernel(
    scale_ref, k_ref, v_ref, tok_ref, fac_ref, ro_ref, re_ref, co_ref, ce_ref, s_buf, k_buf, v_buf, t_buf, sem
):
    members, height, breadth, features = k_ref.shape
    tiles = breadth // 8
    first = pltpu.make_async_copy(scale_ref, s_buf, sem.at[0])
    first.start()
    copies = []
    for b in range(members):
        copies.append([
            pltpu.make_async_copy(src.at[b], dst.at[b], sem.at[1 + 3 * b + n])
            for n, (src, dst) in enumerate(((k_ref, k_buf), (v_ref, v_buf), (tok_ref, t_buf)))
        ])
        for c in copies[b]:
            c.start()
    count = scale_ref.shape[3]
    per = 3 * features // count
    hot = (
        lax.broadcasted_iota(jnp.int32, (count, 3 * features), 0)
        == lax.broadcasted_iota(jnp.int32, (count, 3 * features), 1) // per
    ).astype(f32).astype(bf16)
    first.wait()
    for b in range(members):
        for i in range(height // 8):
            factor = jnp.exp2(s_buf[b, i].astype(f32)).astype(bf16)
            fac_ref[b, i] = jnp.dot(factor, hot, preferred_element_type=f32)
    half, last = height // 2, height // 8 - 1
    even_c, even_r = even_column(), even_row()
    for b in range(members):
        for c in copies[b]:
            c.wait()
        ends = {}
        for i in range(last + 1):
            rows = slice(8 * i, 8 * i + 8)
            k = [block_of(k_buf, fac_ref, 1, b, i, j, rows, features) for j in range(tiles)]
            v = [block_of(v_buf, fac_ref, 2, b, i, j, rows, features) for j in range(tiles)]
            low = lower(k[0])
            left, right = jnp.where(low, k[0], turn(v[0])), jnp.where(low, turn(v[-1]), k[-1])
            x, y = swap(even_c, right, left)
            ce_ref[b, rows], co_ref[b, rows] = x.astype(bf16), y.astype(bf16)
            for m, parts in enumerate((k, v)):
                if i == 0:
                    ends[m, 0] = jnp.concatenate(parts, 1)[0:4]
                if i == last:
                    ends[m, 1] = jnp.concatenate(parts, 1)[4:8]
        ends[2, 0], ends[2, 1] = t_buf[b, 0:4].astype(f32), t_buf[b, height - 4 : height].astype(f32)
        for m in range(3):
            x, y = swap(even_r, ends[m, 1], ends[m, 0])
            re_ref[m, b], ro_ref[m, b] = x.astype(bf16), y.astype(bf16)
        for r in range(0, half, 4):
            here, there = slice(r, r + 4), slice(half + r, half + r + 4)
            out = slice(height + r, height + r + 4)
            left, right = pack_columns(t_buf[b, here], t_buf[b, there])
            x, y = swap(even_c, right, left)
            ce_ref[b, out], co_ref[b, out] = x.astype(bf16), y.astype(bf16)


def pack_columns(one, two):
    last = one.shape[1] - 8
    x0, y0 = one[:, 0:8].astype(f32), two[:, 0:8].astype(f32)
    x1, y1 = one[:, last:].astype(f32), two[:, last:].astype(f32)
    low = lower(x0)
    return jnp.where(low, x0, turn(y0)), jnp.where(low, turn(y1), x1)


def corner_kernel(fo_ref, fe_ref, ro_ref, re_ref):
    members, packed = fe_ref.shape[:2]
    height = packed * 2 // 3
    half = height // 2
    even = even_row()
    for b in range(members):
        ends = []
        for n, row in enumerate((0, height - 4)):
            k, v = rims_of(fe_ref, fo_ref, b, slice(row, row + 4))
            first = height + (row if n == 0 else row - half)
            t = rims_of(fe_ref, fo_ref, b, slice(first, first + 4))[n]
            ends.append(jnp.concatenate([k, v, t], 0))
        x, y = swap(even, ends[1], ends[0])
        re_ref[b], ro_ref[b] = x.astype(bf16), y.astype(bf16)


def columns_of(fe_ref, fo_ref, b, rows):
    right, left = swap(even_column(), fe_ref[b, rows].astype(f32), fo_ref[b, rows].astype(f32))
    return left, right


def rims_of(fe_ref, fo_ref, b, rows):
    left, right = columns_of(fe_ref, fo_ref, b, rows)
    low = lower(left)
    return jnp.where(low, right, left), turn(jnp.where(low, left, right))


def prepare_kernel(crop_ref, q_ref, g_ref, fac_ref, w_ref, qs_ref, gm_ref, do_ref):
    members, height, breadth, features = q_ref.shape
    tiles = breadth // 8
    row0 = lax.axis_index("row") * height
    col0 = (lax.axis_index("pair") * 2 + lax.axis_index("core")) * breadth
    for b in range(members):
        for i in range(height // 8):
            rows = slice(8 * i, 8 * i + 8)
            parts = [block_of(q_ref, fac_ref, 0, b, i, j, rows, features) for j in range(tiles)]
            qs_ref[b, rows] = (jnp.concatenate(parts, 1) * 0.125).astype(bf16)
            g = g_ref[b, rows].astype(f32)
            r = lax.broadcasted_iota(jnp.int32, g.shape, 0) + (8 * i + row0)
            c = lax.broadcasted_iota(jnp.int32, g.shape, 1) + col0
            keep = (r >= crop_ref[b, 0]) & (c >= crop_ref[b, 1])
            gm = jnp.where(keep, g, 0.0).astype(bf16)
            gm_ref[b, rows] = gm
            do = lax.dot_general(
                gm.reshape(8 * breadth, features), w_ref[...], (((1,), (1,)), ((), ())),
                preferred_element_type=f32,
            )
            do_ref[b, rows] = do.astype(bf16).reshape(8, breadth, features)


def key_tile(blocks, rim, t):
    low = lower(rim)
    before = rim if t == 0 else blocks[t - 1]
    after = rim if t == len(blocks) - 1 else blocks[t + 1]
    return jnp.concatenate([blocks[t], jnp.where(low, after, before)], 1).astype(bf16)


def place_of(height, breadth):
    row0 = lax.axis_index("row") * height
    col0 = (lax.axis_index("pair") * 2 + lax.axis_index("core")) * breadth
    return row0, col0, height * lax.axis_size("row"), breadth * lax.axis_size("pair") * 2


def mask_biases(bias_ref, strips, tiles, place):
    row0, col0, frame_rows, frame_cols = place
    wide = bias_ref.shape[2]

    def key_cell(n):
        kn = lax.broadcasted_iota(jnp.int32, (256, n), 0)
        ks = kn % 16
        return kn // 16, jnp.where(ks < 12, ks, ks - 16)

    kr, kc = key_cell(wide)
    qn = lax.broadcasted_iota(jnp.int32, (256, wide), 1) % 64
    qr, qc = qn // 8, qn % 8
    seen = (kr >= qr) & (kr <= qr + 8) & (kc >= qc - 4) & (kc <= qc + 4)
    window = jnp.where(seen, 0.0, masked_score)
    kr, kc = key_cell(128)
    for n, i in enumerate(strips):
        for t in range(tiles):
            row, col = kr + (row0 + 8 * i - 4), kc + (col0 + 8 * t)
            inside = (row >= 0) & (row < frame_rows) & (col >= 0) & (col < frame_cols)
            edge = jnp.where(inside, 0.0, masked_score)
            bias_ref[n * tiles + t] = window + jnp.concatenate([edge] * (wide // 128), 1)


def attend(q, g, keys_of, bias_of, emit):
    features = q.shape[2]
    tiles = q.shape[1] // 8
    head_lanes = features // HEADS
    wide = GROUP * head_lanes
    lane = lax.broadcasted_iota(jnp.int32, (1, wide), 1) // head_lanes
    head_mask = [(lane == h).astype(f32).astype(bf16) for h in range(GROUP)]
    first = lax.broadcasted_iota(jnp.int32, (64, 2 * head_lanes), 1) < head_lanes

    def spread(x):
        return jnp.concatenate([x * m for m in head_mask], 0)

    def gather(x):
        parts = []
        for n in range(GROUP // 2):
            lanes = slice(128 * n, 128 * n + 128)
            parts.append(jnp.where(first, x[128 * n : 128 * n + 64, lanes], x[128 * n + 64 : 128 * n + 128, lanes]))
        return jnp.concatenate(parts, 1)

    def dot(x, y, left, right):
        return lax.dot_general(x, y, (((left,), (right,)), ((), ())), preferred_element_type=f32)

    groups = []
    for t in range(tiles):
        q64 = q[:, 8 * t : 8 * t + 8].reshape(64, features).astype(bf16)
        g64 = g[:, 8 * t : 8 * t + 8].reshape(64, features).astype(bf16)
        for n in range(HEADS // GROUP):
            lanes = slice(n * wide, (n + 1) * wide)
            k, v = keys_of(t, lanes)
            groups.append((t, lanes, spread(q64[:, lanes]), spread(g64[:, lanes]), k, v))
    scores = [dot(k, qx, 1, 1) + bias_of(t) for t, _, qx, _, k, _ in groups]
    grad_probs = [dot(v, gx, 1, 1) for _, _, _, gx, _, v in groups]
    halves = []
    for s, dp in zip(scores, grad_probs):
        w = jnp.exp(s - jnp.max(s, 0, keepdims=True))
        scale = 1.0 / jnp.sum(w, 0, keepdims=True)
        delta = jnp.sum(w * dp, 0, keepdims=True) * scale
        p = w * scale
        halves.append((p.astype(bf16), (p * (dp - delta)).astype(bf16)))
    outs, grads = [[] for _ in range(tiles)], [[] for _ in range(tiles)]
    for (t, lanes, qx, gx, k, v), (ph, ds) in zip(groups, halves):
        outs[t].append(gather(dot(ph, v, 0, 0)))
        grads[t].append(gather(dot(ds, k, 0, 0)) * 0.125)
        dk = dot(ds, qx, 1, 0).reshape(16, 16, wide)
        dv = dot(ph, gx, 1, 0).reshape(16, 16, wide)
        emit(t, lanes, dk, dv)
    join = lambda x: jnp.concatenate([jnp.concatenate(y, 1).reshape(8, 8, features) for y in x], 1)
    return join(outs), join(grads)


def middle_kernel(
    qs_ref, do_ref, k_ref, v_ref, fac_ref, fr_ref, fl_ref, kt_ref, vt_ref, dk_ref, dv_ref, o_ref, dq_ref, bias_ref
):
    members, height, breadth, features = qs_ref.shape
    strips, tiles = height // 8, breadth // 8
    mask_biases(bias_ref, (1,), tiles, place_of(height, breadth))
    for b in range(members):
        for i in range(strips):
            rows = slice(8 * i, 8 * i + 8)
            rims = rims_of(fl_ref, fr_ref, b, rows)
            for m, (ref, out) in enumerate(((k_ref, kt_ref), (v_ref, vt_ref))):
                blocks = [block_of(ref, fac_ref, m + 1, b, i, j, rows, features) for j in range(tiles)]
                for t in range(tiles):
                    out[b, t, rows] = key_tile(blocks, rims[m], t)

    def step(b, _):
        def keys_of(t, lanes):
            return tuple(ref[b, t, 4:20, :, lanes].reshape(256, -1) for ref in (kt_ref, vt_ref))

        def emit(t, lanes, dk, dv):
            dk_ref[b, t, :, :, lanes] = dk
            dv_ref[b, t, :, :, lanes] = dv

        o, dq = attend(qs_ref[b, 8:16].astype(f32), do_ref[b, 8:16].astype(f32), keys_of, lambda t: bias_ref[t], emit)
        o_ref[b] = o.astype(bf16)
        dq_ref[b] = dq.astype(bf16)
        return 0

    lax.fori_loop(0, members, step, 0)


def main_kernel(
    qs_ref, do_ref, kt_ref, vt_ref, dkm_ref, dvm_ref, om_ref, dqm_ref, gm_ref, tok_ref,
    fr_ref, fl_ref, ho_ref, he_ref, ko_ref, ke_ref,
    keep_ref, send_ref, dq_out, kv_out,
    kh_ref, vh_ref, dkt_ref, dvt_ref, o_ref, tp_ref, all_ref, dq_ref, kv_ref, bias_ref, sem,
):
    members, height, breadth, features = qs_ref.shape
    tall = height + 8
    tiles = breadth // 8
    mask_biases(bias_ref, (0, height // 8 - 1), tiles, place_of(height, breadth))
    even = even_row()
    for b in range(members):
        corners = swap(even, ke_ref[b].astype(f32), ko_ref[b].astype(f32))[::-1]
        strips = [swap(even, he_ref[m, b].astype(f32), ho_ref[m, b].astype(f32))[::-1] for m in range(3)]
        for n, corner in enumerate(corners):
            rims = [corner[4 * m : 4 * m + 4] for m in range(3)]
            for m, out in enumerate((kh_ref, vh_ref)):
                blocks = [strips[m][n][:, 8 * j : 8 * j + 8] for j in range(tiles)]
                for t in range(tiles):
                    out[n, b, t] = key_tile(blocks, rims[m], t)
            halo = slice(0, 4) if n == 0 else slice(tall - 4, tall)
            tp_ref[b, halo] = jnp.concatenate([strips[2][n], rims[2]], 1).astype(bf16)
            dq_ref[b, halo] = jnp.zeros((4, breadth, features), bf16)
        half = height // 2
        for r in range(0, half, 4):
            pair = rims_of(fl_ref, fr_ref, b, slice(height + r, height + r + 4))
            for rim, row in zip(pair, (r, half + r)):
                own = tok_ref[b, row : row + 4].astype(f32)
                tp_ref[b, row + 4 : row + 8] = jnp.concatenate([own, rim], 1).astype(bf16)
        o_ref[b, 8:16] = om_ref[b]
        dq_ref[b, 12:20] = dqm_ref[b]

    def step(b, _):
        for n, i in enumerate((0, height // 8 - 1)):
            def keys_of(t, lanes):
                parts = []
                for ref, halo in ((kt_ref, kh_ref), (vt_ref, vh_ref)):
                    rim = halo[n, b, t, :, :, lanes]
                    own = ref[b, t, slice(0, 12) if n == 0 else slice(height - 12, height), :, lanes]
                    both = [rim, own] if n == 0 else [own, rim]
                    parts.append(jnp.concatenate(both, 0).reshape(256, -1))
                return tuple(parts)

            def emit(t, lanes, dk, dv):
                for ref, mid, x in ((dkt_ref, dkm_ref, dk), (dvt_ref, dvm_ref, dv)):
                    if n == 0:
                        ref[b, t, 0:8, :, lanes] = x[0:8]
                        ref[b, t, 8:16, :, lanes] = x[8:16] + mid[b, t, 0:8, :, lanes]
                    else:
                        ref[b, t, 16:24, :, lanes] = x[0:8] + mid[b, t, 8:16, :, lanes]
                        ref[b, t, 24:32, :, lanes] = x[8:16]

            rows = slice(8 * i, 8 * i + 8)
            o, dq = attend(qs_ref[b, rows].astype(f32), do_ref[b, rows].astype(f32), keys_of, lambda t: bias_ref[n * tiles + t], emit)
            o_ref[b, rows] = o.astype(bf16)
            dq_ref[b, 8 * i + 4 : 8 * i + 12] = dq.astype(bf16)
        return 0

    lax.fori_loop(0, members, step, 0)

    for b in range(members):
        for r in range(0, tall, 8):
            rows = slice(r, r + 8)
            for m, ref in enumerate((dkt_ref, dvt_ref)):
                rim = [ref[b, t, rows, 8:16] for t in range(tiles)]
                low = lower(rim[0])
                own = []
                for t in range(tiles):
                    x = ref[b, t, rows, 0:8]
                    if t > 0:
                        x = x + jnp.where(low, rim[t - 1], 0.0)
                    if t < tiles - 1:
                        x = x + jnp.where(low, 0.0, rim[t + 1])
                    own.append(x)
                own.append(jnp.where(low, rim[tiles - 1], rim[0]))
                kv_ref[b, rows, :, m * features : (m + 1) * features] = jnp.concatenate(own, 1).astype(bf16)

    copies = [
        pltpu.make_async_copy(src, dst, sem.at[n])
        for n, (src, dst) in enumerate(
            (x.at[b], y.at[b]) for x, y in ((dq_ref, dq_out), (kv_ref, kv_out)) for b in range(members)
        )
    ]
    for c in copies:
        c.start()
    down = (((0,), (0,)), ((), ()))
    cells = members * height * breadth
    padded = members * tall * (breadth + 8)
    for b in range(members):
        x = lax.dot_general(
            tok_ref[b].reshape(cells // members, features),
            dq_ref[b, 4 : tall - 4].reshape(cells // members, features), down,
            preferred_element_type=f32,
        )
        y = lax.dot_general(
            o_ref[b].reshape(cells // members, features), gm_ref[b].reshape(cells // members, features), down,
            preferred_element_type=f32,
        )
        if b:
            x, y = x + all_ref[:, 0:features], y + all_ref[:, 3 * features :]
        all_ref[:, 0:features] = x
        all_ref[:, 3 * features :] = y
    kv = kv_ref[...].reshape(padded, 2 * features)
    all_ref[:, features : 3 * features] = lax.dot_general(
        tp_ref[...].reshape(padded, features), kv, down, preferred_element_type=f32
    )

    deep_rows, pairs, deep, broad = keep_ref.shape
    count = 2 * pairs
    main, rest = 3 * features // count, features // count
    lanes = lax.broadcasted_iota(jnp.int32, (features, broad), 1)

    def window(start, end):
        base, off = start // broad * broad, start % broad
        x = all_ref[:, base : base + broad]
        if off:
            x = pltpu.roll(x, broad - off, 1)
        if end > base + broad:
            y = pltpu.roll(all_ref[:, base + broad : base + 2 * broad], broad - off, 1)
            x = jnp.where(lanes < broad - off, x, y)
        return x

    def block(c):
        x = window(main * c, main * (c + 1))
        base, off = 3 * features + rest * c // broad * broad, rest * c % broad
        y = all_ref[:, base : base + broad]
        if off != main:
            y = pltpu.roll(y, (main - off) % broad, 1)
        return jnp.where(lanes < main, x, y).astype(bf16).reshape(deep_rows, deep, broad)

    mine = lax.axis_index("core") == 0
    for p in range(pairs):
        even, odd = block(2 * p), block(2 * p + 1)
        keep_ref[:, p] = jnp.where(mine, even, odd)
        send_ref[:, p] = jnp.where(mine, odd, even)
    for c in copies:
        c.wait()


def token_kernel(kv_ref, dq_ref, w_ref, gt_ref, co_ref, ce_ref):
    members, tall, breadth, features = dq_ref.shape
    across = (((1,), (1,)), ((), ()))
    middle = tall // 2
    for b in range(members):
        y = lax.dot_general(
            kv_ref[b].reshape(tall * (breadth + 8), 2 * features), w_ref[:, features:], across,
            preferred_element_type=f32,
        ).reshape(tall, breadth + 8, features)
        z = lax.dot_general(
            dq_ref[b].reshape(tall * breadth, features), w_ref[:, 0:features], across,
            preferred_element_type=f32,
        ).reshape(tall, breadth, features)
        gt_ref[b] = (y[:, 0:breadth] + z).astype(bf16)
        here, there = y[0:middle, breadth:], turn(y[middle:, breadth:])
        low = lower(here)
        x, y = swap(even_column(), jnp.where(low, here, there), jnp.where(low, there, here))
        ce_ref[b], co_ref[b] = x.astype(bf16), y.astype(bf16)


def back_rims(fl, fr):
    low = lower(fl)
    here = (jnp.where(low, fl, 0.0), jnp.where(low, 0.0, fr))
    there = (jnp.where(low, turn(fl), 0.0), jnp.where(low, 0.0, turn(fr)))
    return here, there


def plus_rims(x, rims):
    last = x.shape[1] - 8
    return jnp.concatenate([x[:, 0:8] + rims[0], x[:, 8:last], x[:, last:] + rims[1]], 1) if last > 8 else (
        jnp.concatenate([x[:, 0:8] + rims[0], x[:, 8:] + rims[1]], 1)
    )


def add_kernel(x_ref, y_ref, sum_ref):
    sum_ref[...] = (x_ref[...].astype(f32) + y_ref[...].astype(f32)).astype(bf16)


def total_kernel(x_ref, sum_ref, square_ref):
    x = jnp.sum(x_ref[...].astype(f32), 0)
    sum_ref[...] = x
    square = jnp.sum(x * x, 0, keepdims=True)
    square_ref[...] = jnp.broadcast_to(square, square_ref.shape)


def halo_kernel(gt_ref, fo_ref, fe_ref, ro_ref, re_ref):
    members, tall = gt_ref.shape[:2]
    half = tall // 2
    for b in range(members):
        here, _ = back_rims(*columns_of(fe_ref, fo_ref, b, slice(0, 4)))
        _, there = back_rims(*columns_of(fe_ref, fo_ref, b, slice(half - 4, half)))
        up = plus_rims(gt_ref[b, 0:4].astype(f32), here)
        down = plus_rims(gt_ref[b, tall - 4 : tall].astype(f32), there)
        x, y = swap(even_row(), down, up)
        re_ref[b], ro_ref[b] = x.astype(bf16), y.astype(bf16)


def join_kernel(gt_ref, fo_ref, fe_ref, ho_ref, he_ref, tok_ref):
    members, height = tok_ref.shape[:2]
    half = (height + 8) // 2
    for b in range(members):
        bottom, top = swap(even_row(), he_ref[b].astype(f32), ho_ref[b].astype(f32))
        for r in range(0, half, 4):
            pair = back_rims(*columns_of(fe_ref, fo_ref, b, slice(r, r + 4)))
            for rims, row in zip(pair, (r, half + r)):
                if row == 0 or row == height + 4:
                    continue
                y = plus_rims(gt_ref[b, row : row + 4].astype(f32), rims)
                if row == 4:
                    y = y + top
                if row == height:
                    y = y + bottom
                tok_ref[b, row - 4 : row] = y.astype(bf16)


def clip_kernel(x_ref, square_ref, qkv_ref, out_ref):
    total = jnp.sum(jnp.sum(square_ref[...], 0, keepdims=True), 1, keepdims=True)
    clip = jnp.minimum(1.0, max_norm / jnp.sqrt(total + tiny_square))
    x = x_ref[...] * clip
    main = qkv_ref.shape[1]
    qkv_ref[...] = x[:, 0:main]
    out_ref[...] = x.T[main:]


def exchange(odd, even, axes):
    size = lax.axis_size(axes)
    out = []
    for x, first in ((odd, 1), (even, 0)):
        pairs = [(i, i + 1) for i in range(first, size - 1, 2)]
        out.append(lax.ppermute(x, axes, pairs + [(j, i) for i, j in pairs]))
    return out


def body(tokens, w_qkv, w_out, q_saved, k_saved, v_saved, scale_exp, grad_out, crop_start):
    members, height, breadth, features = tokens.shape
    tall = height + 8
    packed = height + height // 2
    packed_columns = shape(members, packed, 8, features)
    strip = shape(3, members, 4, breadth, features)
    factor, *sides = call(
        edge_kernel,
        (
            shape(*scale_exp.shape[:3], 3 * features, dtype=f32),
            strip, strip, packed_columns, packed_columns,
        ),
        (scale_exp, k_saved, v_saved, tokens),
        scratch=(pltpu.VMEM(scale_exp.shape, jnp.int32),)
        + (pltpu.VMEM(tokens.shape, bf16),) * 3
        + (pltpu.SemaphoreType.DMA((1 + 3 * members,)),),
        far=(0, 1, 2, 3),
        limit=58 << 20,
    )
    halo_rows = exchange(*sides[0:2], "row")
    cells = members * height * breadth
    qs, gm, do = call(
        prepare_kernel,
        (shape(*tokens.shape),) * 3,
        (crop_start, q_saved, grad_out, factor, w_out),
        smem=(0,),
        flops=2 * cells * features * features,
    )
    *halo_columns, do = lax.optimization_barrier((*exchange(*sides[2:4], COLS), do))
    corner = shape(members, 12, 8, features)
    corners = exchange(*call(corner_kernel, (corner, corner), halo_columns), "row")
    tiles = breadth // 8
    own_tiles = shape(members, tiles, height, 16, features)
    middle_tiles = shape(members, tiles, 16, 16, features, dtype=f32)
    middle_rows = shape(members, 8, breadth, features)
    kt, vt, dk, dv, out, dq = call(
        middle_kernel,
        (own_tiles, own_tiles, middle_tiles, middle_tiles, middle_rows, middle_rows),
        (qs, do, k_saved, v_saved, factor, *halo_columns),
        scratch=(pltpu.VMEM((tiles, 256, features // 2), f32),),
        flops=4 * cells * features * features,
        limit=20 << 20,
    )
    rows, pairs = lax.axis_size("row"), lax.axis_size("pair")
    deep, wide = features // rows, 4 * features // (2 * pairs)
    halo_tiles = pltpu.VMEM((2, members, tiles, 4, 16, features), bf16)
    all_tiles = pltpu.VMEM((members, tiles, tall, 16, features), f32)
    keep, send, dq, kv = call(
        main_kernel,
        (
            shape(rows, pairs, deep, wide),
            shape(rows, pairs, deep, wide),
            shape(members, tall, breadth, features),
            shape(members, tall, breadth + 8, 2 * features),
        ),
        (
            qs, do, kt, vt, dk, dv, out, dq, gm, tokens,
            *halo_columns, *halo_rows, *corners,
        ),
        scratch=(
            halo_tiles, halo_tiles, all_tiles, all_tiles,
            pltpu.VMEM(tokens.shape, bf16),
            pltpu.VMEM((members, tall, breadth + 8, features), bf16),
            pltpu.VMEM((features, 4 * features), f32),
            pltpu.VMEM((members, tall, breadth, features), bf16),
            pltpu.VMEM((members, tall, breadth + 8, 2 * features), bf16),
            pltpu.VMEM((2 * tiles, 256, features // 2), f32),
            pltpu.SemaphoreType.DMA((2 * members,)),
        ),
        far_outs=(2, 3),
        flops=12 * cells * features * features,
        limit=37 << 20,
    )
    other = lax.ppermute(send, "core", [(0, 1), (1, 0)])
    both = call(add_kernel, shape(rows, pairs, deep, wide), (keep, other)).reshape(rows * pairs, deep, wide)
    parts = lax.all_to_all(both, ("row", "pair"), 0, 0, tiled=True)
    gt, *sides = call(
        token_kernel,
        (
            shape(members, tall, breadth, features),
            shape(members, tall // 2, 8, features),
            shape(members, tall // 2, 8, features),
        ),
        (kv, dq, w_qkv),
        flops=6 * cells * features * features,
        limit=20 << 20,
    )
    back_columns = exchange(*sides, COLS)
    halo = shape(members, 4, breadth, features)
    back_rows = exchange(*call(halo_kernel, (halo, halo), (gt, *back_columns)), "row")
    grad_tokens = call(
        join_kernel, shape(*tokens.shape), (gt, *back_columns, *back_rows)
    )
    total, square = call(
        total_kernel,
        (shape(deep, wide, dtype=f32), shape(2 * rows * pairs, wide, dtype=f32)),
        (parts,),
    )
    squares = lax.all_to_all(square, ("row", "pair", "core"), 0, 0, tiled=True)
    main = 3 * features // (2 * pairs)
    grad_qkv, grad_w_out = call(
        clip_kernel,
        (shape(deep, main, dtype=f32), shape(wide - main, deep, dtype=f32)),
        (total, squares),
    )
    return grad_tokens, grad_qkv, grad_w_out.T


def solution(mesh):
    rows, cols = mesh.devices.shape
    split = jax.sharding.Mesh(mesh.devices.reshape(rows, cols // 2, 2), ("row",) + COLS)
    cells = P(None, "row", COLS, None)
    return jax.shard_map(
        body,
        mesh=split,
        in_specs=(cells, P(), P(), cells, cells, cells, cells, cells, P()),
        out_specs=(cells, P("row", COLS), P("row", COLS)),
        check_vma=False,
    )
```
